32 devices in a mesh: dp: 8 (over y, x, core), tensor: 4 (over z).
Axes of the slice: x: 2, y: 2, z: 4, core: 2. Of those that a mesh axis runs over, the one named last changes fastest.
Arguments:
- hidden_in: bfloat16 [16384, 1024], P(('dp', 'tensor')), may hold values from -6 to 6
- out_grad: bfloat16 [16384, 1024], P(('dp', 'tensor')), may hold values from -6 to 6
- attn_weight: bfloat16 [4, 1024, 1024], P(None, 'dp', 'tensor'), may hold values from -2 to 2
- mlp_weight: bfloat16 [3, 1024, 2624], P(None, 'dp', 'tensor'), may hold values from -2 to 2
- norm_gain: bfloat16 [2, 1024], replicated, may hold values from 0.5 to 1.5
- attn_first: float32 [4, 1024, 1024], P(None, 'dp', 'tensor'), may hold values from -60 to 60
- attn_second: float32 [4, 1024, 1024], P(None, 'dp', 'tensor'), may hold values from 100 to 3000
- attn_left: float32 [4, 1024, 512], P(None, 'dp', 'tensor'), may hold values from -2 to 3
- attn_right: float32 [4, 2048, 1024], P(None, 'dp', 'tensor'), may hold values from -2 to 3
- mlp_first: float32 [3, 1024, 2624], P(None, 'dp', 'tensor'), may hold values from -60 to 60
- mlp_second: float32 [3, 1024, 2624], P(None, 'dp', 'tensor'), may hold values from 100 to 3000
- mlp_left: float32 [3, 1024, 512], P(None, 'dp', 'tensor'), may hold values from -2 to 3
- mlp_right: float32 [3, 5248, 2624], P(None, 'dp', 'tensor'), may hold values from -2 to 3
- gain_first: float32 [2, 1024], replicated, may hold values from -60 to 60
- gain_second: float32 [2, 1024], replicated, may hold values from 100 to 3000
- owner_rows: int32 [8], replicated, may hold values from 0 to 7, each once
- segment_ids: int32 [16384], P('dp'), may hold values from 0 to 15, as said below
- positions: int32 [16384], P('dp'), may hold values from 0 to 1023, as said below
- valid: int32 [16384], P('dp'), may hold values from 0 to 1, as said below
- step: int32 [], replicated, may hold values from 1 to 20
- learn_rate: float32 [], replicated, may hold values from 0.03 to 0.08
- beta_first: float32 [], replicated, may hold values from 0.8 to 0.95
- beta_second: float32 [], replicated, may hold values from 0.9 to 0.99
Outputs:
- output: bfloat16 [16384, 1024], P(('dp', 'tensor'))
- input_grad: bfloat16 [16384, 1024], P(('dp', 'tensor'))
- attn_grad: float32 [4, 1024, 1024], P(None, 'dp', 'tensor')
- mlp_grad: float32 [3, 1024, 2624], P(None, 'dp', 'tensor')
- gain_grad: float32 [2, 1024], replicated
- attn_first_new: float32 [4, 1024, 1024], P(None, 'dp', 'tensor')
- attn_second_new: float32 [4, 1024, 1024], P(None, 'dp', 'tensor')
- mlp_first_new: float32 [3, 1024, 2624], P(None, 'dp', 'tensor')
- mlp_second_new: float32 [3, 1024, 2624], P(None, 'dp', 'tensor')
- gain_first_new: float32 [2, 1024], replicated
- gain_second_new: float32 [2, 1024], replicated
- attn_update: float32 [4, 1024, 1024], P(None, 'dp', 'tensor')
- mlp_update: float32 [3, 1024, 2624], P(None, 'dp', 'tensor')
- gain_update: float32 [2, 1024], replicated
- norm_scale: float32 [7, 8, 4], P(None, 'dp', 'tensor')
- root_means: float32 [4], replicated
The draws below stay inside these ranges and needn't reach their ends.
Inputs may be any that keep to these rules, and one draw needn't show every extreme that they name: `owner_rows`: each index of dp owns a different row block of 128 rows. `segment_ids`: ids restart at 0 with every sequence of 1024 tokens and never fall within it; every document but the last of a sequence has 64 tokens or more. `positions`: 0 at the start of every sequence and wherever segment_ids changes, else one more than the token before. `valid`: within each sequence: 1 on a leading run of at least half of its tokens, 0 after it.
All inputs are finite; a program needn't handle non-finite values.
Results may differ from the reference program's by a relative error of at most 0.014.
Values may be sent and summed in bfloat16 or wider, within the bound.
No kernel may reach another device: no remote copies, remote signals or barrier semaphores. Data moves between devices by JAX's collectives and lax.ppermute only.
A program may use at most 256 MiB of HBM per device.

```python
import math
import jax
import jax.numpy as jnp
from jax import lax

D = 1024
HEADS = 16
HEAD_DIM = 64
FF = 2624
SEQ_LEN = 1024
TOK_GROUP = 2048
TOKENS = 16384
SLAB = 128
ATT_COLS = 256
HID_COLS = 656
BASIS_COLS = 512
ATT_BASIS_ROWS = 2048
HID_BASIS_ROWS = 5248
N_DP = 8
N_TENSOR = 4


def doc_layout(key):
    base_key = jax.random.fold_in(key, 11)
    shortest = max(SEQ_LEN // 16, 1)
    doc_count = SEQ_LEN // shortest
    seq_count = TOKENS // SEQ_LEN
    ticket = jax.random.randint(base_key, (seq_count, doc_count), 1, 4097)
    lengths = jnp.minimum(shortest * (4096 // ticket), SEQ_LEN)
    seq_index = jnp.arange(seq_count, dtype=jnp.int32)[:, None]
    lengths = jnp.where(seq_index == 0, shortest, lengths)
    lengths = jnp.where(seq_index == 1, SEQ_LEN, lengths)
    ends = jnp.cumsum(lengths, axis=1)
    location = jnp.arange(SEQ_LEN, dtype=jnp.int32)
    passed = ends[:, None, :] <= location[None, :, None]
    seg_ids = jnp.sum(passed.astype(jnp.int32), axis=2)
    starts = jnp.max(jnp.where(passed, ends[:, None, :], 0), axis=2)
    return (seg_ids.reshape(TOKENS).astype(jnp.int32), (location[None, :] - starts).reshape(TOKENS).astype(jnp.int32))


def draw_segment_ids(key, part):
    return doc_layout(key)[0]


def draw_positions(key, part):
    return doc_layout(key)[1]


def draw_valid(key, part):
    seq_count = TOKENS // SEQ_LEN
    lengths = jax.random.randint(jax.random.fold_in(key, 23), (seq_count, 1), SEQ_LEN // 2, SEQ_LEN + 1)
    location = jnp.arange(SEQ_LEN, dtype=jnp.int32)[None, :]
    return (location < lengths).astype(jnp.int32).reshape(TOKENS)


def draw_attn_weight(key, part):
    noise = jnp.clip(jax.random.normal(jax.random.fold_in(key, 31), (4, D, D), jnp.float32), -4.0, 4.0)
    factor = jnp.array([1.0, 1.0, 1.0, 4.0], jnp.float32)[:, None, None] * D ** (-0.5)
    return (noise * factor).astype(jnp.bfloat16)


def draw_mlp_weight(key, part):
    noise = jnp.clip(jax.random.normal(jax.random.fold_in(key, 37), (3, D, FF), jnp.float32), -4.0, 4.0)
    factor = jnp.array([D ** (-0.5), D ** (-0.5), 2.0 * FF ** (-0.5)], jnp.float32)[:, None, None]
    return (noise * factor).astype(jnp.bfloat16)


def basis(key, kind_count, row_total, col_total, block_size):
    row_ids = jnp.arange(row_total)[:, None] % block_size
    col_ids = jnp.arange(col_total)[None, :] % block_size
    diagonal = (row_ids == col_ids).astype(jnp.float32)
    noise = jnp.clip(jax.random.normal(key, (kind_count, row_total, col_total), jnp.float32), -4.0, 4.0)
    return diagonal[None] + noise * (0.4 * block_size ** (-0.5))


def draw_attn_left(key, part):
    return basis(jax.random.fold_in(key, 41), 4, D, BASIS_COLS, SLAB)


def draw_attn_right(key, part):
    return basis(jax.random.fold_in(key, 43), 4, ATT_BASIS_ROWS, D, ATT_COLS)


def draw_mlp_left(key, part):
    return basis(jax.random.fold_in(key, 47), 3, D, BASIS_COLS, SLAB)


def draw_mlp_right(key, part):
    return basis(jax.random.fold_in(key, 53), 3, HID_BASIS_ROWS, FF, HID_COLS)


def levels(own_key, extent, shards, least, high):
    def one(dim, parts):
        steps = jax.random.uniform(jax.random.fold_in(jax.random.fold_in(own_key, 6), dim), (parts,), jnp.float32, least / len(shards), high / len(shards))
        return jnp.repeat(jnp.exp(steps), extent[dim] // parts).reshape((-1,) + (1,) * (len(extent) - dim - 1))

    level = one(*shards[0])
    for cut in shards[1:]:
        level = level * one(*cut)
    return level


def bell_draw(own_key, dims, scale, most, cuts=(), kind=jnp.bfloat16):
    loudness = levels(own_key, dims, cuts, -0.22, 0.18) if cuts else 1.0
    drawn = jax.random.normal(own_key, dims, jnp.float32) * scale * loudness
    return jnp.minimum(jnp.maximum(drawn, -most), most).astype(kind)


def setup_inputs(seed: int = 0) -> dict:
    key_list = jax.random.split(jax.random.key(seed), 24)
    return {
        "hidden_in": bell_draw(key_list[0], (TOKENS, D), 1.0, 6.0, ((0, 32),)),
        "out_grad": bell_draw(key_list[1], (TOKENS, D), 1.0, 6.0, ((0, 32),)),
        "attn_weight": draw_attn_weight(jax.random.fold_in(key_list[23], 71), 0),
        "mlp_weight": draw_mlp_weight(jax.random.fold_in(key_list[23], 71), 0),
        "norm_gain": jnp.clip(1.0 + 0.1 * jax.random.normal(key_list[4], (2, D), jnp.float32), 0.5, 1.5).astype(jnp.bfloat16),
        "attn_first": bell_draw(key_list[5], (4, D, D), 10.0, 60.0, ((1, 8), (2, 4)), jnp.float32),
        "attn_second": jnp.clip(jnp.exp(math.log(3000.0) - 3.4011974 * jax.random.uniform(key_list[6], (4, D, D), jnp.float32) ** levels(key_list[6], (4, D, D), ((1, 8), (2, 4)), -0.2, 0.2)), 100.0, 3000.0),
        "attn_left": draw_attn_left(jax.random.fold_in(key_list[23], 71), 0),
        "attn_right": draw_attn_right(jax.random.fold_in(key_list[23], 71), 0),
        "mlp_first": bell_draw(key_list[9], (3, D, FF), 10.0, 60.0, ((1, 8), (2, 4)), jnp.float32),
        "mlp_second": jnp.clip(jnp.exp(math.log(3000.0) - 3.4011974 * jax.random.uniform(key_list[10], (3, D, FF), jnp.float32) ** levels(key_list[10], (3, D, FF), ((1, 8), (2, 4)), -0.2, 0.2)), 100.0, 3000.0),
        "mlp_left": draw_mlp_left(jax.random.fold_in(key_list[23], 71), 0),
        "mlp_right": draw_mlp_right(jax.random.fold_in(key_list[23], 71), 0),
        "gain_first": bell_draw(key_list[13], (2, D), 10.0, 60.0, (), jnp.float32),
        "gain_second": jnp.clip(jnp.exp(jax.random.uniform(key_list[14], (2, D), jnp.float32, math.log(100.0), math.log(3000.0))), 100.0, 3000.0),
        "owner_rows": jax.random.permutation(key_list[15], N_DP).astype(jnp.int32),
        "segment_ids": draw_segment_ids(jax.random.fold_in(key_list[23], 71), 0),
        "positions": draw_positions(jax.random.fold_in(key_list[23], 71), 0),
        "valid": draw_valid(jax.random.fold_in(key_list[23], 71), 0),
        "step": jax.random.randint(key_list[19], (), 1, 21).astype(jnp.int32),
        "learn_rate": jnp.clip(jax.random.uniform(key_list[20], (), jnp.float32, 0.03, 0.08), 0.03, 0.08),
        "beta_first": jnp.clip(jax.random.uniform(key_list[21], (), jnp.float32, 0.8, 0.95), 0.8, 0.95),
        "beta_second": jnp.clip(jax.random.uniform(key_list[22], (), jnp.float32, 0.9, 0.99), 0.9, 0.99),
    }


NORM_EPS = 1e-05
ROPE_BASE = 160000.0
ADAM_EPS = 1e-08
SCALE_EPS = 1e-06
MASKED = -1e+30
PRECISE = lax.Precision.HIGHEST

@jax.custom_vjp
def low(v):
    return lax.optimization_barrier(v.astype(jnp.bfloat16)).astype(jnp.float32)

@jax.custom_vjp
def low_back(v):
    return v

def low_keep(v):
    return (low(v), None)

def low_pass(kept, grad):
    return (grad,)

def back_keep(v):
    return (v, None)

def back_low(kept, grad):
    return (low(grad),)
low.defvjp(low_keep, low_pass)
low_back.defvjp(back_keep, back_low)

def layer_norm(values, gain_row):
    average = lax.optimization_barrier(jnp.mean(values, axis=-1, keepdims=True))
    centred = values - average
    spread = lax.optimization_barrier(jnp.mean(centred * centred, axis=-1, keepdims=True))
    return centred * lax.rsqrt(spread + NORM_EPS) * gain_row

def rope_tables(positions):
    half_dim = HEAD_DIM // 2
    frequency = jnp.exp(jnp.arange(half_dim, dtype=jnp.float32) * (-2.0 * math.log(ROPE_BASE) / HEAD_DIM))
    angles = positions.astype(jnp.float32)[:, None] * frequency[None, :]
    return (jnp.cos(angles)[:, None, :], jnp.sin(angles)[:, None, :])

def rotate(values, cos_table, sin_table):
    half_dim = values.shape[-1] // 2
    lower_half = values[..., :half_dim]
    upper_half = values[..., half_dim:]
    return jnp.concatenate([lower_half * cos_table - upper_half * sin_table, upper_half * cos_table + lower_half * sin_table], axis=-1)

def attend(pieces):
    queries, key_rows, value_rows, seg_row, keep_row = pieces
    location = jnp.arange(seg_row.shape[0])
    allowed = (seg_row[:, None] == seg_row[None, :]) & ((keep_row[None, :] > 0) | (location[:, None] == location[None, :]))
    raw = low_back(jnp.einsum('qhe,khe->hqk', queries, key_rows, precision=PRECISE))
    scores = jnp.where(allowed[None], raw * (1.0 / math.sqrt(HEAD_DIM)), MASKED)
    weights = low(jax.nn.softmax(scores, axis=-1))
    return jnp.einsum('hqk,khe->qhe', weights, value_rows, precision=PRECISE)

def forward(hidden_rows, qkv_weight, out_weight, gate_up_weight, down_weight, gain_rows, seg_rows, pos_rows, keep_rows):
    tokens = hidden_rows.shape[0]
    normed = low(layer_norm(hidden_rows, gain_rows[0]))
    projected = jnp.einsum('td,kdc->ktc', normed, qkv_weight, precision=PRECISE)
    cos_table, sin_table = rope_tables(pos_rows)
    head_shape = (tokens, HEADS, HEAD_DIM)
    queries = low(rotate(low_back(projected[0]).reshape(head_shape), cos_table, sin_table))
    key_rows = low(rotate(low_back(projected[1]).reshape(head_shape), cos_table, sin_table))
    value_rows = low(low_back(projected[2])).reshape(head_shape)
    seq_shape = (tokens // SEQ_LEN, SEQ_LEN, HEADS, HEAD_DIM)
    attended = lax.map(jax.checkpoint(attend), (queries.reshape(seq_shape), key_rows.reshape(seq_shape), value_rows.reshape(seq_shape), seg_rows.reshape(-1, SEQ_LEN), keep_rows.reshape(-1, SEQ_LEN)))
    mixture = low(low_back(attended.reshape(tokens, D)))
    attn_branch = low_back(jnp.einsum('tc,dc->td', mixture, out_weight, precision=PRECISE))
    resid = hidden_rows + attn_branch
    second = low(layer_norm(resid, gain_rows[1]))
    gate_up = jnp.einsum('td,kdf->ktf', second, gate_up_weight, precision=PRECISE)
    activated = low(jax.nn.gelu(low_back(gate_up[0]), approximate=False) * low_back(gate_up[1]))
    mlp_branch = low_back(jnp.einsum('tf,df->td', activated, down_weight, precision=PRECISE))
    return (resid + mlp_branch, (attn_branch, resid, mlp_branch))

def to_model(stored, owner_rows):
    kind_count, row_total, col_total = stored.shape
    blocks = stored.reshape(kind_count, N_DP, SLAB, col_total)
    return jnp.zeros_like(blocks).at[:, owner_rows].set(blocks).reshape(kind_count, row_total, col_total)

def to_owner(model, owner_rows):
    kind_count, row_total, col_total = model.shape
    return model.reshape(kind_count, N_DP, SLAB, col_total)[:, owner_rows].reshape(kind_count, row_total, col_total)

def soap_step(grad_full, first, second, left, right, width, step_size, beta_one, beta_two):
    kind_count = grad_full.shape[0]
    grad_five = grad_full.reshape(kind_count, N_DP, SLAB, N_TENSOR, width)
    left_five = left.reshape(kind_count, N_DP, SLAB, N_TENSOR, SLAB)
    right_five = right.reshape(kind_count, N_DP, width, N_TENSOR, width)
    half_turn = jnp.einsum('kiajb,kiajc->kibjc', left_five, grad_five, precision=PRECISE)
    rotated = jnp.einsum('kibjc,kicje->kibje', half_turn, right_five, precision=PRECISE).reshape(grad_full.shape)
    first_new = beta_one * first + (1.0 - beta_one) * rotated
    second_new = beta_two * second + (1.0 - beta_two) * rotated * rotated
    direction = first_new / (jnp.sqrt(second_new) + ADAM_EPS)
    dir_five = direction.reshape(kind_count, N_DP, SLAB, N_TENSOR, width)
    back_half = jnp.einsum('kiajb,kibje->kiaje', left_five, dir_five, precision=PRECISE)
    turned = jnp.einsum('kiaje,kicje->kiajc', back_half, right_five, precision=PRECISE)
    factor = jnp.sqrt(lax.optimization_barrier(jnp.mean(dir_five * dir_five, axis=(2, 4)))) * lax.rsqrt(lax.optimization_barrier(jnp.mean(turned * turned, axis=(2, 4))) + SCALE_EPS)
    update = -step_size * factor[:, :, None, :, None] * turned
    return (first_new, second_new, update.reshape(grad_full.shape), factor)

def reference(hidden_in, out_grad, attn_weight, mlp_weight, norm_gain, attn_first, attn_second, attn_left, attn_right, mlp_first, mlp_second, mlp_left, mlp_right, gain_first, gain_second, owner_rows, segment_ids, positions, valid, step, learn_rate, beta_first, beta_second):
    attn_model = to_model(attn_weight.astype(jnp.float32), owner_rows)
    mlp_model = to_model(mlp_weight.astype(jnp.float32), owner_rows)
    gain_rows = norm_gain.astype(jnp.float32)

    def one_group(totals, pieces):
        rows_in, grad_rows, seg_rows, pos_rows, keep_rows = pieces

        def run_layer(hidden_rows, qkv_weight, out_weight, gate_up_weight, down_weight, gain_vals):
            return forward(hidden_rows, qkv_weight, out_weight, gate_up_weight, down_weight, gain_vals, seg_rows, pos_rows, keep_rows)
        result, pullback, extras = jax.vjp(run_layer, rows_in.astype(jnp.float32), attn_model[:3], attn_model[3], mlp_model[:2], mlp_model[2], gain_rows, has_aux=True)
        grads = pullback(grad_rows.astype(jnp.float32))
        attn_branch, resid, mlp_branch = extras
        keep_mask = keep_rows.astype(jnp.float32)[:, None]
        stat_terms = jnp.stack([jnp.sum(keep_mask), jnp.sum(keep_mask * attn_branch * attn_branch), jnp.sum(keep_mask * resid * resid), jnp.sum(keep_mask * mlp_branch * mlp_branch), jnp.sum(keep_mask * result * result)])
        totals = (totals[0] + grads[1], totals[1] + grads[2], totals[2] + grads[3], totals[3] + grads[4], totals[4] + grads[5], totals[5] + stat_terms)
        return (totals, (result.astype(jnp.bfloat16), grads[0].astype(jnp.bfloat16)))
    start_totals = (jnp.zeros((3, D, D), jnp.float32), jnp.zeros((D, D), jnp.float32), jnp.zeros((2, D, FF), jnp.float32), jnp.zeros((D, FF), jnp.float32), jnp.zeros((2, D), jnp.float32), jnp.zeros((5,), jnp.float32))
    sliced = (hidden_in.reshape(N_DP, TOK_GROUP, D), out_grad.reshape(N_DP, TOK_GROUP, D), segment_ids.reshape(N_DP, TOK_GROUP), positions.reshape(N_DP, TOK_GROUP), valid.reshape(N_DP, TOK_GROUP))
    totals, (outputs, input_grads) = lax.scan(one_group, start_totals, sliced)
    attn_grad = to_owner(jnp.concatenate([totals[0], totals[1][None]], axis=0), owner_rows)
    mlp_grad = to_owner(jnp.concatenate([totals[2], totals[3][None]], axis=0), owner_rows)
    gain_grad = totals[4]
    step_count = step.astype(jnp.float32)
    step_size = learn_rate * jnp.sqrt(1.0 - jnp.power(beta_second, step_count)) / (1.0 - jnp.power(beta_first, step_count))
    attn_first_new, attn_second_new, attn_update, attn_scale = soap_step(attn_grad, attn_first, attn_second, attn_left, attn_right, ATT_COLS, step_size, beta_first, beta_second)
    mlp_first_new, mlp_second_new, mlp_update, mlp_scale = soap_step(mlp_grad, mlp_first, mlp_second, mlp_left, mlp_right, HID_COLS, step_size, beta_first, beta_second)
    gain_first_new = beta_first * gain_first + (1.0 - beta_first) * gain_grad
    gain_second_new = beta_second * gain_second + (1.0 - beta_second) * gain_grad * gain_grad
    gain_update = -step_size * gain_first_new / (jnp.sqrt(gain_second_new) + ADAM_EPS)
    stat_sums = totals[5]
    root_means = jnp.sqrt(stat_sums[1:] / (stat_sums[0] * D))
    norm_scale = jnp.concatenate([attn_scale, mlp_scale], axis=0)
    return (outputs.reshape(TOKENS, D), input_grads.reshape(TOKENS, D), attn_grad, mlp_grad, gain_grad, attn_first_new, attn_second_new, mlp_first_new, mlp_second_new, gain_first_new, gain_second_new, attn_update, mlp_update, gain_update, norm_scale, root_means)
```

```python
import functools
import math

import jax
import jax.numpy as jnp
from jax import lax
from jax.experimental import pallas as pl
from jax.experimental.pallas import tpu as pltpu
from jax.sharding import PartitionSpec as P

HEAD_DIM = 64
SEQ_LEN = 1024
NORM_EPS = 1e-05
ROPE_BASE = 160000.0
ADAM_EPS = 1e-08
SCALE_EPS = 1e-06
PRECISE = lax.Precision.HIGHEST
BF = jnp.bfloat16
F32 = jnp.float32
ANY = pl.ANY


def dot(a,b,ca,cb):
    return lax.dot_general(a,b,(((ca,),(cb,)),((),())),preferred_element_type=F32)

def turn(x, cos, sin, lower):
    w=x.shape[1]
    sw=jnp.where(lower, pltpu.roll(x, w-32, 1), pltpu.roll(x, 32, 1))
    return x*cos+sw*sin

def lower_lanes(rows, cols):
    return lax.broadcasted_iota(jnp.int32,(rows,cols),1)%64<32

def wide(t, n):
    return t if n==1 else jnp.concatenate([t]*n,axis=1)

def fwd_attn_kernel(perm, a1, hid, gain, cos, sin, kseg, qseg, keep, wp,
                    q_out, k_out, v_out, o_out, lse_out, resid_out, a2_out, stat_out,
                    W, acc, bias, osc, sem, *, T, KV, C, R, S, SLAB, QB):
    s=pl.program_id(0)
    def fetch(step, slot):
        for r in range(R):
            pltpu.make_async_copy(wp.at[r, step], W.at[slot, :, pl.ds(pl.multiple_of(perm[r]*SLAB,SLAB),SLAB), :], sem.at[slot]).start()
    slot=lax.rem(s,2)
    @pl.when(s==0)
    def _():
        fetch(0,0)
        row=lax.broadcasted_iota(jnp.int32,(KV,T),0); col=lax.broadcasted_iota(jnp.int32,(KV,T),1)
        ok=(kseg[...]==qseg[...])|(row==col)
        bias[...]=jnp.where(ok,0.0,-1e30)
        acc[...]=jnp.zeros_like(acc)
    @pl.when(s+1<S)
    def _(): fetch(s+1,1-slot)
    pltpu.make_async_copy(W.at[slot],W.at[slot],sem.at[slot]).wait()
    n=C//128
    low_q=lower_lanes(T,C); low_k=lower_lanes(KV,C)
    cw=wide(cos[...],n); sw=wide(sin[...],n)
    q=dot(a1[:T,:],W[slot,0],1,0)
    q_out[0]=(turn(q,cw[:T],sw[:T],low_q).astype(BF)*BF(1/math.sqrt(HEAD_DIM))).astype(BF)
    k=dot(a1[...],W[slot,1],1,0)
    k_out[0]=turn(k,cw,sw,low_k).astype(BF)
    v_out[0]=dot(a1[...],W[slot,2],1,0).astype(BF)
    for p in range(n):
        kp=k_out[0,:,p*128:(p+1)*128]; vp=v_out[0,:,p*128:(p+1)*128]
        for b in range(T//QB):
            qp=q_out[0,b*QB:(b+1)*QB,p*128:(p+1)*128]
            half=lax.broadcasted_iota(jnp.int32,qp.shape,1)<64
            parts=[]
            for h in range(2):
                qm=jnp.where(half if h==0 else ~half,qp,jnp.zeros_like(qp))
                st=dot(kp,qm,1,1)+bias[:,b*QB:(b+1)*QB]
                m=jnp.max(st,axis=0,keepdims=True)
                e=jnp.exp(st-m)
                l=jnp.sum(e,axis=0,keepdims=True)
                ot=dot(vp,e.astype(BF),0,0)
                parts.append(ot[h*64:(h+1)*64]*(1.0/l))
                lse_out[0,pl.ds(2*p+h,1),b*QB:(b+1)*QB]=m+jnp.log(l)
            op=jnp.concatenate(parts,axis=0)
            osc[b*QB:(b+1)*QB,p*128:(p+1)*128]=op.T.astype(BF)
    o_out[0]=osc[...]
    acc[...]+=dot(osc[...],W[slot,3],1,1)
    @pl.when(s==S-1)
    def _():
        at=acc[...]
        rs=hid[...].astype(F32)+at
        resid_out[...]=rs
        mu=jnp.mean(rs,axis=1,keepdims=True); ce=rs-mu
        var=jnp.mean(ce*ce,axis=1,keepdims=True)
        a2_out[...]=(ce*lax.rsqrt(var+NORM_EPS)*gain[...]).astype(BF)
        kp=keep[...]
        s1=jnp.sum(kp*at*at,axis=0,keepdims=True); s2=jnp.sum(kp*rs*rs,axis=0,keepdims=True)
        stat_out[...]=jnp.concatenate([s1,s2],axis=0)

def full(shape):
    nd=len(shape)
    return pl.BlockSpec(shape,lambda *a:(0,)*nd)

def fwd_attn(perm,a1,hid,gain,cos,sin,kseg,qseg,keep,wp,QB=512):
    R,S,_,SLAB,C=wp.shape
    KV,D=a1.shape; T=hid.shape[0]; HG=C//HEAD_DIM
    sb=lambda rows:pl.BlockSpec((1,rows,C),lambda s,p:(s,0,0))
    gs=pltpu.PrefetchScalarGridSpec(num_scalar_prefetch=1,grid=(S,),
        in_specs=[full((KV,D)),full((T,D)),full((1,D)),full((KV,128)),full((KV,128)),full((KV,1)),full((1,T)),full((T,1)),pl.BlockSpec(memory_space=ANY)],
        out_specs=[sb(T),sb(KV),sb(KV),sb(T),pl.BlockSpec((1,HG,T),lambda s,p:(s,0,0)),full((T,D)),full((T,D)),full((2,D))],
        scratch_shapes=[pltpu.VMEM((2,4,D,C),BF),pltpu.VMEM((T,D),F32),pltpu.VMEM((KV,T),F32),pltpu.VMEM((T,C),BF),pltpu.SemaphoreType.DMA((2,))])
    sd=jax.ShapeDtypeStruct
    fl=2*(2*KV+2*T)*D*D+4*T*KV*D
    return pl.pallas_call(functools.partial(fwd_attn_kernel,T=T,KV=KV,C=C,R=R,S=S,SLAB=SLAB,QB=min(QB,T)),grid_spec=gs,
        out_shape=[sd((S,T,C),BF),sd((S,KV,C),BF),sd((S,KV,C),BF),sd((S,T,C),BF),sd((S,HG,T),F32),sd((T,D),F32),sd((T,D),BF),sd((2,D),F32)],
        cost_estimate=pl.CostEstimate(flops=fl,transcendentals=T*KV*D//HEAD_DIM,bytes_accessed=24<<20),name="attn_fwd")(perm,a1,hid,gain,cos,sin,kseg,qseg,keep,wp)

def gelu_parts(x):
    phi=0.5*(1.0+lax.erf(x*(1.0/math.sqrt(2.0))))
    den=jnp.exp(-0.5*x*x)*(1.0/math.sqrt(2.0*math.pi))
    return phi,den

def mlp_kernel(perm, slots, a2, g, resid, gain, keep, wp,
               out, dres_out, dresb_out, dresT_out, gg_out, stat_out, d0, d1,
               W, stg, hT, dgT, duT, y, da, sem, osem, *, T, D, HC, R, S, SLAB, TB):
    s=pl.program_id(0)
    slot=lax.rem(s,2)
    def fetch(step, sl):
        for r in range(R):
            pltpu.make_async_copy(wp.at[r, step], W.at[sl, :, :, pl.ds(pl.multiple_of(perm[r]*SLAB,SLAB),SLAB)], sem.at[sl]).start()
    @pl.when(s==0)
    def _(): fetch(0,0)
    @pl.when(s+1<S)
    def _(): fetch(s+1,1-slot)
    pltpu.make_async_copy(W.at[slot],W.at[slot],sem.at[slot]).wait()
    for b in range(T//TB):
        lo,hi=b*TB,(b+1)*TB
        ga=dot(W[slot,0],a2[lo:hi,:],1,1)
        up=dot(W[slot,1],a2[lo:hi,:],1,1)
        dh=dot(W[slot,2],g[lo:hi,:],1,1)
        phi,den=gelu_parts(ga)
        ge=ga*phi
        hT[:,lo:hi]=(ge*up).astype(BF)
        dgT[:,lo:hi]=(dh*up*(phi+ga*den)).astype(BF)
        duT[:,lo:hi]=(dh*ge).astype(BF)
    yc=dot(hT[...],W[slot,2],0,0)
    dc=dot(dgT[...],W[slot,0],0,0)+dot(duT[...],W[slot,1],0,0)
    @pl.when(s==0)
    def _():
        y[...]=yc; da[...]=dc
    @pl.when(s>0)
    def _():
        y[...]+=yc; da[...]+=dc
    @pl.when(s>=2)
    def _(): pltpu.make_async_copy(stg.at[slot],stg.at[slot],osem.at[slot]).wait()
    stg[slot,0]=dot(dgT[...],a2[...],1,0).astype(BF)
    stg[slot,1]=dot(duT[...],a2[...],1,0).astype(BF)
    stg[slot,2]=dot(hT[...],g[...],1,0).astype(BF)
    for r in range(R):
        dst=(d0,d1)[r%2]
        pltpu.make_async_copy(stg.at[slot,:,:,pl.ds(pl.multiple_of(perm[R+r]*SLAB,SLAB),SLAB)], dst.at[r//2, slots[s]], osem.at[slot]).start()
    @pl.when(s==S-1)
    def _():
        br=y[...]; rs=resid[...]; gf=g[...].astype(F32)
        res=rs+br
        out[...]=res.astype(BF)
        kp=keep[...]
        s1=jnp.sum(kp*br*br,axis=0,keepdims=True); s2=jnp.sum(kp*res*res,axis=0,keepdims=True)
        stat_out[...]=jnp.concatenate([s1,s2],axis=0)
        mu=jnp.mean(rs,axis=1,keepdims=True); ce=rs-mu
        rstd=lax.rsqrt(jnp.mean(ce*ce,axis=1,keepdims=True)+NORM_EPS)
        xh=ce*rstd
        d=da[...]
        gg_out[...]=jnp.sum(d*xh,axis=0,keepdims=True)
        e=d*gain[...]
        dr=gf+rstd*(e-jnp.mean(e,axis=1,keepdims=True)-xh*jnp.mean(e*xh,axis=1,keepdims=True))
        dres_out[...]=dr
        db=dr.astype(BF)
        dresb_out[...]=db
        dresT_out[...]=dr.T.astype(BF)
        for sl in range(min(S,2)):
            pltpu.make_async_copy(stg.at[sl],stg.at[sl],osem.at[sl]).wait()

def mlp(perm2,slots,a2,g,resid,gain,keep,wp,TB=256):
    R,S,_,HC,SLAB=wp.shape
    T,D=a2.shape
    A=pl.BlockSpec(memory_space=ANY)
    gs=pltpu.PrefetchScalarGridSpec(num_scalar_prefetch=2,grid=(S,),
        in_specs=[full((T,D)),full((T,D)),full((T,D)),full((1,D)),full((T,1)),A],
        out_specs=[full((T,D)),full((T,D)),full((T,D)),full((D,T)),full((1,D)),full((2,D)),A,A],
        scratch_shapes=[pltpu.VMEM((2,3,HC,D),BF),pltpu.VMEM((2,3,HC,D),BF)]+[pltpu.VMEM((HC,T),BF)]*3+[pltpu.VMEM((T,D),F32)]*2+[pltpu.SemaphoreType.DMA((2,)),pltpu.SemaphoreType.DMA((2,))])
    sd=jax.ShapeDtypeStruct
    piece=sd((R//2,S,3,HC,SLAB),BF)
    return pl.pallas_call(functools.partial(mlp_kernel,T=T,D=D,HC=HC,R=R,S=S,SLAB=SLAB,TB=min(TB,T)),grid_spec=gs,
        out_shape=[sd((T,D),BF),sd((T,D),F32),sd((T,D),BF),sd((D,T),BF),sd((1,D),F32),sd((2,D),F32),piece,piece],
        cost_estimate=pl.CostEstimate(flops=18*T*D*HC*S,transcendentals=2*T*HC*S,bytes_accessed=40<<20),name="mlp_both")(perm2,slots,a2,g,resid,gain,keep,wp)

def bwd_attn_kernel(perm, dres, cos, sin, kseg, qseg, q_in, k_in, v_in, lse_in, wp,
                    dq_out, dk_out, dv_out, W, bias, dob, dqs, dks, sem, *, T, KV, C, R, S, SLAB, S0, N):
    s=pl.program_id(0)
    slot=lax.rem(s,2)
    def fetch(step, sl):
        for r in range(R):
            pltpu.make_async_copy(wp.at[r, S0+step, 3], W.at[sl, pl.ds(pl.multiple_of(perm[r]*SLAB,SLAB),SLAB), :], sem.at[sl]).start()
    @pl.when(s==0)
    def _():
        fetch(0,0)
        row=lax.broadcasted_iota(jnp.int32,(KV,T),0); col=lax.broadcasted_iota(jnp.int32,(KV,T),1)
        ok=(kseg[...]==qseg[...])|(row==col)
        bias[...]=jnp.where(ok,0.0,-1e30)
    @pl.when(s+1<N)
    def _(): fetch(s+1,1-slot)
    pltpu.make_async_copy(W.at[slot],W.at[slot],sem.at[slot]).wait()
    n=C//128
    dob[...]=dot(dres[...],W[slot],1,0).astype(BF)
    for p in range(n):
        kp=k_in[0,:,p*128:(p+1)*128]; vp=v_in[0,:,p*128:(p+1)*128]
        qp=q_in[0,:,p*128:(p+1)*128]; dp_=dob[:,p*128:(p+1)*128]
        half=lax.broadcasted_iota(jnp.int32,qp.shape,1)<64
        parts=[]
        dvs=None
        for h in range(2):
            mk=half if h==0 else ~half
            qm=jnp.where(mk,qp,jnp.zeros_like(qp)); dm=jnp.where(mk,dp_,jnp.zeros_like(dp_))
            pt=jnp.exp(dot(kp,qm,1,1)+bias[...]-lse_in[0,2*p+h:2*p+h+1,:])
            dpt=dot(vp,dm,1,1)
            delta=jnp.sum(pt*dpt,axis=0,keepdims=True)
            ds=(pt*(dpt-delta)).astype(BF)
            dv=dot(pt.astype(BF),dm,1,0); dk=dot(ds,qm,1,0)
            dqt=dot(kp,ds,0,0)
            parts.append(dqt[h*64:(h+1)*64])
            if h==0: dva,dka=dv,dk
            else: dva,dka=dva+dv,dka+dk
        dqs[:,p*128:(p+1)*128]=jnp.concatenate(parts,axis=0).T*(1.0/math.sqrt(HEAD_DIM))
        dks[:,p*128:(p+1)*128]=dka
        dv_out[0,:,p*128:(p+1)*128]=dva.astype(BF)
    cw=wide(cos[...],n); sw=wide(sin[...],n)
    dq_out[0]=turn(dqs[...],cw[:T],-sw[:T],lower_lanes(T,C)).astype(BF)
    dk_out[0]=turn(dks[...],cw,-sw,lower_lanes(KV,C)).astype(BF)

def bwd_attn(perm,dres,cos,sin,kseg,qseg,q,k,v,lse,wp,S0=0,N=None):
    R,S,_,SLAB,C=wp.shape
    T,D=dres.shape; KV=k.shape[1]; HG=C//HEAD_DIM
    N=S if N is None else N
    ib=lambda rows:pl.BlockSpec((1,rows,C),lambda s,p:(s+S0,0,0))
    ob=lambda rows:pl.BlockSpec((1,rows,C),lambda s,p:(s,0,0))
    gs=pltpu.PrefetchScalarGridSpec(num_scalar_prefetch=1,grid=(N,),
        in_specs=[full((T,D)),full((KV,128)),full((KV,128)),full((KV,1)),full((1,T)),ib(T),ib(KV),ib(KV),pl.BlockSpec((1,HG,T),lambda s,p:(s+S0,0,0)),pl.BlockSpec(memory_space=ANY)],
        out_specs=[ob(T),ob(KV),ob(KV)],
        scratch_shapes=[pltpu.VMEM((2,D,C),BF),pltpu.VMEM((KV,T),F32),pltpu.VMEM((T,C),BF),pltpu.VMEM((T,C),F32),pltpu.VMEM((KV,C),F32),pltpu.SemaphoreType.DMA((2,))])
    sd=jax.ShapeDtypeStruct
    fl=(2*T*D*C+10*T*KV*C)*N
    return pl.pallas_call(functools.partial(bwd_attn_kernel,T=T,KV=KV,C=C,R=R,S=S,SLAB=SLAB,S0=S0,N=N),grid_spec=gs,
        out_shape=[sd((N,T,C),BF),sd((N,KV,C),BF),sd((N,KV,C),BF)],
        cost_estimate=pl.CostEstimate(flops=fl*4,transcendentals=T*KV*N*C//HEAD_DIM,bytes_accessed=(8<<20)*N//S+(2<<20)),name="attn_bwd")(perm,dres,cos,sin,kseg,qseg,q,k,v,lse,wp)

def grad_attn_kernel(perm, slots, a1T, dresT, xhat, o_in, dq_in, dk_in, dv_in, wp,
                     da_own, da_far, gg_out, d0, d1, W, stg, acc, sem, osem, *, T, KV, C, R, S, SLAB):
    s=pl.program_id(0)
    slot=lax.rem(s,2)
    def fetch(step, sl):
        for r in range(R):
            pltpu.make_async_copy(wp.at[r, step, pl.ds(0,3)], W.at[sl, :, pl.ds(pl.multiple_of(perm[r]*SLAB,SLAB),SLAB), :], sem.at[sl]).start()
    @pl.when(s==0)
    def _(): fetch(0,0)
    @pl.when(s+1<S)
    def _(): fetch(s+1,1-slot)
    @pl.when(s>=2)
    def _(): pltpu.make_async_copy(stg.at[slot],stg.at[slot],osem.at[slot]).wait()
    stg[slot,0]=dot(a1T[:,:T],dq_in[0],1,0).astype(BF)
    stg[slot,1]=dot(a1T[...],dk_in[0],1,0).astype(BF)
    stg[slot,2]=dot(a1T[...],dv_in[0],1,0).astype(BF)
    stg[slot,3]=dot(dresT[...],o_in[0],1,0).astype(BF)
    for r in range(R):
        dst=(d0,d1)[r%2]
        pltpu.make_async_copy(stg.at[slot,:,pl.ds(pl.multiple_of(perm[R+r]*SLAB,SLAB),SLAB),:], dst.at[r//2, slots[s]], osem.at[slot]).start()
    pltpu.make_async_copy(W.at[slot],W.at[slot],sem.at[slot]).wait()
    c=dot(dk_in[0],W[slot,1],1,1)+dot(dv_in[0],W[slot,2],1,1)
    cq=dot(dq_in[0],W[slot,0],1,1)
    @pl.when(s==0)
    def _():
        acc[...]=c
        acc[:T,:]=acc[:T,:]+cq
    @pl.when(s>0)
    def _():
        acc[...]=acc[...]+c
        acc[:T,:]=acc[:T,:]+cq
    @pl.when(s==S-1)
    def _():
        gg_out[...]=jnp.sum(acc[...]*xhat[...].astype(F32),axis=0,keepdims=True)
        da_own[...]=acc[:T,:]
        da_far[...]=acc[T:,:].astype(BF)
        for sl in range(min(S,2)):
            pltpu.make_async_copy(stg.at[sl],stg.at[sl],osem.at[sl]).wait()

def grad_attn(perm2,slots,a1T,dresT,xhat,o,dq,dk,dv,wp):
    R,S,_,SLAB,C=wp.shape
    D,T=dresT.shape; KV=dk.shape[1]
    A=pl.BlockSpec(memory_space=ANY)
    ib=lambda rows:pl.BlockSpec((1,rows,C),lambda s,p,q:(s,0,0))
    gs=pltpu.PrefetchScalarGridSpec(num_scalar_prefetch=2,grid=(S,),
        in_specs=[full((D,KV)),full((D,T)),full((KV,D)),ib(T),ib(T),ib(KV),ib(KV),A],
        out_specs=[full((T,D)),full((KV-T,D)),full((1,D)),A,A],
        scratch_shapes=[pltpu.VMEM((2,3,D,C),BF),pltpu.VMEM((2,4,D,C),BF),pltpu.VMEM((KV,D),F32),pltpu.SemaphoreType.DMA((2,)),pltpu.SemaphoreType.DMA((2,))])
    sd=jax.ShapeDtypeStruct
    piece=sd((R//2,S,4,SLAB,C),BF)
    return pl.pallas_call(functools.partial(grad_attn_kernel,T=T,KV=KV,C=C,R=R,S=S,SLAB=SLAB),grid_spec=gs,
        out_shape=[sd((T,D),F32),sd((KV-T,D),BF),sd((1,D),F32),piece,piece],
        cost_estimate=pl.CostEstimate(flops=2*D*D*(2*T+2*KV+2*KV+T),transcendentals=0,bytes_accessed=30<<20),name="attn_grad")(perm2,slots,a1T,dresT,xhat,o,dq,dk,dv,wp)


def ring_order(count):
    return list(range(0, count, 2)) + list(range(1, count, 2))[::-1]


def swap_dp(value, bit, owners):
    return lax.ppermute(value, "dp", [(i, i ^ bit) for i in range(owners)])


def to_ring_pred(value, shards):
    ring = ring_order(shards)
    return lax.ppermute(
        value, "tensor", [(ring[p], ring[(p - 1) % shards]) for p in range(shards)]
    )


def add_low(one, two):
    return (one.astype(F32) + two.astype(F32)).astype(BF)


def halve(pieces, bits, owners):
    for bit in bits:
        live = sorted(bits[bits.index(bit):], reverse=True)
        axis = live.index(bit)
        send = lax.index_in_dim(pieces, 1, axis, keepdims=False)
        keep = lax.index_in_dim(pieces, 0, axis, keepdims=False)
        pieces = add_low(keep, swap_dp(send, bit, owners))
    return pieces


def reduce_pieces(even, odd, cut, owners, shards):
    mine = add_low(even, swap_dp(odd, 1, owners))
    bits = [1 << b for b in range(1, owners.bit_length() - 1)]
    mine = mine.reshape((2,) * len(bits) + mine.shape[1:])
    low = halve(mine[..., :cut, :], bits[::-1], owners)
    high = halve(mine[..., cut:, :], bits, owners)
    both = jnp.concatenate([low, high], axis=-2)
    moving = both[shards - 1]
    for left in range(shards - 2, -1, -1):
        moving = to_ring_pred(moving, shards)
        moving = moving.astype(F32) + both[left].astype(F32)
        if left:
            moving = moving.astype(BF)
    return moving


def all_sum(value, owners, shards):
    for axis, count in (("dp", owners), ("tensor", shards)):
        step = 1
        while step < count:
            value = value + lax.ppermute(value, axis, [(i, i ^ step) for i in range(count)])
            step *= 2
    return value


def soap_block(grad_block, first, second, left, right, step_size, beta_one, beta_two):
    half_turn = jnp.einsum("kab,kac->kbc", left, grad_block, precision=PRECISE)
    rotated = jnp.einsum("kbc,kce->kbe", half_turn, right, precision=PRECISE)
    first_new = beta_one * first + (1.0 - beta_one) * rotated
    second_new = beta_two * second + (1.0 - beta_two) * rotated * rotated
    direction = first_new / (jnp.sqrt(second_new) + ADAM_EPS)
    back_half = jnp.einsum("kab,kbe->kae", left, direction, precision=PRECISE)
    turned = jnp.einsum("kae,kce->kac", back_half, right, precision=PRECISE)
    factor = jnp.sqrt(jnp.mean(direction * direction, axis=(1, 2))) * lax.rsqrt(
        jnp.mean(turned * turned, axis=(1, 2)) + SCALE_EPS
    )
    update = -step_size * factor[:, None, None] * turned
    return (first_new, second_new, update, factor)


def per_device(
    hidden_in, out_grad, attn_weight, mlp_weight, norm_gain,
    attn_first, attn_second, attn_left, attn_right,
    mlp_first, mlp_second, mlp_left, mlp_right,
    gain_first, gain_second, owner_rows, segment_ids, positions, valid,
    step, learn_rate, beta_first, beta_second,
):
    owners = lax.axis_size("dp")
    shards = lax.axis_size("tensor")
    dp_index = lax.axis_index("dp")
    place = lax.axis_index("tensor")
    rows, width = hidden_in.shape
    slab = attn_weight.shape[1]
    hid_cols = mlp_weight.shape[2]
    span = SEQ_LEN // rows
    within = place % span
    base = place - within
    gain_rows = norm_gain.astype(F32)

    def from_peer(value, ahead):
        pairs = [(g + (w + ahead) % span, g + w) for g in range(0, shards, span) for w in range(span)]
        return lax.ppermute(value, "tensor", pairs)

    def sequence_rows(column):
        return jnp.concatenate(
            [lax.dynamic_slice_in_dim(column, (base + (within + d) % span) * rows, rows, 0) for d in range(span)]
        )

    both = ("dp", "tensor")
    attn_all = lax.all_gather(attn_weight, both, axis=0, tiled=False).reshape((owners, shards) + attn_weight.shape)
    mlp_turned = jnp.swapaxes(mlp_weight, 1, 2)
    mlp_all = lax.all_gather(mlp_turned, both, axis=0, tiled=False).reshape((owners, shards) + mlp_turned.shape)

    slot_ids = jnp.arange(owners, dtype=jnp.int32)
    rel_owner = jnp.sum(
        jnp.where((slot_ids[:, None] ^ dp_index) == slot_ids[None, :], owner_rows[None, :], 0), axis=1
    )
    ring = ring_order(shards)
    ring_place = jnp.array([ring.index(z) for z in range(shards)], jnp.int32)
    my_place = jnp.sum(jnp.where(jnp.arange(shards) == place, ring_place, 0))
    slots = (my_place - ring_place) % shards
    attn_perm = jnp.concatenate([owner_rows, rel_owner]).astype(jnp.int32)
    joined = 128 // slab if slab < 128 else 1
    if joined == 1:
        mlp_perm = attn_perm
    else:
        inverse = jnp.sum(jnp.where(owner_rows[None, :] == slot_ids[:, None], slot_ids[None, :], 0), axis=1)
        mlp_all = jnp.take(mlp_all, inverse, axis=0).reshape((owners // joined, joined) + mlp_all.shape[1:])
        mlp_all = jnp.moveaxis(mlp_all, 1, 4)
        mlp_all = mlp_all.reshape(mlp_all.shape[:4] + (joined * slab,))
        blocks = jnp.arange(owners // joined, dtype=jnp.int32)
        mlp_perm = jnp.concatenate([blocks, blocks])

    hidden_seq = jnp.concatenate([hidden_in] + [from_peer(hidden_in, d) for d in range(1, span)]).astype(F32)
    centred = hidden_seq - jnp.mean(hidden_seq, axis=-1, keepdims=True)
    rstd = lax.rsqrt(jnp.mean(centred * centred, axis=-1, keepdims=True) + NORM_EPS)
    xhat = centred * rstd
    first_norm = (xhat * gain_rows[0]).astype(BF)
    xhat_low = xhat.astype(BF)

    seg = sequence_rows(segment_ids)
    keep_seq = sequence_rows(valid)
    pos = sequence_rows(positions)
    half_dim = HEAD_DIM // 2
    frequency = jnp.exp(jnp.arange(half_dim, dtype=F32) * (-2.0 * math.log(ROPE_BASE) / HEAD_DIM))
    angles = pos.astype(F32)[:, None] * frequency[None, :]
    cos_half, sin_half = jnp.cos(angles), jnp.sin(angles)
    cos_table = jnp.concatenate([cos_half] * 4, axis=1)
    sin_table = jnp.concatenate([-sin_half, sin_half] * 2, axis=1)
    key_seg = jnp.where(keep_seq > 0, seg, -1)[:, None]
    query_seg = seg[None, :rows]
    keep_own = keep_seq[:rows].astype(F32)[:, None]

    queries, keys, values, attended, log_sums, resid, second_norm, stat_a = fwd_attn(
        attn_perm, first_norm, hidden_in, gain_rows[1:2], cos_table, sin_table, key_seg, query_seg, keep_own, attn_all
    )
    output, dresid, dres_low, dres_turned, gain_two, stat_m, mlp_even, mlp_odd = mlp(
        mlp_perm, slots, second_norm, out_grad, resid, gain_rows[1:2], keep_own, mlp_all
    )
    if joined > 1:
        merged = jnp.stack([mlp_even, mlp_odd], axis=1).reshape((owners // joined,) + mlp_even.shape[1:])
        merged = merged.reshape(merged.shape[:-1] + (joined, slab))
        merged = jnp.moveaxis(merged, -2, 1).reshape((owners,) + mlp_even.shape[1:-1] + (slab,))
        merged = jnp.take(merged, rel_owner, axis=0)
        mlp_even, mlp_odd = merged[0::2], merged[1::2]
    mlp_cut = -(-hid_cols // 32) * 16
    mlp_sum = reduce_pieces(mlp_even, mlp_odd, mlp_cut, owners, shards)
    mlp_grad = jnp.swapaxes(mlp_sum, 1, 2)

    parts = [
        bwd_attn(attn_perm, dres_low, cos_table, sin_table, key_seg, query_seg, queries, keys, values, log_sums, attn_all, S0=s, N=1)
        for s in range(shards)
    ]
    dq, dk, dv = (jnp.concatenate([p[i] for p in parts]) for i in range(3))
    first_turned = first_norm.T
    da_own, da_far, gain_one, attn_even, attn_odd = grad_attn(
        attn_perm, slots, first_turned, dres_turned, xhat_low, attended, dq, dk, dv, attn_all
    )
    first_grad = da_own
    for d in range(1, span):
        pairs = [(g + w, g + (w + d) % span) for g in range(0, shards, span) for w in range(span)]
        first_grad = first_grad + lax.ppermute(da_far[(d - 1) * rows : d * rows], "tensor", pairs).astype(F32)
    attn_grad = reduce_pieces(attn_even, attn_odd, slab // 2, owners, shards)

    scaled = first_grad * gain_rows[0]
    own_hat = xhat[:rows]
    input_part = rstd[:rows] * (
        scaled
        - jnp.mean(scaled, axis=-1, keepdims=True)
        - own_hat * jnp.mean(scaled * own_hat, axis=-1, keepdims=True)
    )
    input_grad = (dresid + input_part).astype(BF)

    sums = jnp.concatenate([jnp.sum(stat_a, axis=1), jnp.sum(stat_m, axis=1), jnp.sum(keep_own)[None]])
    small = jnp.concatenate([gain_one, gain_two, jnp.pad(sums, (0, width - 5))[None]], axis=0)
    small = all_sum(small, owners, shards)
    gain_grad = small[:2]
    stat_sums = small[2]

    step_count = step.astype(F32)
    step_size = (
        learn_rate
        * jnp.sqrt(1.0 - jnp.power(beta_second, step_count))
        / (1.0 - jnp.power(beta_first, step_count))
    )
    attn_first_new, attn_second_new, attn_update, attn_scale = soap_block(
        attn_grad, attn_first, attn_second, attn_left, attn_right, step_size, beta_first, beta_second
    )
    mlp_first_new, mlp_second_new, mlp_update, mlp_scale = soap_block(
        mlp_grad, mlp_first, mlp_second, mlp_left, mlp_right, step_size, beta_first, beta_second
    )
    gain_first_new = beta_first * gain_first + (1.0 - beta_first) * gain_grad
    gain_second_new = beta_second * gain_second + (1.0 - beta_second) * gain_grad * gain_grad
    gain_update = -step_size * gain_first_new / (jnp.sqrt(gain_second_new) + ADAM_EPS)
    root_means = jnp.sqrt(stat_sums[:4] / (stat_sums[4] * width))
    norm_scale = jnp.concatenate([attn_scale, mlp_scale], axis=0).reshape(7, 1, 1)
    return (
        output, input_grad, attn_grad, mlp_grad, gain_grad,
        attn_first_new, attn_second_new, mlp_first_new, mlp_second_new,
        gain_first_new, gain_second_new, attn_update, mlp_update, gain_update,
        norm_scale, root_means,
    )


def solution(mesh):
    rows = P(("dp", "tensor"), None)
    block = P(None, "dp", "tensor")
    return jax.shard_map(
        per_device,
        mesh=mesh,
        in_specs=(rows, rows, block, block, P()) + (block,) * 8 + (P(),) * 3 + (P("dp"),) * 3 + (P(),) * 4,
        out_specs=(rows, rows, block, block, P(), block, block, block, block, P(), P(), block, block, P(), block, P()),
        check_vma=False,
    )
```

```python
import functools
import math

import jax
import jax.numpy as jnp
from jax import lax
from jax.experimental import pallas as pl
from jax.experimental.pallas import tpu as pltpu
from jax.sharding import PartitionSpec as P

HEAD_DIM = 64
SEQ_LEN = 1024
NORM_EPS = 1e-05
ROPE_BASE = 160000.0
ADAM_EPS = 1e-08
SCALE_EPS = 1e-06
PRECISE = lax.Precision.HIGHEST
BF = jnp.bfloat16
F32 = jnp.float32
ANY = pl.ANY


def dot(a,b,ca,cb):
    return lax.dot_general(a,b,(((ca,),(cb,)),((),())),preferred_element_type=F32)

def turn(x, cos, sin, lower):
    w=x.shape[1]
    sw=jnp.where(lower, pltpu.roll(x, w-32, 1), pltpu.roll(x, 32, 1))
    return x*cos+sw*sin

def lower_lanes(rows, cols):
    return lax.broadcasted_iota(jnp.int32,(rows,cols),1)%64<32

def wide(t, n):
    return t if n==1 else jnp.concatenate([t]*n,axis=1)

def fetch_pieces(refs, metas, perm, step, copy):
    for ref, meta in zip(refs, metas):
        if meta is None:
            for r in range(ref.shape[0]):
                copy(ref.at[r, step], perm[r])
        else:
            r, first, count, total = meta
            if count == total:
                copy(ref.at[step], perm[r])
            else:
                @pl.when((step >= first) & (step < first + count))
                def _(ref=ref, r=r, first=first):
                    copy(ref.at[jnp.clip(step - first, 0, ref.shape[0] - 1)], perm[r])

def fwd_attn_kernel(perm, a1, hid, gain, cos, sin, kseg, qseg, keep, *rest, T, KV, C, metas, S, SLAB, QB, S0, N):
    wps = rest[:len(metas)]
    rest = rest[len(metas):]
    if S0:
        acc_in, rest = rest[0], rest[6:]
    q_out, k_out, v_out, o_out, lse_out = rest[:5]
    if S0+N==S:
        resid_out, a2_out, stat_out, acc = rest[5:9]
    else:
        acc = rest[5]
    W, bias, osc, sem = rest[-4:]
    s=pl.program_id(0)
    def fetch(step, slot):
        fetch_pieces(wps, metas, perm, S0+step, lambda src, blk: pltpu.make_async_copy(src, W.at[slot, :, pl.ds(pl.multiple_of(blk*SLAB,SLAB),SLAB), :], sem.at[slot]).start())
    slot=lax.rem(s,2)
    @pl.when(s==0)
    def _():
        fetch(0,0)
        row=lax.broadcasted_iota(jnp.int32,(KV,T),0); col=lax.broadcasted_iota(jnp.int32,(KV,T),1)
        ok=(kseg[...]==qseg[...])|(row==col)
        bias[...]=jnp.where(ok,0.0,-1e30)
        acc[...]=acc_in[...] if S0 else jnp.zeros_like(acc)
    @pl.when(s+1<N)
    def _(): fetch(s+1,1-slot)
    pltpu.make_async_copy(W.at[slot],W.at[slot],sem.at[slot]).wait()
    n=C//128
    low_q=lower_lanes(T,C); low_k=lower_lanes(KV,C)
    cw=wide(cos[...],n); sw=wide(sin[...],n)
    q=dot(a1[:T,:],W[slot,0],1,0)
    q_out[0]=(turn(q,cw[:T],sw[:T],low_q).astype(BF)*BF(1/math.sqrt(HEAD_DIM))).astype(BF)
    k=dot(a1[...],W[slot,1],1,0)
    k_out[0]=turn(k,cw,sw,low_k).astype(BF)
    v_out[0]=dot(a1[...],W[slot,2],1,0).astype(BF)
    for p in range(n):
        kp=k_out[0,:,p*128:(p+1)*128]; vp=v_out[0,:,p*128:(p+1)*128]
        for b in range(T//QB):
            qp=q_out[0,b*QB:(b+1)*QB,p*128:(p+1)*128]
            half=lax.broadcasted_iota(jnp.int32,qp.shape,1)<64
            parts=[]
            for h in range(2):
                qm=jnp.where(half if h==0 else ~half,qp,jnp.zeros_like(qp))
                st=dot(kp,qm,1,1)+bias[:,b*QB:(b+1)*QB]
                m=jnp.max(st,axis=0,keepdims=True)
                e=jnp.exp(st-m)
                l=jnp.sum(e,axis=0,keepdims=True)
                ot=dot(vp,e.astype(BF),0,0)
                parts.append(ot[h*64:(h+1)*64]*(1.0/l))
                lse_out[0,pl.ds(2*p+h,1),b*QB:(b+1)*QB]=m+jnp.log(l)
            op=jnp.concatenate(parts,axis=0)
            osc[b*QB:(b+1)*QB,p*128:(p+1)*128]=op.T.astype(BF)
    o_out[0]=osc[...]
    acc[...]+=dot(osc[...],W[slot,3],1,1)
    if S0+N<S:
        return
    @pl.when(s==N-1)
    def _():
        at=acc[...]
        rs=hid[...].astype(F32)+at
        resid_out[...]=rs
        mu=jnp.mean(rs,axis=1,keepdims=True); ce=rs-mu
        var=jnp.mean(ce*ce,axis=1,keepdims=True)
        a2_out[...]=(ce*lax.rsqrt(var+NORM_EPS)*gain[...]).astype(BF)
        kp=keep[...]
        s1=jnp.sum(kp*at*at,axis=0,keepdims=True); s2=jnp.sum(kp*rs*rs,axis=0,keepdims=True)
        stat_out[...]=jnp.concatenate([s1,s2],axis=0)

def full(shape):
    nd=len(shape)
    return pl.BlockSpec(shape,lambda *a:(0,)*nd)

def fwd_attn(perm,a1,hid,gain,cos,sin,kseg,qseg,keep,pieces,S0=0,N=None,carry=(),QB=512):
    wps,metas,S,SLAB,C=pieces
    N=S if N is None else N
    KV,D=a1.shape; T=hid.shape[0]; HG=C//HEAD_DIM
    A=pl.BlockSpec(memory_space=ANY)
    sb=lambda rows:pl.BlockSpec((1,rows,C),lambda s,p:(s+S0,0,0))
    sd=jax.ShapeDtypeStruct
    last=S0+N==S
    tail=[sd((T,D),F32),sd((T,D),BF),sd((2,D),F32)] if last else [sd((T,D),F32)]
    gs=pltpu.PrefetchScalarGridSpec(num_scalar_prefetch=1,grid=(N,),
        in_specs=[full((KV,D)),full((T,D)),full((1,D)),full((KV,128)),full((KV,128)),full((KV,1)),full((1,T)),full((T,1))]+[A]*len(wps)+([full((T,D))]+[A]*5 if S0 else []),
        out_specs=[sb(T),sb(KV),sb(KV),sb(T),pl.BlockSpec((1,HG,T),lambda s,p:(s+S0,0,0))]+[full(t.shape) for t in tail],
        scratch_shapes=([pltpu.VMEM((T,D),F32)] if last else [])+[pltpu.VMEM((2,4,D,C),BF),pltpu.VMEM((KV,T),F32),pltpu.VMEM((T,C),BF),pltpu.SemaphoreType.DMA((2,))])
    return pl.pallas_call(functools.partial(fwd_attn_kernel,T=T,KV=KV,C=C,metas=metas,S=S,SLAB=SLAB,QB=min(QB,T),S0=S0,N=N),grid_spec=gs,
        out_shape=[sd((S,T,C),BF),sd((S,KV,C),BF),sd((S,KV,C),BF),sd((S,T,C),BF),sd((S,HG,T),F32)]+tail,
        input_output_aliases={10+len(wps)+i:i for i in range(5)} if S0 else {},
        cost_estimate=pl.CostEstimate(flops=1,transcendentals=0,bytes_accessed=1),name="attn_fwd")(perm,a1,hid,gain,cos,sin,kseg,qseg,keep,*wps,*((carry[5],)+tuple(carry[:5]) if S0 else ()))

def gelu_parts(x):
    phi=0.5*(1.0+lax.erf(x*(1.0/math.sqrt(2.0))))
    den=jnp.exp(-0.5*x*x)*(1.0/math.sqrt(2.0*math.pi))
    return phi,den

def mlp_kernel(perm, slots, a2, g, resid, gain, keep, *rest, T, D, HC, R, metas, S, SLAB, TB, S0, N):
    wps = rest[:len(metas)]
    rest = rest[len(metas):]
    if S0:
        y_in, da_in = rest[:2]
        rest = rest[2:]
    if S0+N==S:
        out, dres_out, dresb_out, dresT_out, gg_out, stat_out = rest[:6]
        rest = rest[6:]
        d0, d1, y, da = rest[:4]
    else:
        y, da, d0, d1 = rest[:4]
    W, stg, hT, dgT, duT, sem, osem = rest[4:]
    s=pl.program_id(0)
    slot=lax.rem(s,2)
    def fetch(step, sl):
        fetch_pieces(wps, metas, perm, S0+step, lambda src, blk: pltpu.make_async_copy(src, W.at[sl, :, :, pl.ds(pl.multiple_of(blk*SLAB,SLAB),SLAB)], sem.at[sl]).start())
    @pl.when(s==0)
    def _(): fetch(0,0)
    @pl.when(s+1<N)
    def _(): fetch(s+1,1-slot)
    pltpu.make_async_copy(W.at[slot],W.at[slot],sem.at[slot]).wait()
    for b in range(T//TB):
        lo,hi=b*TB,(b+1)*TB
        ga=dot(W[slot,0],a2[lo:hi,:],1,1)
        up=dot(W[slot,1],a2[lo:hi,:],1,1)
        dh=dot(W[slot,2],g[lo:hi,:],1,1)
        phi,den=gelu_parts(ga)
        ge=ga*phi
        hT[:,lo:hi]=(ge*up).astype(BF)
        dgT[:,lo:hi]=(dh*up*(phi+ga*den)).astype(BF)
        duT[:,lo:hi]=(dh*ge).astype(BF)
    yc=dot(hT[...],W[slot,2],0,0)
    dc=dot(dgT[...],W[slot,0],0,0)+dot(duT[...],W[slot,1],0,0)
    @pl.when(s==0)
    def _():
        y[...]=yc+y_in[...] if S0 else yc
        da[...]=dc+da_in[...] if S0 else dc
    @pl.when(s>0)
    def _():
        y[...]+=yc; da[...]+=dc
    @pl.when(s>=2)
    def _(): pltpu.make_async_copy(stg.at[slot],stg.at[slot],osem.at[slot]).wait()
    stg[slot,0]=dot(dgT[...],a2[...],1,0).astype(BF)
    stg[slot,1]=dot(duT[...],a2[...],1,0).astype(BF)
    stg[slot,2]=dot(hT[...],g[...],1,0).astype(BF)
    for r in range(R):
        dst=(d0,d1)[r%2]
        pltpu.make_async_copy(stg.at[slot,:,:,pl.ds(pl.multiple_of(perm[R+r]*SLAB,SLAB),SLAB)], dst.at[r//2, slots[S0+s]-S0], osem.at[slot]).start()
    if S0+N==S:
        @pl.when(s==N-1)
        def _():
            br=y[...]; rs=resid[...]; gf=g[...].astype(F32)
            res=rs+br
            out[...]=res.astype(BF)
            kp=keep[...]
            s1=jnp.sum(kp*br*br,axis=0,keepdims=True); s2=jnp.sum(kp*res*res,axis=0,keepdims=True)
            stat_out[...]=jnp.concatenate([s1,s2],axis=0)
            mu=jnp.mean(rs,axis=1,keepdims=True); ce=rs-mu
            rstd=lax.rsqrt(jnp.mean(ce*ce,axis=1,keepdims=True)+NORM_EPS)
            xh=ce*rstd
            d=da[...]
            gg_out[...]=jnp.sum(d*xh,axis=0,keepdims=True)
            e=d*gain[...]
            dr=gf+rstd*(e-jnp.mean(e,axis=1,keepdims=True)-xh*jnp.mean(e*xh,axis=1,keepdims=True))
            dres_out[...]=dr
            db=dr.astype(BF)
            dresb_out[...]=db
            dresT_out[...]=dr.T.astype(BF)
    @pl.when(s==N-1)
    def _():
        for sl in range(min(N,2)):
            pltpu.make_async_copy(stg.at[sl],stg.at[sl],osem.at[sl]).wait()

def mlp(perm2,slots,a2,g,resid,gain,keep,pieces,S0=0,N=None,carry=(),TB=256):
    wps,metas,S,SLAB,HC=pieces
    N=S if N is None else N
    R=perm2.shape[0]//2
    T,D=a2.shape
    A=pl.BlockSpec(memory_space=ANY)
    sd=jax.ShapeDtypeStruct
    last=S0+N==S
    outs=[sd((T,D),BF),sd((T,D),F32),sd((T,D),BF),sd((D,T),BF),sd((1,D),F32),sd((2,D),F32)] if last else [sd((T,D),F32)]*2
    gs=pltpu.PrefetchScalarGridSpec(num_scalar_prefetch=2,grid=(N,),
        in_specs=[full((T,D)),full((T,D)),full((T,D)),full((1,D)),full((T,1))]+[A]*len(wps)+[full((T,D))]*len(carry),
        out_specs=[full(o.shape) for o in outs]+[A,A],
        scratch_shapes=([pltpu.VMEM((T,D),F32)]*2 if last else [])+[pltpu.VMEM((2,3,HC,D),BF),pltpu.VMEM((2,3,HC,D),BF)]+[pltpu.VMEM((HC,T),BF)]*3+[pltpu.SemaphoreType.DMA((2,)),pltpu.SemaphoreType.DMA((2,))])
    piece=sd((R//2,N,3,HC,SLAB),BF)
    return pl.pallas_call(functools.partial(mlp_kernel,T=T,D=D,HC=HC,R=R,metas=metas,S=S,SLAB=SLAB,TB=min(TB,T),S0=S0,N=N),grid_spec=gs,
        out_shape=outs+[piece,piece],
        cost_estimate=pl.CostEstimate(flops=1,transcendentals=0,bytes_accessed=1),name="mlp_both")(perm2,slots,a2,g,resid,gain,keep,*wps,*carry)

def bwd_attn_kernel(perm, dres, cos, sin, kseg, qseg, q_in, k_in, v_in, lse_in, *rest, T, KV, C, metas, S, SLAB, S0, N):
    wps = rest[:len(metas)]
    dq_out, dk_out, dv_out, W, bias, dob, dqs, dks, sem = rest[-9:]
    s=pl.program_id(0)
    slot=lax.rem(s,2)
    def fetch(step, sl):
        fetch_pieces(wps, metas, perm, S0+step, lambda src, blk: pltpu.make_async_copy(src.at[3], W.at[sl, pl.ds(pl.multiple_of(blk*SLAB,SLAB),SLAB), :], sem.at[sl]).start())
    @pl.when(s==0)
    def _():
        fetch(0,0)
        row=lax.broadcasted_iota(jnp.int32,(KV,T),0); col=lax.broadcasted_iota(jnp.int32,(KV,T),1)
        ok=(kseg[...]==qseg[...])|(row==col)
        bias[...]=jnp.where(ok,0.0,-1e30)
    @pl.when(s+1<N)
    def _(): fetch(s+1,1-slot)
    pltpu.make_async_copy(W.at[slot],W.at[slot],sem.at[slot]).wait()
    n=C//128
    dob[...]=dot(dres[...],W[slot],1,0).astype(BF)
    for p in range(n):
        kp=k_in[0,:,p*128:(p+1)*128]; vp=v_in[0,:,p*128:(p+1)*128]
        qp=q_in[0,:,p*128:(p+1)*128]; dp_=dob[:,p*128:(p+1)*128]
        half=lax.broadcasted_iota(jnp.int32,qp.shape,1)<64
        parts=[]
        dvs=None
        for h in range(2):
            mk=half if h==0 else ~half
            qm=jnp.where(mk,qp,jnp.zeros_like(qp)); dm=jnp.where(mk,dp_,jnp.zeros_like(dp_))
            pt=jnp.exp(dot(kp,qm,1,1)+bias[...]-lse_in[0,2*p+h:2*p+h+1,:])
            dpt=dot(vp,dm,1,1)
            delta=jnp.sum(pt*dpt,axis=0,keepdims=True)
            ds=(pt*(dpt-delta)).astype(BF)
            dv=dot(pt.astype(BF),dm,1,0); dk=dot(ds,qm,1,0)
            dqt=dot(kp,ds,0,0)
            parts.append(dqt[h*64:(h+1)*64])
            if h==0: dva,dka=dv,dk
            else: dva,dka=dva+dv,dka+dk
        dqs[:,p*128:(p+1)*128]=jnp.concatenate(parts,axis=0).T*(1.0/math.sqrt(HEAD_DIM))
        dks[:,p*128:(p+1)*128]=dka
        dv_out[0,:,p*128:(p+1)*128]=dva.astype(BF)
    cw=wide(cos[...],n); sw=wide(sin[...],n)
    dq_out[0]=turn(dqs[...],cw[:T],-sw[:T],lower_lanes(T,C)).astype(BF)
    dk_out[0]=turn(dks[...],cw,-sw,lower_lanes(KV,C)).astype(BF)

def bwd_attn(perm,dres,cos,sin,kseg,qseg,q,k,v,lse,pieces,S0=0,N=None,carry=()):
    wps,metas,S,SLAB,C=pieces
    T,D=dres.shape; KV=k.shape[1]; HG=C//HEAD_DIM
    N=S if N is None else N
    ib=lambda rows:pl.BlockSpec((1,rows,C),lambda s,p:(s+S0,0,0))
    gs=pltpu.PrefetchScalarGridSpec(num_scalar_prefetch=1,grid=(N,),
        in_specs=[full((T,D)),full((KV,128)),full((KV,128)),full((KV,1)),full((1,T)),ib(T),ib(KV),ib(KV),pl.BlockSpec((1,HG,T),lambda s,p:(s+S0,0,0))]+[pl.BlockSpec(memory_space=ANY)]*(len(wps)+len(carry)),
        out_specs=[ib(T),ib(KV),ib(KV)],
        scratch_shapes=[pltpu.VMEM((2,D,C),BF),pltpu.VMEM((KV,T),F32),pltpu.VMEM((T,C),BF),pltpu.VMEM((T,C),F32),pltpu.VMEM((KV,C),F32),pltpu.SemaphoreType.DMA((2,))])
    sd=jax.ShapeDtypeStruct
    fl=(2*T*D*C+10*T*KV*C)*N
    return pl.pallas_call(functools.partial(bwd_attn_kernel,T=T,KV=KV,C=C,metas=metas,S=S,SLAB=SLAB,S0=S0,N=N),grid_spec=gs,
        out_shape=[sd((S,T,C),BF),sd((S,KV,C),BF),sd((S,KV,C),BF)],
        input_output_aliases={10+len(wps)+i:i for i in range(len(carry))},
        cost_estimate=pl.CostEstimate(flops=1,transcendentals=0,bytes_accessed=1),name="attn_bwd")(perm,dres,cos,sin,kseg,qseg,q,k,v,lse,*wps,*carry)

def grad_attn_kernel(perm, slots, a1T, dresT, xhat, o_in, dq_in, dk_in, dv_in, *rest, T, KV, C, R, metas, S, SLAB):
    wps = rest[:len(metas)]
    da_own, da_far, gg_out, d0, d1, W, stg, acc, sem, osem = rest[len(metas):]
    s=pl.program_id(0)
    slot=lax.rem(s,2)
    def fetch(step, sl):
        fetch_pieces(wps, metas, perm, step, lambda src, blk: pltpu.make_async_copy(src.at[pl.ds(0,3)], W.at[sl, :, pl.ds(pl.multiple_of(blk*SLAB,SLAB),SLAB), :], sem.at[sl]).start())
    @pl.when(s==0)
    def _(): fetch(0,0)
    @pl.when(s+1<S)
    def _(): fetch(s+1,1-slot)
    @pl.when(s>=2)
    def _(): pltpu.make_async_copy(stg.at[slot],stg.at[slot],osem.at[slot]).wait()
    stg[slot,0]=dot(a1T[:,:T],dq_in[0],1,0).astype(BF)
    stg[slot,1]=dot(a1T[...],dk_in[0],1,0).astype(BF)
    stg[slot,2]=dot(a1T[...],dv_in[0],1,0).astype(BF)
    stg[slot,3]=dot(dresT[...],o_in[0],1,0).astype(BF)
    for r in range(R):
        dst=(d0,d1)[r%2]
        pltpu.make_async_copy(stg.at[slot,:,pl.ds(pl.multiple_of(perm[R+r]*SLAB,SLAB),SLAB),:], dst.at[r//2, slots[s]], osem.at[slot]).start()
    pltpu.make_async_copy(W.at[slot],W.at[slot],sem.at[slot]).wait()
    c=dot(dk_in[0],W[slot,1],1,1)+dot(dv_in[0],W[slot,2],1,1)
    cq=dot(dq_in[0],W[slot,0],1,1)
    @pl.when(s==0)
    def _():
        acc[...]=c
        acc[:T,:]=acc[:T,:]+cq
    @pl.when(s>0)
    def _():
        acc[...]=acc[...]+c
        acc[:T,:]=acc[:T,:]+cq
    @pl.when(s==S-1)
    def _():
        gg_out[...]=jnp.sum(acc[...]*xhat[...].astype(F32),axis=0,keepdims=True)
        da_own[...]=acc[:T,:]
        da_far[...]=acc[T:,:].astype(BF)
        for sl in range(min(S,2)):
            pltpu.make_async_copy(stg.at[sl],stg.at[sl],osem.at[sl]).wait()

def grad_attn(perm2,slots,a1T,dresT,xhat,o,dq,dk,dv,pieces):
    wps,metas,S,SLAB,C=pieces
    R=perm2.shape[0]//2
    D,T=dresT.shape; KV=dk.shape[1]
    A=pl.BlockSpec(memory_space=ANY)
    ib=lambda rows:pl.BlockSpec((1,rows,C),lambda s,p,q:(s,0,0))
    gs=pltpu.PrefetchScalarGridSpec(num_scalar_prefetch=2,grid=(S,),
        in_specs=[full((D,KV)),full((D,T)),full((KV,D)),ib(T),ib(T),ib(KV),ib(KV)]+[A]*len(wps),
        out_specs=[full((T,D)),full((KV-T,D)),full((1,D)),A,A],
        scratch_shapes=[pltpu.VMEM((2,3,D,C),BF),pltpu.VMEM((2,4,D,C),BF),pltpu.VMEM((KV,D),F32),pltpu.SemaphoreType.DMA((2,)),pltpu.SemaphoreType.DMA((2,))])
    sd=jax.ShapeDtypeStruct
    piece=sd((R//2,S,4,SLAB,C),BF)
    return pl.pallas_call(functools.partial(grad_attn_kernel,T=T,KV=KV,C=C,R=R,metas=metas,S=S,SLAB=SLAB),grid_spec=gs,
        out_shape=[sd((T,D),F32),sd((KV-T,D),BF),sd((1,D),F32),piece,piece],
        cost_estimate=pl.CostEstimate(flops=1,transcendentals=0,bytes_accessed=1),name="attn_grad")(perm2,slots,a1T,dresT,xhat,o,dq,dk,dv,*wps)

def split3(x):
    hi=x.astype(BF)
    return hi,(x-hi.astype(F32)).astype(BF)

def dot3(a,b,ca,cb):
    ah,al=a; bh,bl=b
    return dot(ah,bh,ca,cb)+(dot(ah,bl,ca,cb)+dot(al,bh,ca,cb))

def soap_kernel(sc, g_in, first, second, left, right, *rest, turned):
    f_out, s_out, u_out, n_out = rest[-4:]
    step,b1,b2=sc[0],sc[1],sc[2]
    ql=split3(left[0]); qr=split3(right[0])
    if turned:
        x=dot3(split3(g_in[0]),ql,1,0)
        r=dot3(split3(x),qr,0,0).T
    else:
        x=dot3(ql,split3(g_in[0]),0,0)
        r=dot3(split3(x),qr,1,0)
    fn=b1*first[0]+(1.0-b1)*r
    sn=b2*second[0]+(1.0-b2)*r*r
    f_out[0]=fn; s_out[0]=sn
    n=fn/(jnp.sqrt(sn)+ADAM_EPS)
    if turned:
        t=dot3(split3(dot3(qr,split3(n),1,0)),ql,1,1)
    else:
        t=dot3(split3(dot3(ql,split3(n),1,0)),qr,1,1)
    size=n.shape[0]*n.shape[1]
    fac=jnp.sqrt(jnp.sum(n*n,keepdims=True)*(1.0/size))*lax.rsqrt(jnp.sum(t*t,keepdims=True)*(1.0/size)+SCALE_EPS)
    u_out[0]=(-step*fac)*t
    n_out[0]=jnp.broadcast_to(fac,(8,128))

def soap(scalars,g,first,second,left,right,turned,K0=0,N=None,carry=()):
    K=first.shape[0]
    N=K if N is None else N
    b=lambda x:pl.BlockSpec((1,)+x.shape[1:],lambda k,s:(k+K0,0,0))
    sd=jax.ShapeDtypeStruct
    o=sd(first.shape,F32)
    outs=[o,o,o,sd((K,8,128),F32)]
    gs=pltpu.PrefetchScalarGridSpec(num_scalar_prefetch=1,grid=(N,),
        in_specs=[b(x) for x in (g,first,second,left,right)]+[pl.BlockSpec(memory_space=ANY)]*len(carry),out_specs=[b(x) for x in outs])
    return pl.pallas_call(functools.partial(soap_kernel,turned=turned),grid_spec=gs,out_shape=outs,
        input_output_aliases={6+i:i for i in range(len(carry))},
        cost_estimate=pl.CostEstimate(flops=1,transcendentals=0,bytes_accessed=1),
        name="soap_"+("mlp" if turned else "attn"))(scalars,g,first,second,left,right,*carry)


def ring_order(count):
    return list(range(0, count, 2)) + list(range(1, count, 2))[::-1]


def swap_dp(value, bit, owners):
    return lax.ppermute(value, "dp", [(i, i ^ bit) for i in range(owners)])


def to_ring_pred(value, shards):
    ring = ring_order(shards)
    return lax.ppermute(
        value, "tensor", [(ring[p], ring[(p - 1) % shards]) for p in range(shards)]
    )


def to_ring_succ(value, shards):
    ring = ring_order(shards)
    return lax.ppermute(
        value, "tensor", [(ring[p], ring[(p + 1) % shards]) for p in range(shards)]
    )


def along_line(value, steps, shards):
    ring = ring_order(shards)
    return lax.ppermute(
        value, "tensor", [(ring[p], ring[(p + steps) % shards]) for p in range(shards)]
    )


def add_low(one, two):
    return (one.astype(F32) + two.astype(F32)).astype(BF)


def halve(pieces, bits, owners):
    for bit in bits:
        live = sorted(bits[bits.index(bit):], reverse=True)
        axis = live.index(bit)
        send = lax.index_in_dim(pieces, 1, axis, keepdims=False)
        keep = lax.index_in_dim(pieces, 0, axis, keepdims=False)
        pieces = add_low(keep, swap_dp(send, bit, owners))
    return pieces


def reduce_pieces(even, odd, cut, owners, shards):
    mine = add_low(even, swap_dp(odd, 1, owners))
    bits = [1 << b for b in range(1, owners.bit_length() - 1)]
    mine = mine.reshape((2,) * len(bits) + mine.shape[1:])
    low = halve(mine[..., :cut, :], bits[::-1], owners)
    high = halve(mine[..., cut:, :], bits, owners)
    both = jnp.concatenate([low, high], axis=-2)
    moving = both[shards - 1]
    for left in range(shards - 2, -1, -1):
        moving = to_ring_pred(moving, shards)
        moving = moving.astype(F32) + both[left].astype(F32)
        if left:
            moving = moving.astype(BF)
    return moving


def all_sum(value, owners, shards):
    for axis, count in (("dp", owners), ("tensor", shards)):
        step = 1
        while step < count:
            value = value + lax.ppermute(value, axis, [(i, i ^ step) for i in range(count)])
            step *= 2
    return value


def after(value, *earlier):
    return lax.optimization_barrier((value,) + earlier)[0]


def add_all(*values):
    total = values[0].astype(F32)
    for value in values[1:]:
        total = total + value.astype(F32)
    return total


def gather_stack(stacked, owners):
    half = stacked.shape[0] // 2
    by_x, by_y = swap_dp(stacked, 2, owners), swap_dp(stacked, 4, owners)
    return by_x, by_y, swap_dp(by_x[:half], 4, owners), swap_dp(by_y[half:], 2, owners)


def to_core(arrays, owners):
    return [swap_dp(a, 1, owners) for a in arrays]


def with_partner(arrays, metas, owners):
    return arrays + [swap_dp(a, 1, owners) for a in arrays], metas + tuple((m[0] + 1,) + m[1:] for m in metas)


def cross_sends(even, core, half):
    low = add_all(even[3, :half], core[3, :half]).astype(BF)
    high = add_all(even[3, half:], core[3, half:]).astype(BF)
    return low, high


def side_sends(even, core, from_y, from_x, half):
    to_x = jnp.concatenate(
        [add_all(even[1, :half], core[1, :half], from_y), add_all(even[1, half:], core[1, half:])]
    ).astype(BF)
    to_y = jnp.concatenate(
        [add_all(even[2, :half], core[2, :half]), add_all(even[2, half:], core[2, half:], from_x)]
    ).astype(BF)
    return to_x, to_y


def own_part(even, core, from_x, from_y, slot):
    return add_all(even[0, slot], core[0, slot], from_x[slot], from_y[slot])


def ring_sum(even, core, from_x, from_y, shards):
    moving = None
    for slot in list(range(1, shards)) + [0]:
        part = own_part(even, core, from_x, from_y, slot)
        if moving is not None:
            part = part + to_ring_succ(moving, shards).astype(F32)
        moving = part.astype(BF)
    return part


def per_device(
    hidden_in, out_grad, attn_weight, mlp_weight, norm_gain,
    attn_first, attn_second, attn_left, attn_right,
    mlp_first, mlp_second, mlp_left, mlp_right,
    gain_first, gain_second, owner_rows, segment_ids, positions, valid,
    step, learn_rate, beta_first, beta_second,
):
    owners = lax.axis_size("dp")
    shards = lax.axis_size("tensor")
    dp_index = lax.axis_index("dp")
    place = lax.axis_index("tensor")
    rows, width = hidden_in.shape
    slab = attn_weight.shape[1]
    hid_cols = mlp_weight.shape[2]
    span = SEQ_LEN // rows
    within = place % span
    base = place - within
    half = shards // 2
    gain_rows = norm_gain.astype(F32)

    def from_peer(value, ahead):
        pairs = [(g + (w + ahead) % span, g + w) for g in range(0, shards, span) for w in range(span)]
        return lax.ppermute(value, "tensor", pairs)

    def sequence_rows(column):
        return jnp.concatenate(
            [lax.dynamic_slice_in_dim(column, (base + (within + d) % span) * rows, rows, 0) for d in range(span)]
        )

    joined = 128 // slab if slab < 128 else 1
    fast = owners == 8 and joined == 1 and shards == 4 and span == 2
    both = ("dp", "tensor")
    mlp_turned = jnp.swapaxes(mlp_weight, 1, 2)
    if not fast:
        attn_all = lax.all_gather(attn_weight, both, axis=0, tiled=False).reshape((owners, shards) + attn_weight.shape)
        mlp_all = lax.all_gather(mlp_turned, both, axis=0, tiled=False).reshape((owners, shards) + mlp_turned.shape)

    slot_ids = jnp.arange(owners, dtype=jnp.int32)
    rel_owner = jnp.sum(
        jnp.where((slot_ids[:, None] ^ dp_index) == slot_ids[None, :], owner_rows[None, :], 0), axis=1
    )
    ring = ring_order(shards)
    ring_place = jnp.array([ring.index(z) for z in range(shards)], jnp.int32)
    my_place = jnp.sum(jnp.where(jnp.arange(shards) == place, ring_place, 0))
    slots = (my_place - ring_place) % shards
    attn_perm = jnp.concatenate([rel_owner if fast else owner_rows, rel_owner]).astype(jnp.int32)
    if fast:
        slots = jnp.arange(shards, dtype=jnp.int32)
    if joined == 1:
        mlp_perm = attn_perm
    else:
        inverse = jnp.sum(jnp.where(owner_rows[None, :] == slot_ids[:, None], slot_ids[None, :], 0), axis=1)
        mlp_all = jnp.take(mlp_all, inverse, axis=0).reshape((owners // joined, joined) + mlp_all.shape[1:])
        mlp_all = jnp.moveaxis(mlp_all, 1, 4)
        mlp_all = mlp_all.reshape(mlp_all.shape[:4] + (joined * slab,))
        blocks = jnp.arange(owners // joined, dtype=jnp.int32)
        mlp_perm = jnp.concatenate([blocks, blocks])

    seg = sequence_rows(segment_ids)
    keep_seq = sequence_rows(valid)
    pos = sequence_rows(positions)
    half_dim = HEAD_DIM // 2
    frequency = jnp.exp(jnp.arange(half_dim, dtype=F32) * (-2.0 * math.log(ROPE_BASE) / HEAD_DIM))
    angles = pos.astype(F32)[:, None] * frequency[None, :]
    cos_half, sin_half = jnp.cos(angles), jnp.sin(angles)
    cos_table = jnp.concatenate([cos_half] * 4, axis=1)
    sin_table = jnp.concatenate([-sin_half, sin_half] * 2, axis=1)
    key_seg = jnp.where(keep_seq > 0, seg, -1)[:, None]
    query_seg = seg[None, :rows]
    keep_own = keep_seq[:rows].astype(F32)[:, None]

    def normalize_first(far_rows):
        hidden_seq = jnp.concatenate([hidden_in] + far_rows).astype(F32)
        centred = hidden_seq - jnp.mean(hidden_seq, axis=-1, keepdims=True)
        rstd = lax.rsqrt(jnp.mean(centred * centred, axis=-1, keepdims=True) + NORM_EPS)
        xhat = centred * rstd
        first_norm = (xhat * gain_rows[0]).astype(BF)
        return first_norm, first_norm.T, xhat.astype(BF), xhat[:rows], rstd[:rows]

    back_args = (cos_table, sin_table, key_seg, query_seg)
    if fast:
        line = [attn_weight] + [None] * 3
        for t in (1, 3, 2):
            line[t] = along_line(attn_weight, t, shards)
        mlp_line = [mlp_turned] + [None] * 3
        mlp_x, mlp_y, mlp_z = [None] * 4, [None] * 4, [None] * 4
        mlp_x[0], mlp_y[0] = swap_dp(mlp_turned, 2, owners), swap_dp(mlp_turned, 4, owners)
        line, mlp_x[0], mlp_y[0] = lax.optimization_barrier((line, mlp_x[0], mlp_y[0]))
        far_rows = from_peer(after(hidden_in, line[2]), 1)
        stacked = jnp.stack(line)
        by_x, by_y = swap_dp(stacked, 2, owners), swap_dp(stacked, 4, owners)
        by_x, by_y, far_rows = lax.optimization_barrier((by_x, by_y, far_rows))
        across = [swap_dp(by_x[:half], 4, owners), swap_dp(by_y[half:], 2, owners)]
        turn = after(mlp_turned, far_rows)
        for t in (1, 3, 2):
            mlp_line[t] = along_line(turn, t, shards)
        normal = normalize_first([far_rows])
        across, normal, mlp_line[1] = lax.optimization_barrier((across, normal, mlp_line[1]))
        first_norm, first_turned, xhat_low, own_hat, own_rstd = normal
        arrays = [stacked, by_x, by_y, *across]
        metas = tuple((r, f, n, shards) for r, f, n in ((0, 0, shards), (2, 0, shards), (4, 0, shards), (6, 0, half), (6, half, half)))
        attn_pieces = (*with_partner(arrays, metas, owners), shards, slab, attn_weight.shape[2])
        mlp_x[1], mlp_y[1] = swap_dp(mlp_line[1], 2, owners), swap_dp(mlp_line[1], 4, owners)
        mlp_z[0] = swap_dp(after(mlp_x[0], mlp_line[1]), 4, owners)
    else:
        far_rows = [from_peer(hidden_in, d) for d in range(1, span)]
        attn_pieces = ([attn_all], (None,), shards, slab, attn_weight.shape[2])
        first_norm, first_turned, xhat_low, own_hat, own_rstd = normalize_first(far_rows)
    fwd_args = (attn_perm, first_norm, hidden_in, gain_rows[1:2], cos_table, sin_table, key_seg, query_seg, keep_own)
    if fast:
        carry = fwd_attn(*fwd_args, attn_pieces, S0=0, N=half)
        set_0 = [mlp_line[0], mlp_x[0], mlp_y[0], mlp_z[0]]
        set_1 = [mlp_line[1], mlp_x[1], mlp_y[1]]
        set_0, set_1, mlp_line[3], carry = lax.optimization_barrier((set_0, set_1, mlp_line[3], tuple(carry)))
        mlp_z[1] = swap_dp(set_1[2], 2, owners)
        mlp_x[3], mlp_y[3] = swap_dp(mlp_line[3], 2, owners), swap_dp(mlp_line[3], 4, owners)
        core_0, core_1 = to_core(set_0, owners), to_core(set_1, owners)
        out = fwd_attn(*fwd_args, attn_pieces, S0=half, N=half, carry=carry)
        set_3 = [mlp_line[3], mlp_x[3], mlp_y[3]]
        core_0, core_1, far_z, set_3, mlp_line[2], out = lax.optimization_barrier((core_0, core_1, mlp_z[1], set_3, mlp_line[2], tuple(out)))
        queries, keys, values, attended, log_sums, resid, second_norm, stat_a = out
        set_1, core_1 = set_1 + [far_z], core_1 + to_core([far_z], owners)
        core_1, second_norm, set_3, mlp_line[2] = lax.optimization_barrier((core_1, second_norm, set_3, mlp_line[2]))

        def mlp_pieces(*slots_of):
            arrays, metas = [], []
            for slot, got in slots_of:
                arrays += [a[None] for a in got]
                metas += [(r, slot, 1, shards) for r in (0, 2, 4, 6, 1, 3, 5, 7)]
            return arrays, tuple(metas), shards, slab, hid_cols

        mlp_z[3] = swap_dp(set_3[1], 4, owners)
        set_2 = [mlp_line[2], swap_dp(mlp_line[2], 2, owners), swap_dp(mlp_line[2], 4, owners)]
        core_3 = to_core(set_3, owners)
        mlp_args = (mlp_perm, slots, second_norm, out_grad, resid, gain_rows[1:2], keep_own)
        out = mlp(*mlp_args, mlp_pieces((0, set_0 + core_0), (1, set_1 + core_1)), S0=0, N=half)
        far_z, core_3, set_2, out = lax.optimization_barrier((mlp_z[3], core_3, set_2, tuple(out)))
        set_3, core_3 = set_3 + [far_z], core_3 + to_core([far_z], owners)
        far_z = swap_dp(set_2[2], 2, owners)
        core_2 = to_core(set_2, owners)
        set_2, core_2 = set_2 + [far_z], core_2 + to_core([far_z], owners)
        *carry, even_a, odd_a = out
        core_a = swap_dp(odd_a, 1, owners)
        low, high = cross_sends(even_a, core_a, 1)
        low, high, core_2, core_3, carry = lax.optimization_barrier((low, high, core_2, core_3, carry))
        from_y, from_x = swap_dp(low, 4, owners), swap_dp(high, 2, owners)
        out = mlp(*mlp_args, mlp_pieces((2, set_2 + core_2), (3, set_3 + core_3)), S0=half, N=half, carry=carry)
        from_y, from_x, *out = lax.optimization_barrier((from_y, from_x, *out))
        output, dresid, dres_low, dres_turned, gain_two, stat_m, even_b, odd_b = out
        core_b = swap_dp(odd_b, 1, owners)
        to_x, to_y = side_sends(even_a, core_a, from_y, from_x, 1)
        to_x, to_y, dres_low = lax.optimization_barrier((to_x, to_y, dres_low))
        back_x, back_y = swap_dp(to_x, 2, owners), swap_dp(to_y, 4, owners)
        fwd_kept = (queries, keys, values, log_sums, attn_pieces)
        grads = bwd_attn(attn_perm, dres_low, *back_args, *fwd_kept, S0=0, N=half)
        back_x, back_y, core_b, *grads = lax.optimization_barrier((back_x, back_y, core_b, *grads))
        low, high = cross_sends(even_b, core_b, 1)
        ring_1 = own_part(even_a, core_a, back_x, back_y, 1).astype(BF)
        low, high, ring_1, dres_low = lax.optimization_barrier((low, high, ring_1, dres_low))
        from_y, from_x = swap_dp(low, 4, owners), swap_dp(high, 2, owners)
        ring_1 = to_ring_succ(ring_1, shards)
        grads = bwd_attn(attn_perm, dres_low, *back_args, *fwd_kept, S0=half, N=half, carry=tuple(grads))
        from_y, from_x, ring_1, *grads = lax.optimization_barrier((from_y, from_x, ring_1, *grads))
        to_x, to_y = side_sends(even_b, core_b, from_y, from_x, 1)
        to_x, to_y, dres_turned = lax.optimization_barrier((to_x, to_y, dres_turned))
        from_x, from_y = swap_dp(to_x, 2, owners), swap_dp(to_y, 4, owners)
        out = grad_attn(attn_perm, slots, first_turned, dres_turned, xhat_low, attended, *grads, attn_pieces)
        from_x, from_y, *out = lax.optimization_barrier((from_x, from_y, *out))
        da_own, da_far, gain_one, attn_even, attn_odd = out
    else:
        queries, keys, values, attended, log_sums, resid, second_norm, stat_a = fwd_attn(*fwd_args, attn_pieces)
        output, dresid, dres_low, dres_turned, gain_two, stat_m, mlp_even, mlp_odd = mlp(
            mlp_perm, slots, second_norm, out_grad, resid, gain_rows[1:2], keep_own,
            ([mlp_all], (None,), shards, mlp_all.shape[-1], hid_cols),
        )
        if joined > 1:
            merged = jnp.stack([mlp_even, mlp_odd], axis=1).reshape((owners // joined,) + mlp_even.shape[1:])
            merged = merged.reshape(merged.shape[:-1] + (joined, slab))
            merged = jnp.moveaxis(merged, -2, 1).reshape((owners,) + mlp_even.shape[1:-1] + (slab,))
            merged = jnp.take(merged, rel_owner, axis=0)
            mlp_even, mlp_odd = merged[0::2], merged[1::2]
        mlp_sum = reduce_pieces(mlp_even, mlp_odd, -(-hid_cols // 32) * 16, owners, shards)
        grads = bwd_attn(attn_perm, dres_low, *back_args, queries, keys, values, log_sums, attn_pieces)
        da_own, da_far, gain_one, attn_even, attn_odd = grad_attn(
            attn_perm, slots, first_turned, dres_turned, xhat_low, attended, *grads, attn_pieces
        )
    def send_back(da_far):
        got = []
        for d in range(1, span):
            pairs = [(g + w, g + (w + d) % span) for g in range(0, shards, span) for w in range(span)]
            got.append(lax.ppermute(da_far[(d - 1) * rows : d * rows], "tensor", pairs))
        return got

    def swap_line(value, bit):
        return lax.ppermute(value, "tensor", [(i, i ^ bit) for i in range(shards)])

    def finish_input(da_back):
        first_grad = add_all(da_own, *da_back)
        scaled = first_grad * gain_rows[0]
        input_part = own_rstd * (
            scaled
            - jnp.mean(scaled, axis=-1, keepdims=True)
            - own_hat * jnp.mean(scaled * own_hat, axis=-1, keepdims=True)
        )
        return (dresid + input_part).astype(BF)

    step_count = step.astype(F32)
    step_size = (
        learn_rate
        * jnp.sqrt(1.0 - jnp.power(beta_second, step_count))
        / (1.0 - jnp.power(beta_first, step_count))
    )
    scalars = jnp.stack([step_size, beta_first, beta_second])

    def flip(value):
        return jnp.swapaxes(value, 1, 2)

    def soap_mlp(total, *part):
        return soap(scalars, total, flip(mlp_first), flip(mlp_second), mlp_left, mlp_right, True, *part)

    sums = jnp.concatenate([jnp.sum(stat_a, axis=1), jnp.sum(stat_m, axis=1), jnp.sum(keep_own)[None]])
    small = jnp.concatenate([gain_one, gain_two, jnp.pad(sums, (0, width - 5))[None]], axis=0)
    if fast:
        attn_core = swap_dp(attn_odd, 1, owners)
        da_back = send_back(da_far)
        small = small + swap_dp(small, 1, owners)
        small, attn_core = lax.optimization_barrier((small, attn_core))
        ring_2 = (own_part(even_b, core_b, from_x, from_y, 0) + ring_1.astype(F32)).astype(BF)
        ring_2 = to_ring_succ(ring_2, shards)
        low, high = cross_sends(attn_even, attn_core, half)
        cross_y, cross_x = swap_dp(low, 4, owners), swap_dp(high, 2, owners)
        small = (small + swap_dp(small, 2, owners)) + (swap_dp(small, 4, owners) + swap_dp(small, 6, owners))
        small, cross_x, cross_y = lax.optimization_barrier((small, cross_x, cross_y))
        to_x, to_y = side_sends(attn_even, attn_core, cross_y, cross_x, half)
        to_x, to_y, ring_2, da_back, small = lax.optimization_barrier((to_x, to_y, ring_2, da_back, small))
        attn_x, attn_y = swap_dp(to_x, 2, owners), swap_dp(to_y, 4, owners)
        ring_3 = (own_part(even_b, core_b, from_x, from_y, 1) + ring_2.astype(F32)).astype(BF)
        ring_3 = to_ring_succ(ring_3, shards)
        small = (small + swap_line(small, 1)) + (swap_line(small, 2) + swap_line(small, 3))
        input_grad = finish_input(da_back)
        small, attn_x, attn_y, ring_3, input_grad = lax.optimization_barrier((small, attn_x, attn_y, ring_3, input_grad))
        moving = own_part(attn_even, attn_core, attn_x, attn_y, 1).astype(BF)
        mlp_sum = own_part(even_a, core_a, back_x, back_y, 0) + ring_3.astype(F32)
        mlp_new = ()
        for slot in range(1, shards):
            moving, mlp_sum = lax.optimization_barrier((moving, mlp_sum))
            moving = to_ring_succ(moving, shards)
            mlp_new = soap_mlp(mlp_sum, slot - 1, 1, mlp_new)
            moving, mlp_new = lax.optimization_barrier((moving, tuple(mlp_new)))
            moving = moving.astype(F32) + own_part(attn_even, attn_core, attn_x, attn_y, (slot + 1) % shards)
            if slot + 1 < shards:
                moving = moving.astype(BF)
        attn_sum = moving
    else:
        attn_sum = reduce_pieces(attn_even, attn_odd, slab // 2, owners, shards)
        small = all_sum(small, owners, shards)
        mlp_new = soap_mlp(mlp_sum)
        input_grad = finish_input(send_back(da_far))
    gain_grad = small[:2]
    stat_sums = small[2]

    attn_grad = attn_sum
    attn_first_new, attn_second_new, attn_update, attn_scale = soap(
        scalars, attn_sum, attn_first, attn_second, attn_left, attn_right, False
    )
    mlp_grad, mlp_first_new, mlp_second_new, mlp_update = (flip(v) for v in (mlp_sum, *mlp_new[:3]))
    mlp_scale = mlp_new[3]
    gain_first_new = beta_first * gain_first + (1.0 - beta_first) * gain_grad
    gain_second_new = beta_second * gain_second + (1.0 - beta_second) * gain_grad * gain_grad
    gain_update = -step_size * gain_first_new / (jnp.sqrt(gain_second_new) + ADAM_EPS)
    root_means = jnp.sqrt(stat_sums[:4] / (stat_sums[4] * width))
    norm_scale = jnp.concatenate([attn_scale[:, :1, :1], mlp_scale[:, :1, :1]], axis=0)
    return (
        output, input_grad, attn_grad, mlp_grad, gain_grad,
        attn_first_new, attn_second_new, mlp_first_new, mlp_second_new,
        gain_first_new, gain_second_new, attn_update, mlp_update, gain_update,
        norm_scale, root_means,
    )


def solution(mesh):
    rows = P(("dp", "tensor"), None)
    block = P(None, "dp", "tensor")
    return jax.shard_map(
        per_device,
        mesh=mesh,
        in_specs=(rows, rows, block, block, P()) + (block,) * 8 + (P(),) * 3 + (P("dp"),) * 3 + (P(),) * 4,
        out_specs=(rows, rows, block, block, P(), block, block, block, block, P(), P(), block, block, P(), block, P()),
        check_vma=False,
    )
```

```python
import functools
import math

import jax
import jax.numpy as jnp
from jax import lax
from jax.experimental import pallas as pl
from jax.experimental.pallas import tpu as pltpu
from jax.sharding import PartitionSpec as P

HEAD_DIM = 64
SEQ_LEN = 1024
NORM_EPS = 1e-05
ROPE_BASE = 160000.0
ADAM_EPS = 1e-08
SCALE_EPS = 1e-06
PRECISE = lax.Precision.HIGHEST
BF = jnp.bfloat16
F32 = jnp.float32
ANY = pl.ANY


def dot(a,b,ca,cb):
    return lax.dot_general(a,b,(((ca,),(cb,)),((),())),preferred_element_type=F32)

def turn(x, cos, sin, lower):
    w=x.shape[1]
    sw=jnp.where(lower, pltpu.roll(x, w-32, 1), pltpu.roll(x, 32, 1))
    return x*cos+sw*sin

def lower_lanes(rows, cols):
    return lax.broadcasted_iota(jnp.int32,(rows,cols),1)%64<32

def wide(t, n):
    return t if n==1 else jnp.concatenate([t]*n,axis=1)

def fetch_pieces(refs, metas, perm, step, copy):
    for ref, meta in zip(refs, metas):
        if meta is None:
            for r in range(ref.shape[0]):
                copy(ref.at[r, step], perm[r])
        else:
            r, first, count, total = meta
            if count == total:
                copy(ref.at[step], perm[r])
            else:
                @pl.when((step >= first) & (step < first + count))
                def _(ref=ref, r=r, first=first):
                    copy(ref.at[jnp.clip(step - first, 0, ref.shape[0] - 1)], perm[r])

def fwd_attn_kernel(perm, a1, hid, gain, cos, sin, kseg, qseg, keep, *rest, T, KV, C, metas, S, SLAB, QB, S0, N):
    wps = rest[:len(metas)]
    rest = rest[len(metas):]
    if S0:
        acc_in, rest = rest[0], rest[6:]
    q_out, k_out, v_out, o_out, lse_out = rest[:5]
    if S0+N==S:
        resid_out, a2_out, stat_out, acc = rest[5:9]
    else:
        acc = rest[5]
    W, bias, osc, sem = rest[-4:]
    s=pl.program_id(0)
    def fetch(step, slot):
        fetch_pieces(wps, metas, perm, S0+step, lambda src, blk: pltpu.make_async_copy(src, W.at[slot, :, pl.ds(pl.multiple_of(blk*SLAB,SLAB),SLAB), :], sem.at[slot]).start())
    slot=lax.rem(s,2)
    @pl.when(s==0)
    def _():
        fetch(0,0)
        row=lax.broadcasted_iota(jnp.int32,(KV,T),0); col=lax.broadcasted_iota(jnp.int32,(KV,T),1)
        ok=(kseg[...]==qseg[...])|(row==col)
        bias[...]=jnp.where(ok,0.0,-1e30)
        acc[...]=acc_in[...] if S0 else jnp.zeros_like(acc)
    @pl.when(s+1<N)
    def _(): fetch(s+1,1-slot)
    pltpu.make_async_copy(W.at[slot],W.at[slot],sem.at[slot]).wait()
    n=C//128
    low_q=lower_lanes(T,C); low_k=lower_lanes(KV,C)
    cw=wide(cos[...],n); sw=wide(sin[...],n)
    q=dot(a1[:T,:],W[slot,0],1,0)
    q_out[0]=(turn(q,cw[:T],sw[:T],low_q).astype(BF)*BF(1/math.sqrt(HEAD_DIM))).astype(BF)
    k=dot(a1[...],W[slot,1],1,0)
    k_out[0]=turn(k,cw,sw,low_k).astype(BF)
    v_out[0]=dot(a1[...],W[slot,2],1,0).astype(BF)
    for p in range(n):
        kp=k_out[0,:,p*128:(p+1)*128]; vp=v_out[0,:,p*128:(p+1)*128]
        for b in range(T//QB):
            qp=q_out[0,b*QB:(b+1)*QB,p*128:(p+1)*128]
            half=lax.broadcasted_iota(jnp.int32,qp.shape,1)<64
            parts=[]
            for h in range(2):
                qm=jnp.where(half if h==0 else ~half,qp,jnp.zeros_like(qp))
                st=dot(kp,qm,1,1)+bias[:,b*QB:(b+1)*QB]
                m=jnp.max(st,axis=0,keepdims=True)
                e=jnp.exp(st-m)
                l=jnp.sum(e,axis=0,keepdims=True)
                ot=dot(vp,e.astype(BF),0,0)
                parts.append(ot[h*64:(h+1)*64]*(1.0/l))
                lse_out[0,pl.ds(2*p+h,1),b*QB:(b+1)*QB]=m+jnp.log(l)
            op=jnp.concatenate(parts,axis=0)
            osc[b*QB:(b+1)*QB,p*128:(p+1)*128]=op.T.astype(BF)
    o_out[0]=osc[...]
    acc[...]+=dot(osc[...],W[slot,3],1,1)
    if S0+N<S:
        return
    @pl.when(s==N-1)
    def _():
        at=acc[...]
        rs=hid[...].astype(F32)+at
        resid_out[...]=rs
        mu=jnp.mean(rs,axis=1,keepdims=True); ce=rs-mu
        var=jnp.mean(ce*ce,axis=1,keepdims=True)
        a2_out[...]=(ce*lax.rsqrt(var+NORM_EPS)*gain[...]).astype(BF)
        kp=keep[...]
        s1=jnp.sum(kp*at*at,axis=0,keepdims=True); s2=jnp.sum(kp*rs*rs,axis=0,keepdims=True)
        stat_out[...]=jnp.concatenate([s1,s2],axis=0)

def full(shape):
    nd=len(shape)
    return pl.BlockSpec(shape,lambda *a:(0,)*nd)

def fwd_attn(perm,a1,hid,gain,cos,sin,kseg,qseg,keep,pieces,S0=0,N=None,carry=(),QB=512):
    wps,metas,S,SLAB,C=pieces
    N=S if N is None else N
    KV,D=a1.shape; T=hid.shape[0]; HG=C//HEAD_DIM
    A=pl.BlockSpec(memory_space=ANY)
    sb=lambda rows:pl.BlockSpec((1,rows,C),lambda s,p:(s+S0,0,0))
    sd=jax.ShapeDtypeStruct
    last=S0+N==S
    tail=[sd((T,D),F32),sd((T,D),BF),sd((2,D),F32)] if last else [sd((T,D),F32)]
    gs=pltpu.PrefetchScalarGridSpec(num_scalar_prefetch=1,grid=(N,),
        in_specs=[full((KV,D)),full((T,D)),full((1,D)),full((KV,128)),full((KV,128)),full((KV,1)),full((1,T)),full((T,1))]+[A]*len(wps)+([full((T,D))]+[A]*5 if S0 else []),
        out_specs=[sb(T),sb(KV),sb(KV),sb(T),pl.BlockSpec((1,HG,T),lambda s,p:(s+S0,0,0))]+[full(t.shape) for t in tail],
        scratch_shapes=([pltpu.VMEM((T,D),F32)] if last else [])+[pltpu.VMEM((2,4,D,C),BF),pltpu.VMEM((KV,T),F32),pltpu.VMEM((T,C),BF),pltpu.SemaphoreType.DMA((2,))])
    return pl.pallas_call(functools.partial(fwd_attn_kernel,T=T,KV=KV,C=C,metas=metas,S=S,SLAB=SLAB,QB=min(QB,T),S0=S0,N=N),grid_spec=gs,
        out_shape=[sd((S,T,C),BF),sd((S,KV,C),BF),sd((S,KV,C),BF),sd((S,T,C),BF),sd((S,HG,T),F32)]+tail,
        input_output_aliases={10+len(wps)+i:i for i in range(5)} if S0 else {},
        cost_estimate=pl.CostEstimate(flops=1,transcendentals=0,bytes_accessed=1),name="attn_fwd")(perm,a1,hid,gain,cos,sin,kseg,qseg,keep,*wps,*((carry[5],)+tuple(carry[:5]) if S0 else ()))

def gelu_parts(x):
    phi=0.5*(1.0+lax.erf(x*(1.0/math.sqrt(2.0))))
    den=jnp.exp(-0.5*x*x)*(1.0/math.sqrt(2.0*math.pi))
    return phi,den

def mlp_kernel(perm, slots, a2, g, resid, gain, keep, *rest, T, D, HC, R, metas, S, SLAB, TB, S0, N):
    wps = rest[:len(metas)]
    rest = rest[len(metas):]
    if S0:
        y_in, da_in = rest[:2]
        rest = rest[2:]
    if S0+N==S:
        out, dres_out, dresb_out, dresT_out, gg_out, stat_out = rest[:6]
        rest = rest[6:]
        d0, d1, y, da = rest[:4]
    else:
        y, da, d0, d1 = rest[:4]
    W, stg, hT, dgT, duT, sem, osem = rest[4:]
    s=pl.program_id(0)
    slot=lax.rem(s,2)
    def fetch(step, sl):
        fetch_pieces(wps, metas, perm, S0+step, lambda src, blk: pltpu.make_async_copy(src, W.at[sl, :, :, pl.ds(pl.multiple_of(blk*SLAB,SLAB),SLAB)], sem.at[sl]).start())
    @pl.when(s==0)
    def _(): fetch(0,0)
    @pl.when(s+1<N)
    def _(): fetch(s+1,1-slot)
    pltpu.make_async_copy(W.at[slot],W.at[slot],sem.at[slot]).wait()
    for b in range(T//TB):
        lo,hi=b*TB,(b+1)*TB
        ga=dot(W[slot,0],a2[lo:hi,:],1,1)
        up=dot(W[slot,1],a2[lo:hi,:],1,1)
        dh=dot(W[slot,2],g[lo:hi,:],1,1)
        phi,den=gelu_parts(ga)
        ge=ga*phi
        hT[:,lo:hi]=(ge*up).astype(BF)
        dgT[:,lo:hi]=(dh*up*(phi+ga*den)).astype(BF)
        duT[:,lo:hi]=(dh*ge).astype(BF)
    yc=dot(hT[...],W[slot,2],0,0)
    dc=dot(dgT[...],W[slot,0],0,0)+dot(duT[...],W[slot,1],0,0)
    @pl.when(s==0)
    def _():
        y[...]=yc+y_in[...] if S0 else yc
        da[...]=dc+da_in[...] if S0 else dc
    @pl.when(s>0)
    def _():
        y[...]+=yc; da[...]+=dc
    @pl.when(s>=2)
    def _(): pltpu.make_async_copy(stg.at[slot],stg.at[slot],osem.at[slot]).wait()
    stg[slot,0]=dot(dgT[...],a2[...],1,0).astype(BF)
    stg[slot,1]=dot(duT[...],a2[...],1,0).astype(BF)
    stg[slot,2]=dot(hT[...],g[...],1,0).astype(BF)
    for r in range(R):
        dst=(d0,d1)[r%2]
        pltpu.make_async_copy(stg.at[slot,:,:,pl.ds(pl.multiple_of(perm[R+r]*SLAB,SLAB),SLAB)], dst.at[r//2, slots[S0+s]-S0], osem.at[slot]).start()
    if S0+N==S:
        @pl.when(s==N-1)
        def _():
            br=y[...]; rs=resid[...]; gf=g[...].astype(F32)
            res=rs+br
            out[...]=res.astype(BF)
            kp=keep[...]
            s1=jnp.sum(kp*br*br,axis=0,keepdims=True); s2=jnp.sum(kp*res*res,axis=0,keepdims=True)
            stat_out[...]=jnp.concatenate([s1,s2],axis=0)
            mu=jnp.mean(rs,axis=1,keepdims=True); ce=rs-mu
            rstd=lax.rsqrt(jnp.mean(ce*ce,axis=1,keepdims=True)+NORM_EPS)
            xh=ce*rstd
            d=da[...]
            gg_out[...]=jnp.sum(d*xh,axis=0,keepdims=True)
            e=d*gain[...]
            dr=gf+rstd*(e-jnp.mean(e,axis=1,keepdims=True)-xh*jnp.mean(e*xh,axis=1,keepdims=True))
            dres_out[...]=dr
            db=dr.astype(BF)
            dresb_out[...]=db
            dresT_out[...]=dr.T.astype(BF)
    @pl.when(s==N-1)
    def _():
        for sl in range(min(N,2)):
            pltpu.make_async_copy(stg.at[sl],stg.at[sl],osem.at[sl]).wait()

def mlp(perm2,slots,a2,g,resid,gain,keep,pieces,S0=0,N=None,carry=(),TB=256):
    wps,metas,S,SLAB,HC=pieces
    N=S if N is None else N
    R=perm2.shape[0]//2
    T,D=a2.shape
    A=pl.BlockSpec(memory_space=ANY)
    sd=jax.ShapeDtypeStruct
    last=S0+N==S
    outs=[sd((T,D),BF),sd((T,D),F32),sd((T,D),BF),sd((D,T),BF),sd((1,D),F32),sd((2,D),F32)] if last else [sd((T,D),F32)]*2
    gs=pltpu.PrefetchScalarGridSpec(num_scalar_prefetch=2,grid=(N,),
        in_specs=[full((T,D)),full((T,D)),full((T,D)),full((1,D)),full((T,1))]+[A]*len(wps)+[full((T,D))]*len(carry),
        out_specs=[full(o.shape) for o in outs]+[A,A],
        scratch_shapes=([pltpu.VMEM((T,D),F32)]*2 if last else [])+[pltpu.VMEM((2,3,HC,D),BF),pltpu.VMEM((2,3,HC,D),BF)]+[pltpu.VMEM((HC,T),BF)]*3+[pltpu.SemaphoreType.DMA((2,)),pltpu.SemaphoreType.DMA((2,))])
    piece=sd((R//2,N,3,HC,SLAB),BF)
    return pl.pallas_call(functools.partial(mlp_kernel,T=T,D=D,HC=HC,R=R,metas=metas,S=S,SLAB=SLAB,TB=min(TB,T),S0=S0,N=N),grid_spec=gs,
        out_shape=outs+[piece,piece],
        cost_estimate=pl.CostEstimate(flops=1,transcendentals=0,bytes_accessed=1),name="mlp_both")(perm2,slots,a2,g,resid,gain,keep,*wps,*carry)

def bwd_attn_kernel(perm, dres, cos, sin, kseg, qseg, q_in, k_in, v_in, lse_in, *rest, T, KV, C, metas, S, SLAB, S0, N):
    wps = rest[:len(metas)]
    dq_out, dk_out, dv_out, W, bias, dob, dqs, dks, sem = rest[-9:]
    s=pl.program_id(0)
    slot=lax.rem(s,2)
    def fetch(step, sl):
        fetch_pieces(wps, metas, perm, S0+step, lambda src, blk: pltpu.make_async_copy(src.at[3], W.at[sl, pl.ds(pl.multiple_of(blk*SLAB,SLAB),SLAB), :], sem.at[sl]).start())
    @pl.when(s==0)
    def _():
        fetch(0,0)
        row=lax.broadcasted_iota(jnp.int32,(KV,T),0); col=lax.broadcasted_iota(jnp.int32,(KV,T),1)
        ok=(kseg[...]==qseg[...])|(row==col)
        bias[...]=jnp.where(ok,0.0,-1e30)
    @pl.when(s+1<N)
    def _(): fetch(s+1,1-slot)
    pltpu.make_async_copy(W.at[slot],W.at[slot],sem.at[slot]).wait()
    n=C//128
    dob[...]=dot(dres[...],W[slot],1,0).astype(BF)
    for p in range(n):
        kp=k_in[0,:,p*128:(p+1)*128]; vp=v_in[0,:,p*128:(p+1)*128]
        qp=q_in[0,:,p*128:(p+1)*128]; dp_=dob[:,p*128:(p+1)*128]
        half=lax.broadcasted_iota(jnp.int32,qp.shape,1)<64
        parts=[]
        dvs=None
        for h in range(2):
            mk=half if h==0 else ~half
            qm=jnp.where(mk,qp,jnp.zeros_like(qp)); dm=jnp.where(mk,dp_,jnp.zeros_like(dp_))
            pt=jnp.exp(dot(kp,qm,1,1)+bias[...]-lse_in[0,2*p+h:2*p+h+1,:])
            dpt=dot(vp,dm,1,1)
            delta=jnp.sum(pt*dpt,axis=0,keepdims=True)
            ds=(pt*(dpt-delta)).astype(BF)
            dv=dot(pt.astype(BF),dm,1,0); dk=dot(ds,qm,1,0)
            dqt=dot(kp,ds,0,0)
            parts.append(dqt[h*64:(h+1)*64])
            if h==0: dva,dka=dv,dk
            else: dva,dka=dva+dv,dka+dk
        dqs[:,p*128:(p+1)*128]=jnp.concatenate(parts,axis=0).T*(1.0/math.sqrt(HEAD_DIM))
        dks[:,p*128:(p+1)*128]=dka
        dv_out[0,:,p*128:(p+1)*128]=dva.astype(BF)
    cw=wide(cos[...],n); sw=wide(sin[...],n)
    dq_out[0]=turn(dqs[...],cw[:T],-sw[:T],lower_lanes(T,C)).astype(BF)
    dk_out[0]=turn(dks[...],cw,-sw,lower_lanes(KV,C)).astype(BF)

def bwd_attn(perm,dres,cos,sin,kseg,qseg,q,k,v,lse,pieces,S0=0,N=None,carry=()):
    wps,metas,S,SLAB,C=pieces
    T,D=dres.shape; KV=k.shape[1]; HG=C//HEAD_DIM
    N=S if N is None else N
    ib=lambda rows:pl.BlockSpec((1,rows,C),lambda s,p:(s+S0,0,0))
    gs=pltpu.PrefetchScalarGridSpec(num_scalar_prefetch=1,grid=(N,),
        in_specs=[full((T,D)),full((KV,128)),full((KV,128)),full((KV,1)),full((1,T)),ib(T),ib(KV),ib(KV),pl.BlockSpec((1,HG,T),lambda s,p:(s+S0,0,0))]+[pl.BlockSpec(memory_space=ANY)]*(len(wps)+len(carry)),
        out_specs=[ib(T),ib(KV),ib(KV)],
        scratch_shapes=[pltpu.VMEM((2,D,C),BF),pltpu.VMEM((KV,T),F32),pltpu.VMEM((T,C),BF),pltpu.VMEM((T,C),F32),pltpu.VMEM((KV,C),F32),pltpu.SemaphoreType.DMA((2,))])
    sd=jax.ShapeDtypeStruct
    fl=(2*T*D*C+10*T*KV*C)*N
    return pl.pallas_call(functools.partial(bwd_attn_kernel,T=T,KV=KV,C=C,metas=metas,S=S,SLAB=SLAB,S0=S0,N=N),grid_spec=gs,
        out_shape=[sd((S,T,C),BF),sd((S,KV,C),BF),sd((S,KV,C),BF)],
        input_output_aliases={10+len(wps)+i:i for i in range(len(carry))},
        cost_estimate=pl.CostEstimate(flops=1,transcendentals=0,bytes_accessed=1),name="attn_bwd")(perm,dres,cos,sin,kseg,qseg,q,k,v,lse,*wps,*carry)

def grad_attn_kernel(perm, slots, a1T, dresT, xhat, o_in, dq_in, dk_in, dv_in, *rest, T, KV, C, R, metas, S, SLAB):
    wps = rest[:len(metas)]
    da_own, da_far, gg_out, d0, d1, W, stg, acc, sem, osem = rest[len(metas):]
    s=pl.program_id(0)
    slot=lax.rem(s,2)
    def fetch(step, sl):
        fetch_pieces(wps, metas, perm, step, lambda src, blk: pltpu.make_async_copy(src.at[pl.ds(0,3)], W.at[sl, :, pl.ds(pl.multiple_of(blk*SLAB,SLAB),SLAB), :], sem.at[sl]).start())
    @pl.when(s==0)
    def _(): fetch(0,0)
    @pl.when(s+1<S)
    def _(): fetch(s+1,1-slot)
    @pl.when(s>=2)
    def _(): pltpu.make_async_copy(stg.at[slot],stg.at[slot],osem.at[slot]).wait()
    stg[slot,0]=dot(a1T[:,:T],dq_in[0],1,0).astype(BF)
    stg[slot,1]=dot(a1T[...],dk_in[0],1,0).astype(BF)
    stg[slot,2]=dot(a1T[...],dv_in[0],1,0).astype(BF)
    stg[slot,3]=dot(dresT[...],o_in[0],1,0).astype(BF)
    for r in range(R):
        dst=(d0,d1)[r%2]
        pltpu.make_async_copy(stg.at[slot,:,pl.ds(pl.multiple_of(perm[R+r]*SLAB,SLAB),SLAB),:], dst.at[r//2, slots[s]], osem.at[slot]).start()
    pltpu.make_async_copy(W.at[slot],W.at[slot],sem.at[slot]).wait()
    c=dot(dk_in[0],W[slot,1],1,1)+dot(dv_in[0],W[slot,2],1,1)
    cq=dot(dq_in[0],W[slot,0],1,1)
    @pl.when(s==0)
    def _():
        acc[...]=c
        acc[:T,:]=acc[:T,:]+cq
    @pl.when(s>0)
    def _():
        acc[...]=acc[...]+c
        acc[:T,:]=acc[:T,:]+cq
    @pl.when(s==S-1)
    def _():
        gg_out[...]=jnp.sum(acc[...]*xhat[...].astype(F32),axis=0,keepdims=True)
        da_own[...]=acc[:T,:]
        da_far[...]=acc[T:,:].astype(BF)
        for sl in range(min(S,2)):
            pltpu.make_async_copy(stg.at[sl],stg.at[sl],osem.at[sl]).wait()

def grad_attn(perm2,slots,a1T,dresT,xhat,o,dq,dk,dv,pieces):
    wps,metas,S,SLAB,C=pieces
    R=perm2.shape[0]//2
    D,T=dresT.shape; KV=dk.shape[1]
    A=pl.BlockSpec(memory_space=ANY)
    ib=lambda rows:pl.BlockSpec((1,rows,C),lambda s,p,q:(s,0,0))
    gs=pltpu.PrefetchScalarGridSpec(num_scalar_prefetch=2,grid=(S,),
        in_specs=[full((D,KV)),full((D,T)),full((KV,D)),ib(T),ib(T),ib(KV),ib(KV)]+[A]*len(wps),
        out_specs=[full((T,D)),full((KV-T,D)),full((1,D)),A,A],
        scratch_shapes=[pltpu.VMEM((2,3,D,C),BF),pltpu.VMEM((2,4,D,C),BF),pltpu.VMEM((KV,D),F32),pltpu.SemaphoreType.DMA((2,)),pltpu.SemaphoreType.DMA((2,))])
    sd=jax.ShapeDtypeStruct
    piece=sd((R//2,S,4,SLAB,C),BF)
    return pl.pallas_call(functools.partial(grad_attn_kernel,T=T,KV=KV,C=C,R=R,metas=metas,S=S,SLAB=SLAB),grid_spec=gs,
        out_shape=[sd((T,D),F32),sd((KV-T,D),BF),sd((1,D),F32),piece,piece],
        cost_estimate=pl.CostEstimate(flops=1,transcendentals=0,bytes_accessed=1),name="attn_grad")(perm2,slots,a1T,dresT,xhat,o,dq,dk,dv,*wps)

def split3(x):
    hi=x.astype(BF)
    return hi,(x-hi.astype(F32)).astype(BF)

def dot3(a,b,ca,cb):
    ah,al=a; bh,bl=b
    return dot(ah,bh,ca,cb)+(dot(ah,bl,ca,cb)+dot(al,bh,ca,cb))

def soap_kernel(sc, g_in, first, second, left, right, *rest, turned):
    f_out, s_out, u_out, n_out = rest[-4:]
    step,b1,b2=sc[0],sc[1],sc[2]
    ql=split3(left[0]); qr=split3(right[0])
    if turned:
        x=dot3(split3(g_in[0]),ql,1,0)
        r=dot3(split3(x),qr,0,0).T
    else:
        x=dot3(ql,split3(g_in[0]),0,0)
        r=dot3(split3(x),qr,1,0)
    fn=b1*first[0]+(1.0-b1)*r
    sn=b2*second[0]+(1.0-b2)*r*r
    f_out[0]=fn; s_out[0]=sn
    n=fn/(jnp.sqrt(sn)+ADAM_EPS)
    if turned:
        t=dot3(split3(dot3(qr,split3(n),1,0)),ql,1,1)
    else:
        t=dot3(split3(dot3(ql,split3(n),1,0)),qr,1,1)
    size=n.shape[0]*n.shape[1]
    fac=jnp.sqrt(jnp.sum(n*n,keepdims=True)*(1.0/size))*lax.rsqrt(jnp.sum(t*t,keepdims=True)*(1.0/size)+SCALE_EPS)
    u_out[0]=(-step*fac)*t
    n_out[0]=jnp.broadcast_to(fac,(8,128))

def soap(scalars,g,first,second,left,right,turned,K0=0,N=None,carry=()):
    K=first.shape[0]
    N=K if N is None else N
    b=lambda x:pl.BlockSpec((1,)+x.shape[1:],lambda k,s:(k+K0,0,0))
    sd=jax.ShapeDtypeStruct
    o=sd(first.shape,F32)
    outs=[o,o,o,sd((K,8,128),F32)]
    gs=pltpu.PrefetchScalarGridSpec(num_scalar_prefetch=1,grid=(N,),
        in_specs=[b(x) for x in (g,first,second,left,right)]+[pl.BlockSpec(memory_space=ANY)]*len(carry),out_specs=[b(x) for x in outs])
    return pl.pallas_call(functools.partial(soap_kernel,turned=turned),grid_spec=gs,out_shape=outs,
        input_output_aliases={6+i:i for i in range(len(carry))},
        cost_estimate=pl.CostEstimate(flops=1,transcendentals=0,bytes_accessed=1),
        name="soap_"+("mlp" if turned else "attn"))(scalars,g,first,second,left,right,*carry)

def norm_kernel(own, far, gain, a1, a1T, xh, *, T):
    for lo,ref in ((0,own),(T,far)):
        v=ref[...].astype(F32)
        ce=v-jnp.mean(v,axis=1,keepdims=True)
        x=ce*lax.rsqrt(jnp.mean(ce*ce,axis=1,keepdims=True)+NORM_EPS)
        n=ref.shape[0]
        xh[lo:lo+n,:]=x.astype(BF)
        y=x*gain[...]
        a1[lo:lo+n,:]=y.astype(BF)
        a1T[:,lo:lo+n]=y.T.astype(BF)

def norm_first(own,far,gain):
    T,D=own.shape; KV=T+far.shape[0]
    sd=jax.ShapeDtypeStruct
    outs=[sd((KV,D),BF),sd((D,KV),BF),sd((KV,D),BF)]
    return pl.pallas_call(functools.partial(norm_kernel,T=T),grid=(1,),in_specs=[full(x.shape) for x in (own,far,gain)],
        out_specs=[full(o.shape) for o in outs],out_shape=outs,
        cost_estimate=pl.CostEstimate(flops=1,transcendentals=0,bytes_accessed=1),name="norm_first")(own,far,gain)

def input_kernel(hid, da, dres, gain, *rest):
    out=rest[-1]
    v=hid[...].astype(F32)
    ce=v-jnp.mean(v,axis=1,keepdims=True)
    rstd=lax.rsqrt(jnp.mean(ce*ce,axis=1,keepdims=True)+NORM_EPS)
    x=ce*rstd
    d=da[...]
    for r in rest[:-1]:
        d=d+r[...].astype(F32)
    e=d*gain[...]
    out[...]=(dres[...]+rstd*(e-jnp.mean(e,axis=1,keepdims=True)-x*jnp.mean(e*x,axis=1,keepdims=True))).astype(BF)

def input_back(hid,da,dres,gain,*back):
    args=(hid,da,dres,gain)+back
    return pl.pallas_call(input_kernel,grid=(1,),in_specs=[full(x.shape) for x in args],out_specs=full(hid.shape),
        out_shape=jax.ShapeDtypeStruct(hid.shape,BF),
        cost_estimate=pl.CostEstimate(flops=1,transcendentals=0,bytes_accessed=1),name="input_back")(*args)


def ring_order(count):
    return list(range(0, count, 2)) + list(range(1, count, 2))[::-1]


def swap_dp(value, bit, owners):
    return lax.ppermute(value, "dp", [(i, i ^ bit) for i in range(owners)])


def to_ring_pred(value, shards):
    ring = ring_order(shards)
    return lax.ppermute(
        value, "tensor", [(ring[p], ring[(p - 1) % shards]) for p in range(shards)]
    )


def to_ring_succ(value, shards):
    ring = ring_order(shards)
    return lax.ppermute(
        value, "tensor", [(ring[p], ring[(p + 1) % shards]) for p in range(shards)]
    )


def along_line(value, steps, shards):
    ring = ring_order(shards)
    return lax.ppermute(
        value, "tensor", [(ring[p], ring[(p + steps) % shards]) for p in range(shards)]
    )


def add_low(one, two):
    return (one.astype(F32) + two.astype(F32)).astype(BF)


def halve(pieces, bits, owners):
    for bit in bits:
        live = sorted(bits[bits.index(bit):], reverse=True)
        axis = live.index(bit)
        send = lax.index_in_dim(pieces, 1, axis, keepdims=False)
        keep = lax.index_in_dim(pieces, 0, axis, keepdims=False)
        pieces = add_low(keep, swap_dp(send, bit, owners))
    return pieces


def reduce_pieces(even, odd, cut, owners, shards):
    mine = add_low(even, swap_dp(odd, 1, owners))
    bits = [1 << b for b in range(1, owners.bit_length() - 1)]
    mine = mine.reshape((2,) * len(bits) + mine.shape[1:])
    low = halve(mine[..., :cut, :], bits[::-1], owners)
    high = halve(mine[..., cut:, :], bits, owners)
    both = jnp.concatenate([low, high], axis=-2)
    moving = both[shards - 1]
    for left in range(shards - 2, -1, -1):
        moving = to_ring_pred(moving, shards)
        moving = moving.astype(F32) + both[left].astype(F32)
        if left:
            moving = moving.astype(BF)
    return moving


def all_sum(value, owners, shards):
    for axis, count in (("dp", owners), ("tensor", shards)):
        step = 1
        while step < count:
            value = value + lax.ppermute(value, axis, [(i, i ^ step) for i in range(count)])
            step *= 2
    return value


def after(value, *earlier):
    return lax.optimization_barrier((value,) + earlier)[0]


def add_all(*values):
    total = values[0].astype(F32)
    for value in values[1:]:
        total = total + value.astype(F32)
    return total


def gather_stack(stacked, owners):
    half = stacked.shape[0] // 2
    by_x, by_y = swap_dp(stacked, 2, owners), swap_dp(stacked, 4, owners)
    return by_x, by_y, swap_dp(by_x[:half], 4, owners), swap_dp(by_y[half:], 2, owners)


def to_core(arrays, owners):
    return [swap_dp(a, 1, owners) for a in arrays]


def with_partner(arrays, metas, owners):
    return arrays + [swap_dp(a, 1, owners) for a in arrays], metas + tuple((m[0] + 1,) + m[1:] for m in metas)


def cross_sends(even, core, half):
    low = add_all(even[3, :half], core[3, :half]).astype(BF)
    high = add_all(even[3, half:], core[3, half:]).astype(BF)
    return low, high


def side_sends(even, core, from_y, from_x, half):
    to_x = jnp.concatenate(
        [add_all(even[1, :half], core[1, :half], from_y), add_all(even[1, half:], core[1, half:])]
    ).astype(BF)
    to_y = jnp.concatenate(
        [add_all(even[2, :half], core[2, :half]), add_all(even[2, half:], core[2, half:], from_x)]
    ).astype(BF)
    return to_x, to_y


def own_part(even, core, from_x, from_y, slot):
    return add_all(even[0, slot], core[0, slot], from_x[slot], from_y[slot])


def ring_sum(even, core, from_x, from_y, shards):
    moving = None
    for slot in list(range(1, shards)) + [0]:
        part = own_part(even, core, from_x, from_y, slot)
        if moving is not None:
            part = part + to_ring_succ(moving, shards).astype(F32)
        moving = part.astype(BF)
    return part


def per_device(
    hidden_in, out_grad, attn_weight, mlp_weight, norm_gain,
    attn_first, attn_second, attn_left, attn_right,
    mlp_first, mlp_second, mlp_left, mlp_right,
    gain_first, gain_second, owner_rows, segment_ids, positions, valid,
    step, learn_rate, beta_first, beta_second,
):
    owners = lax.axis_size("dp")
    shards = lax.axis_size("tensor")
    dp_index = lax.axis_index("dp")
    place = lax.axis_index("tensor")
    rows, width = hidden_in.shape
    slab = attn_weight.shape[1]
    hid_cols = mlp_weight.shape[2]
    span = SEQ_LEN // rows
    within = place % span
    base = place - within
    half = shards // 2
    gain_rows = norm_gain.astype(F32)

    def from_peer(value, ahead):
        pairs = [(g + (w + ahead) % span, g + w) for g in range(0, shards, span) for w in range(span)]
        return lax.ppermute(value, "tensor", pairs)

    def sequence_rows(column):
        return jnp.concatenate(
            [lax.dynamic_slice_in_dim(column, (base + (within + d) % span) * rows, rows, 0) for d in range(span)]
        )

    joined = 128 // slab if slab < 128 else 1
    fast = owners == 8 and joined == 1 and shards == 4 and span == 2
    both = ("dp", "tensor")
    mlp_turned = jnp.swapaxes(mlp_weight, 1, 2)
    if not fast:
        attn_all = lax.all_gather(attn_weight, both, axis=0, tiled=False).reshape((owners, shards) + attn_weight.shape)
        mlp_all = lax.all_gather(mlp_turned, both, axis=0, tiled=False).reshape((owners, shards) + mlp_turned.shape)

    slot_ids = jnp.arange(owners, dtype=jnp.int32)
    rel_owner = jnp.sum(
        jnp.where((slot_ids[:, None] ^ dp_index) == slot_ids[None, :], owner_rows[None, :], 0), axis=1
    )
    ring = ring_order(shards)
    ring_place = jnp.array([ring.index(z) for z in range(shards)], jnp.int32)
    my_place = jnp.sum(jnp.where(jnp.arange(shards) == place, ring_place, 0))
    slots = (my_place - ring_place) % shards
    attn_perm = jnp.concatenate([rel_owner if fast else owner_rows, rel_owner]).astype(jnp.int32)
    if fast:
        slots = jnp.arange(shards, dtype=jnp.int32)
    if joined == 1:
        mlp_perm = attn_perm
    else:
        inverse = jnp.sum(jnp.where(owner_rows[None, :] == slot_ids[:, None], slot_ids[None, :], 0), axis=1)
        mlp_all = jnp.take(mlp_all, inverse, axis=0).reshape((owners // joined, joined) + mlp_all.shape[1:])
        mlp_all = jnp.moveaxis(mlp_all, 1, 4)
        mlp_all = mlp_all.reshape(mlp_all.shape[:4] + (joined * slab,))
        blocks = jnp.arange(owners // joined, dtype=jnp.int32)
        mlp_perm = jnp.concatenate([blocks, blocks])

    seg = sequence_rows(segment_ids)
    keep_seq = sequence_rows(valid)
    pos = sequence_rows(positions)
    half_dim = HEAD_DIM // 2
    frequency = jnp.exp(jnp.arange(half_dim, dtype=F32) * (-2.0 * math.log(ROPE_BASE) / HEAD_DIM))
    angles = pos.astype(F32)[:, None] * frequency[None, :]
    cos_half, sin_half = jnp.cos(angles), jnp.sin(angles)
    cos_table = jnp.concatenate([cos_half] * 4, axis=1)
    sin_table = jnp.concatenate([-sin_half, sin_half] * 2, axis=1)
    key_seg = jnp.where(keep_seq > 0, seg, -1)[:, None]
    query_seg = seg[None, :rows]
    keep_own = keep_seq[:rows].astype(F32)[:, None]

    first_gain, second_gain = gain_rows[0:1], gain_rows[1:2]
    if fast:
        together = lax.optimization_barrier
        mlp_x, mlp_y, mlp_z = [None] * 4, [None] * 4, [None] * 4
        line_1 = along_line(attn_weight, 1, shards)
        mlp_x[0], mlp_y[0] = swap_dp(mlp_turned, 2, owners), swap_dp(mlp_turned, 4, owners)
        tables = (cos_table, sin_table, key_seg, query_seg, keep_own, attn_perm, mlp_perm, slots, first_gain, second_gain)
        line_1, mlp_x[0], mlp_y[0] = together((line_1, mlp_x[0], mlp_y[0]))
        pair_a = jnp.stack([attn_weight, line_1])
        x_a, y_a = swap_dp(pair_a, 2, owners), swap_dp(pair_a, 4, owners)
        line_2, line_3 = along_line(line_1, 1, shards), along_line(after(attn_weight, line_1), 3, shards)
        mlp_z[0] = swap_dp(mlp_y[0], 2, owners)
        x_a, y_a, line_2, line_3, tables = together((x_a, y_a, line_2, line_3, tables))
        cos_table, sin_table, key_seg, query_seg, keep_own, attn_perm, mlp_perm, slots, first_gain, second_gain = tables
        z_a = swap_dp(x_a, 4, owners)
        far_rows = from_peer(after(hidden_in, line_2), 1)
        core_own_a, core_x_a, core_y_a = to_core([after(pair_a, line_2), x_a, y_a], owners)
        mlp_line = [mlp_turned, along_line(after(mlp_turned, core_x_a), 1, shards), None, None]
        pair_b = jnp.stack([line_2, line_3])
        z_a, mlp_z[0], core_own_a, core_x_a, core_y_a, pair_b = together((z_a, mlp_z[0], core_own_a, core_x_a, core_y_a, pair_b))
        x_b, y_b = swap_dp(pair_b, 2, owners), swap_dp(pair_b, 4, owners)
        core_z_a, core_own_b = to_core([z_a, pair_b], owners)
        normal = norm_first(hidden_in, far_rows, first_gain)
        x_b, y_b, core_z_a, core_own_b, normal, mlp_line[1] = together((x_b, y_b, core_z_a, core_own_b, tuple(normal), mlp_line[1]))
        z_b = swap_dp(y_b, 2, owners)
        core_x_b, core_y_b = to_core([x_b, y_b], owners)
        core_0 = to_core([after(a, y_b) for a in (mlp_turned, mlp_x[0], mlp_y[0], mlp_z[0])], owners)
        normal, mlp_line[1], core_x_b, core_y_b, core_0 = together((normal, mlp_line[1], core_x_b, core_y_b, core_0))
        first_norm, first_turned, xhat_low = normal

        def attn_set(arrays, first):
            return arrays, tuple((r, first, 2, shards) for r in (0, 2, 4, 6, 1, 3, 5, 7))

        sizes = (shards, slab, attn_weight.shape[2])
        arrays_a, metas_a = attn_set([pair_a, x_a, y_a, z_a, core_own_a, core_x_a, core_y_a, core_z_a], 0)
        attn_part_a = (arrays_a, metas_a, *sizes)
        mlp_x[1], mlp_y[1] = swap_dp(mlp_line[1], 2, owners), swap_dp(mlp_line[1], 4, owners)
        mlp_line[2], mlp_line[3] = along_line(mlp_line[1], 1, shards), along_line(after(mlp_turned, mlp_line[1]), 3, shards)
    else:
        far_rows = [from_peer(hidden_in, d) for d in range(1, span)]
        attn_pieces = ([attn_all], (None,), shards, slab, attn_weight.shape[2])
        first_norm, first_turned, xhat_low = norm_first(hidden_in, jnp.concatenate(far_rows), first_gain)
    back_args = (cos_table, sin_table, key_seg, query_seg)
    fwd_args = (attn_perm, first_norm, hidden_in, second_gain, cos_table, sin_table, key_seg, query_seg, keep_own)
    if fast:
        carry = fwd_attn(*fwd_args, attn_part_a, S0=0, N=half)
        z_b, mlp_x[1], mlp_y[1], mlp_line[2], mlp_line[3], carry = together(
            (z_b, mlp_x[1], mlp_y[1], mlp_line[2], mlp_line[3], tuple(carry))
        )
        core_z_b = swap_dp(z_b, 1, owners)
        core_z_b, mlp_x[1], mlp_y[1], mlp_line[2], mlp_line[3] = together((core_z_b, mlp_x[1], mlp_y[1], mlp_line[2], mlp_line[3]))
        arrays_b, metas_b = attn_set([pair_b, x_b, y_b, z_b, core_own_b, core_x_b, core_y_b, core_z_b], 2)
        attn_part_b = (arrays_b, metas_b, *sizes)
        attn_pieces = (arrays_a + arrays_b, metas_a + metas_b, *sizes)
        mlp_z[1] = swap_dp(mlp_y[1], 2, owners)
        mlp_x[2], mlp_y[2] = swap_dp(mlp_line[2], 2, owners), swap_dp(mlp_line[2], 4, owners)
        mlp_x[3], mlp_y[3] = swap_dp(mlp_line[3], 2, owners), swap_dp(mlp_line[3], 4, owners)
        out = fwd_attn(*fwd_args, attn_part_b, S0=half, N=half, carry=carry)
        mlp_z[1], mlp_x[2], mlp_y[2], mlp_y[3], mlp_x[0], mlp_x[1], out = together(
            (mlp_z[1], mlp_x[2], mlp_y[2], mlp_y[3], mlp_x[0], mlp_x[1], tuple(out))
        )
        queries, keys, values, attended, log_sums, resid, second_norm, stat_a = out

        def mlp_set(slot):
            return [mlp_line[slot], mlp_x[slot], mlp_y[slot], mlp_z[slot]]

        def mlp_pieces(*slots_of):
            arrays, metas = [], []
            for slot, got in slots_of:
                arrays += [a[None] for a in got]
                metas += [(r, slot, 1, shards) for r in (0, 2, 4, 6, 1, 3, 5, 7)]
            return arrays, tuple(metas), shards, slab, hid_cols

        set_0, set_1 = mlp_set(0), mlp_set(1)
        set_1 = [after(a, mlp_z[1]) for a in set_1]
        core_1 = to_core(set_1, owners)
        core_1, second_norm, mlp_x[2], mlp_y[3] = together((core_1, second_norm, mlp_x[2], mlp_y[3]))
        mlp_z[2], mlp_z[3] = swap_dp(mlp_x[2], 4, owners), swap_dp(mlp_y[3], 2, owners)
        core_2 = to_core([after(mlp_line[2], second_norm), mlp_x[2]], owners)
        mlp_args = (mlp_perm, slots, second_norm, out_grad, resid, second_gain, keep_own)
        out = mlp(*mlp_args, mlp_pieces((0, set_0 + core_0), (1, set_1 + core_1)), S0=0, N=half)
        mlp_x[3], mlp_z[2], mlp_z[3], core_2, out = together((mlp_x[3], mlp_z[2], mlp_z[3], core_2, tuple(out)))
        *carry, even_a, odd_a = out
        set_2, set_3 = mlp_set(2), mlp_set(3)
        set_2, set_3 = [after(a, odd_a) for a in set_2], [after(a, odd_a) for a in set_3]
        core_2, core_3 = core_2 + to_core(set_2[2:], owners), to_core(set_3, owners)
        core_a = swap_dp(odd_a, 1, owners)
        low, high = cross_sends(even_a, core_a, 1)
        low, high, core_2, core_3, carry = lax.optimization_barrier((low, high, core_2, core_3, carry))
        from_y, from_x = swap_dp(low, 4, owners), swap_dp(high, 2, owners)
        out = mlp(*mlp_args, mlp_pieces((2, set_2 + core_2), (3, set_3 + core_3)), S0=half, N=half, carry=carry)
        from_y, from_x, *out = lax.optimization_barrier((from_y, from_x, *out))
        output, dresid, dres_low, dres_turned, gain_two, stat_m, even_b, odd_b = out
        core_b = swap_dp(odd_b, 1, owners)
        to_x, to_y = side_sends(even_a, core_a, from_y, from_x, 1)
        to_x, to_y, dres_low = lax.optimization_barrier((to_x, to_y, dres_low))
        back_x, back_y = swap_dp(to_x, 2, owners), swap_dp(to_y, 4, owners)
        fwd_kept = (queries, keys, values, log_sums, attn_pieces)
        grads = bwd_attn(attn_perm, dres_low, *back_args, *fwd_kept, S0=0, N=half)
        back_x, back_y, core_b, *grads = lax.optimization_barrier((back_x, back_y, core_b, *grads))
        low, high = cross_sends(even_b, core_b, 1)
        ring_1 = own_part(even_a, core_a, back_x, back_y, 1).astype(BF)
        low, high, ring_1, dres_low = lax.optimization_barrier((low, high, ring_1, dres_low))
        from_y, from_x = swap_dp(low, 4, owners), swap_dp(high, 2, owners)
        ring_1 = to_ring_succ(ring_1, shards)
        grads = bwd_attn(attn_perm, dres_low, *back_args, *fwd_kept, S0=half, N=half, carry=tuple(grads))
        from_y, from_x, ring_1, *grads = lax.optimization_barrier((from_y, from_x, ring_1, *grads))
        to_x, to_y = side_sends(even_b, core_b, from_y, from_x, 1)
        to_x, to_y, dres_turned = lax.optimization_barrier((to_x, to_y, dres_turned))
        from_x, from_y = swap_dp(to_x, 2, owners), swap_dp(to_y, 4, owners)
        out = grad_attn(attn_perm, slots, first_turned, dres_turned, xhat_low, attended, *grads, attn_pieces)
        from_x, from_y, *out = lax.optimization_barrier((from_x, from_y, *out))
        da_own, da_far, gain_one, attn_even, attn_odd = out
    else:
        queries, keys, values, attended, log_sums, resid, second_norm, stat_a = fwd_attn(*fwd_args, attn_pieces)
        output, dresid, dres_low, dres_turned, gain_two, stat_m, mlp_even, mlp_odd = mlp(
            mlp_perm, slots, second_norm, out_grad, resid, second_gain, keep_own,
            ([mlp_all], (None,), shards, mlp_all.shape[-1], hid_cols),
        )
        if joined > 1:
            merged = jnp.stack([mlp_even, mlp_odd], axis=1).reshape((owners // joined,) + mlp_even.shape[1:])
            merged = merged.reshape(merged.shape[:-1] + (joined, slab))
            merged = jnp.moveaxis(merged, -2, 1).reshape((owners,) + mlp_even.shape[1:-1] + (slab,))
            merged = jnp.take(merged, rel_owner, axis=0)
            mlp_even, mlp_odd = merged[0::2], merged[1::2]
        mlp_sum = reduce_pieces(mlp_even, mlp_odd, -(-hid_cols // 32) * 16, owners, shards)
        grads = bwd_attn(attn_perm, dres_low, *back_args, queries, keys, values, log_sums, attn_pieces)
        da_own, da_far, gain_one, attn_even, attn_odd = grad_attn(
            attn_perm, slots, first_turned, dres_turned, xhat_low, attended, *grads, attn_pieces
        )
    def send_back(da_far):
        got = []
        for d in range(1, span):
            pairs = [(g + w, g + (w + d) % span) for g in range(0, shards, span) for w in range(span)]
            got.append(lax.ppermute(da_far[(d - 1) * rows : d * rows], "tensor", pairs))
        return got

    def swap_line(value, bit):
        return lax.ppermute(value, "tensor", [(i, i ^ bit) for i in range(shards)])

    def finish_input(da_back):
        return input_back(hidden_in, da_own, dresid, first_gain, *da_back)

    step_count = step.astype(F32)
    step_size = (
        learn_rate
        * jnp.sqrt(1.0 - jnp.power(beta_second, step_count))
        / (1.0 - jnp.power(beta_first, step_count))
    )
    scalars = jnp.stack([step_size, beta_first, beta_second])

    def flip(value):
        return jnp.swapaxes(value, 1, 2)

    def soap_mlp(total, *part):
        return soap(scalars, total, flip(mlp_first), flip(mlp_second), mlp_left, mlp_right, True, *part)

    sums = jnp.concatenate([jnp.sum(stat_a, axis=1), jnp.sum(stat_m, axis=1), jnp.sum(keep_own)[None]])
    small = jnp.concatenate([gain_one, gain_two, jnp.pad(sums, (0, width - 5))[None]], axis=0)
    if fast:
        attn_core = swap_dp(attn_odd, 1, owners)
        ring_2 = (own_part(even_b, core_b, from_x, from_y, 0) + ring_1.astype(F32)).astype(BF)
        ring_2 = to_ring_succ(ring_2, shards)
        small = small + swap_dp(small, 1, owners)
        small, attn_core = lax.optimization_barrier((small, attn_core))
        low, high = cross_sends(attn_even, attn_core, half)
        cross_y, cross_x = swap_dp(low, 4, owners), swap_dp(high, 2, owners)
        da_back = send_back(da_far)
        small = (small + swap_dp(small, 2, owners)) + (swap_dp(small, 4, owners) + swap_dp(small, 6, owners))
        small, cross_x, cross_y, da_back = lax.optimization_barrier((small, cross_x, cross_y, da_back))
        to_x, to_y = side_sends(attn_even, attn_core, cross_y, cross_x, half)
        to_x, to_y, small, ring_2 = lax.optimization_barrier((to_x, to_y, small, ring_2))
        attn_x, attn_y = swap_dp(to_x, 2, owners), swap_dp(to_y, 4, owners)
        ring_3 = (own_part(even_b, core_b, from_x, from_y, 1) + ring_2.astype(F32)).astype(BF)
        ring_3 = to_ring_succ(ring_3, shards)
        mlp_sum = own_part(even_a, core_a, back_x, back_y, 0) + ring_3.astype(F32)
        mlp_new = soap_mlp(mlp_sum)
        attn_x, attn_y, mlp_sum, mlp_new = lax.optimization_barrier((attn_x, attn_y, mlp_sum, tuple(mlp_new)))
        moving = own_part(attn_even, attn_core, attn_x, attn_y, 1).astype(BF)
        for slot in range(1, shards):
            moving, small, da_back = lax.optimization_barrier((moving, small, da_back))
            moving = to_ring_succ(moving, shards)
            if slot < 3:
                small = small + swap_line(small, slot)
            if slot == 1:
                input_grad = finish_input(da_back)
                moving, input_grad = lax.optimization_barrier((moving, input_grad))
            moving, small = lax.optimization_barrier((moving, small))
            moving = moving.astype(F32) + own_part(attn_even, attn_core, attn_x, attn_y, (slot + 1) % shards)
            if slot + 1 < shards:
                moving = moving.astype(BF)
        attn_sum = moving
    else:
        attn_sum = reduce_pieces(attn_even, attn_odd, slab // 2, owners, shards)
        small = all_sum(small, owners, shards)
        mlp_new = soap_mlp(mlp_sum)
        input_grad = finish_input(send_back(da_far))
    gain_grad = small[:2]
    stat_sums = small[2]

    attn_grad = attn_sum
    attn_first_new, attn_second_new, attn_update, attn_scale = soap(
        scalars, attn_sum, attn_first, attn_second, attn_left, attn_right, False
    )
    mlp_grad, mlp_first_new, mlp_second_new, mlp_update = (flip(v) for v in (mlp_sum, *mlp_new[:3]))
    mlp_scale = mlp_new[3]
    gain_first_new = beta_first * gain_first + (1.0 - beta_first) * gain_grad
    gain_second_new = beta_second * gain_second + (1.0 - beta_second) * gain_grad * gain_grad
    gain_update = -step_size * gain_first_new / (jnp.sqrt(gain_second_new) + ADAM_EPS)
    root_means = jnp.sqrt(stat_sums[:4] / (stat_sums[4] * width))
    norm_scale = jnp.concatenate([attn_scale[:, :1, :1], mlp_scale[:, :1, :1]], axis=0)
    return (
        output, input_grad, attn_grad, mlp_grad, gain_grad,
        attn_first_new, attn_second_new, mlp_first_new, mlp_second_new,
        gain_first_new, gain_second_new, attn_update, mlp_update, gain_update,
        norm_scale, root_means,
    )


def solution(mesh):
    rows = P(("dp", "tensor"), None)
    block = P(None, "dp", "tensor")
    return jax.shard_map(
        per_device,
        mesh=mesh,
        in_specs=(rows, rows, block, block, P()) + (block,) * 8 + (P(),) * 3 + (P("dp"),) * 3 + (P(),) * 4,
        out_specs=(rows, rows, block, block, P(), block, block, block, block, P(), P(), block, block, P(), block, P()),
        check_vma=False,
    )
```

```python
import functools
import math

import jax
import jax.numpy as jnp
from jax import lax
from jax.experimental import pallas as pl
from jax.experimental.pallas import tpu as pltpu
from jax.sharding import PartitionSpec as P

HEAD_DIM = 64
SEQ_LEN = 1024
NORM_EPS = 1e-05
ROPE_BASE = 160000.0
ADAM_EPS = 1e-08
SCALE_EPS = 1e-06
PRECISE = lax.Precision.HIGHEST
BF = jnp.bfloat16
F32 = jnp.float32
ANY = pl.ANY


def dot(a,b,ca,cb):
    return lax.dot_general(a,b,(((ca,),(cb,)),((),())),preferred_element_type=F32)

def turn(x, cos, sin, lower):
    w=x.shape[1]
    sw=jnp.where(lower, pltpu.roll(x, w-32, 1), pltpu.roll(x, 32, 1))
    return x*cos+sw*sin

def lower_lanes(rows, cols):
    return lax.broadcasted_iota(jnp.int32,(rows,cols),1)%64<32

def wide(t, n):
    return t if n==1 else jnp.concatenate([t]*n,axis=1)

def fetch_pieces(refs, metas, perm, step, copy):
    for ref, meta in zip(refs, metas):
        if meta is None:
            for r in range(ref.shape[0]):
                copy(ref.at[r, step], perm[r])
        else:
            r, first, count, total = meta
            if count == total:
                copy(ref.at[step], perm[r])
            else:
                @pl.when((step >= first) & (step < first + count))
                def _(ref=ref, r=r, first=first):
                    copy(ref.at[jnp.clip(step - first, 0, ref.shape[0] - 1)], perm[r])

def fwd_attn_kernel(perm, a1, hid, gain, cos, sin, kseg, qseg, keep, *rest, T, KV, C, metas, S, SLAB, QB, S0, N):
    wps = rest[:len(metas)]
    rest = rest[len(metas):]
    if S0:
        acc_in, rest = rest[0], rest[6:]
    q_out, k_out, v_out, o_out, lse_out = rest[:5]
    if S0+N==S:
        resid_out, a2_out, stat_out, acc = rest[5:9]
    else:
        acc = rest[5]
    W, bias, osc, sem = rest[-4:]
    s=pl.program_id(0)
    def fetch(step, slot):
        fetch_pieces(wps, metas, perm, S0+step, lambda src, blk: pltpu.make_async_copy(src, W.at[slot, :, pl.ds(pl.multiple_of(blk*SLAB,SLAB),SLAB), :], sem.at[slot]).start())
    slot=lax.rem(s,2)
    @pl.when(s==0)
    def _():
        fetch(0,0)
        row=lax.broadcasted_iota(jnp.int32,(KV,T),0); col=lax.broadcasted_iota(jnp.int32,(KV,T),1)
        ok=(kseg[...]==qseg[...])|(row==col)
        bias[...]=jnp.where(ok,0.0,-1e30)
        acc[...]=acc_in[...] if S0 else jnp.zeros_like(acc)
    @pl.when(s+1<N)
    def _(): fetch(s+1,1-slot)
    pltpu.make_async_copy(W.at[slot],W.at[slot],sem.at[slot]).wait()
    n=C//128
    low_q=lower_lanes(T,C); low_k=lower_lanes(KV,C)
    cw=wide(cos[...],n); sw=wide(sin[...],n)
    q=dot(a1[:T,:],W[slot,0],1,0)
    q_out[0]=(turn(q,cw[:T],sw[:T],low_q).astype(BF)*BF(1/math.sqrt(HEAD_DIM))).astype(BF)
    k=dot(a1[...],W[slot,1],1,0)
    k_out[0]=turn(k,cw,sw,low_k).astype(BF)
    v_out[0]=dot(a1[...],W[slot,2],1,0).astype(BF)
    for p in range(n):
        kp=k_out[0,:,p*128:(p+1)*128]; vp=v_out[0,:,p*128:(p+1)*128]
        for b in range(T//QB):
            qp=q_out[0,b*QB:(b+1)*QB,p*128:(p+1)*128]
            half=lax.broadcasted_iota(jnp.int32,qp.shape,1)<64
            parts=[]
            for h in range(2):
                qm=jnp.where(half if h==0 else ~half,qp,jnp.zeros_like(qp))
                st=dot(kp,qm,1,1)+bias[:,b*QB:(b+1)*QB]
                m=jnp.max(st,axis=0,keepdims=True)
                e=jnp.exp(st-m)
                l=jnp.sum(e,axis=0,keepdims=True)
                ot=dot(vp,e.astype(BF),0,0)
                parts.append(ot[h*64:(h+1)*64]*(1.0/l))
                lse_out[0,pl.ds(2*p+h,1),b*QB:(b+1)*QB]=m+jnp.log(l)
            op=jnp.concatenate(parts,axis=0)
            osc[b*QB:(b+1)*QB,p*128:(p+1)*128]=op.T.astype(BF)
    o_out[0]=osc[...]
    acc[...]+=dot(osc[...],W[slot,3],1,1)
    if S0+N<S:
        return
    @pl.when(s==N-1)
    def _():
        at=acc[...]
        rs=hid[...].astype(F32)+at
        resid_out[...]=rs
        mu=jnp.mean(rs,axis=1,keepdims=True); ce=rs-mu
        var=jnp.mean(ce*ce,axis=1,keepdims=True)
        a2_out[...]=(ce*lax.rsqrt(var+NORM_EPS)*gain[...]).astype(BF)
        kp=keep[...]
        s1=jnp.sum(kp*at*at,axis=0,keepdims=True); s2=jnp.sum(kp*rs*rs,axis=0,keepdims=True)
        stat_out[...]=jnp.concatenate([s1,s2],axis=0)

def full(shape):
    nd=len(shape)
    return pl.BlockSpec(shape,lambda *a:(0,)*nd)

def fwd_attn(perm,a1,hid,gain,cos,sin,kseg,qseg,keep,pieces,S0=0,N=None,carry=(),QB=512):
    wps,metas,S,SLAB,C=pieces
    N=S if N is None else N
    KV,D=a1.shape; T=hid.shape[0]; HG=C//HEAD_DIM
    A=pl.BlockSpec(memory_space=ANY)
    sb=lambda rows:pl.BlockSpec((1,rows,C),lambda s,p:(s+S0,0,0))
    sd=jax.ShapeDtypeStruct
    last=S0+N==S
    tail=[sd((T,D),F32),sd((T,D),BF),sd((2,D),F32)] if last else [sd((T,D),F32)]
    gs=pltpu.PrefetchScalarGridSpec(num_scalar_prefetch=1,grid=(N,),
        in_specs=[full((KV,D)),full((T,D)),full((1,D)),full((KV,128)),full((KV,128)),full((KV,1)),full((1,T)),full((T,1))]+[A]*len(wps)+([full((T,D))]+[A]*5 if S0 else []),
        out_specs=[sb(T),sb(KV),sb(KV),sb(T),pl.BlockSpec((1,HG,T),lambda s,p:(s+S0,0,0))]+[full(t.shape) for t in tail],
        scratch_shapes=([pltpu.VMEM((T,D),F32)] if last else [])+[pltpu.VMEM((2,4,D,C),BF),pltpu.VMEM((KV,T),F32),pltpu.VMEM((T,C),BF),pltpu.SemaphoreType.DMA((2,))])
    return pl.pallas_call(functools.partial(fwd_attn_kernel,T=T,KV=KV,C=C,metas=metas,S=S,SLAB=SLAB,QB=min(QB,T),S0=S0,N=N),grid_spec=gs,
        out_shape=[sd((S,T,C),BF),sd((S,KV,C),BF),sd((S,KV,C),BF),sd((S,T,C),BF),sd((S,HG,T),F32)]+tail,
        input_output_aliases={10+len(wps)+i:i for i in range(5)} if S0 else {},
        cost_estimate=pl.CostEstimate(flops=1,transcendentals=0,bytes_accessed=1),name="attn_fwd")(perm,a1,hid,gain,cos,sin,kseg,qseg,keep,*wps,*((carry[5],)+tuple(carry[:5]) if S0 else ()))

def gelu_parts(x):
    phi=0.5*(1.0+lax.erf(x*(1.0/math.sqrt(2.0))))
    den=jnp.exp(-0.5*x*x)*(1.0/math.sqrt(2.0*math.pi))
    return phi,den

def mlp_kernel(perm, slots, a2, g, resid, gain, keep, *rest, T, D, HC, R, metas, S, SLAB, TB, S0, N):
    wps = rest[:len(metas)]
    rest = rest[len(metas):]
    if S0:
        y_in, da_in = rest[:2]
        rest = rest[2:]
    if S0+N==S:
        out, dres_out, dresb_out, dresT_out, gg_out, stat_out = rest[:6]
        rest = rest[6:]
        d0, d1, y, da = rest[:4]
    else:
        y, da, d0, d1 = rest[:4]
    W, stg, hT, dgT, duT, sem, osem = rest[4:]
    s=pl.program_id(0)
    slot=lax.rem(s,2)
    def fetch(step, sl):
        fetch_pieces(wps, metas, perm, S0+step, lambda src, blk: pltpu.make_async_copy(src, W.at[sl, :, :, pl.ds(pl.multiple_of(blk*SLAB,SLAB),SLAB)], sem.at[sl]).start())
    @pl.when(s==0)
    def _(): fetch(0,0)
    @pl.when(s+1<N)
    def _(): fetch(s+1,1-slot)
    pltpu.make_async_copy(W.at[slot],W.at[slot],sem.at[slot]).wait()
    for b in range(T//TB):
        lo,hi=b*TB,(b+1)*TB
        ga=dot(W[slot,0],a2[lo:hi,:],1,1)
        up=dot(W[slot,1],a2[lo:hi,:],1,1)
        dh=dot(W[slot,2],g[lo:hi,:],1,1)
        phi,den=gelu_parts(ga)
        ge=ga*phi
        hT[:,lo:hi]=(ge*up).astype(BF)
        dgT[:,lo:hi]=(dh*up*(phi+ga*den)).astype(BF)
        duT[:,lo:hi]=(dh*ge).astype(BF)
    yc=dot(hT[...],W[slot,2],0,0)
    dc=dot(dgT[...],W[slot,0],0,0)+dot(duT[...],W[slot,1],0,0)
    @pl.when(s==0)
    def _():
        y[...]=yc+y_in[...] if S0 else yc
        da[...]=dc+da_in[...] if S0 else dc
    @pl.when(s>0)
    def _():
        y[...]+=yc; da[...]+=dc
    @pl.when(s>=2)
    def _(): pltpu.make_async_copy(stg.at[slot],stg.at[slot],osem.at[slot]).wait()
    stg[slot,0]=dot(dgT[...],a2[...],1,0).astype(BF)
    stg[slot,1]=dot(duT[...],a2[...],1,0).astype(BF)
    stg[slot,2]=dot(hT[...],g[...],1,0).astype(BF)
    for r in range(R):
        dst=(d0,d1)[r%2]
        pltpu.make_async_copy(stg.at[slot,:,:,pl.ds(pl.multiple_of(perm[R+r]*SLAB,SLAB),SLAB)], dst.at[r//2, slots[S0+s]-S0], osem.at[slot]).start()
    if S0+N==S:
        @pl.when(s==N-1)
        def _():
            br=y[...]; rs=resid[...]; gf=g[...].astype(F32)
            res=rs+br
            out[...]=res.astype(BF)
            kp=keep[...]
            s1=jnp.sum(kp*br*br,axis=0,keepdims=True); s2=jnp.sum(kp*res*res,axis=0,keepdims=True)
            stat_out[...]=jnp.concatenate([s1,s2],axis=0)
            mu=jnp.mean(rs,axis=1,keepdims=True); ce=rs-mu
            rstd=lax.rsqrt(jnp.mean(ce*ce,axis=1,keepdims=True)+NORM_EPS)
            xh=ce*rstd
            d=da[...]
            gg_out[...]=jnp.sum(d*xh,axis=0,keepdims=True)
            e=d*gain[...]
            dr=gf+rstd*(e-jnp.mean(e,axis=1,keepdims=True)-xh*jnp.mean(e*xh,axis=1,keepdims=True))
            dres_out[...]=dr
            db=dr.astype(BF)
            dresb_out[...]=db
            dresT_out[...]=dr.T.astype(BF)
    @pl.when(s==N-1)
    def _():
        for sl in range(min(N,2)):
            pltpu.make_async_copy(stg.at[sl],stg.at[sl],osem.at[sl]).wait()

def mlp(perm2,slots,a2,g,resid,gain,keep,pieces,S0=0,N=None,carry=(),TB=256):
    wps,metas,S,SLAB,HC=pieces
    N=S if N is None else N
    R=perm2.shape[0]//2
    T,D=a2.shape
    A=pl.BlockSpec(memory_space=ANY)
    sd=jax.ShapeDtypeStruct
    last=S0+N==S
    outs=[sd((T,D),BF),sd((T,D),F32),sd((T,D),BF),sd((D,T),BF),sd((1,D),F32),sd((2,D),F32)] if last else [sd((T,D),F32)]*2
    gs=pltpu.PrefetchScalarGridSpec(num_scalar_prefetch=2,grid=(N,),
        in_specs=[full((T,D)),full((T,D)),full((T,D)),full((1,D)),full((T,1))]+[A]*len(wps)+[full((T,D))]*len(carry),
        out_specs=[full(o.shape) for o in outs]+[A,A],
        scratch_shapes=([pltpu.VMEM((T,D),F32)]*2 if last else [])+[pltpu.VMEM((2,3,HC,D),BF),pltpu.VMEM((2,3,HC,D),BF)]+[pltpu.VMEM((HC,T),BF)]*3+[pltpu.SemaphoreType.DMA((2,)),pltpu.SemaphoreType.DMA((2,))])
    piece=sd((R//2,N,3,HC,SLAB),BF)
    return pl.pallas_call(functools.partial(mlp_kernel,T=T,D=D,HC=HC,R=R,metas=metas,S=S,SLAB=SLAB,TB=min(TB,T),S0=S0,N=N),grid_spec=gs,
        out_shape=outs+[piece,piece],
        cost_estimate=pl.CostEstimate(flops=1,transcendentals=0,bytes_accessed=1),name="mlp_both")(perm2,slots,a2,g,resid,gain,keep,*wps,*carry)

def bwd_attn_kernel(perm, dres, cos, sin, kseg, qseg, q_in, k_in, v_in, lse_in, *rest, T, KV, C, metas, S, SLAB, S0, N):
    wps = rest[:len(metas)]
    dq_out, dk_out, dv_out, W, bias, dob, dqs, dks, sem = rest[-9:]
    s=pl.program_id(0)
    slot=lax.rem(s,2)
    def fetch(step, sl):
        fetch_pieces(wps, metas, perm, S0+step, lambda src, blk: pltpu.make_async_copy(src.at[3], W.at[sl, pl.ds(pl.multiple_of(blk*SLAB,SLAB),SLAB), :], sem.at[sl]).start())
    @pl.when(s==0)
    def _():
        fetch(0,0)
        row=lax.broadcasted_iota(jnp.int32,(KV,T),0); col=lax.broadcasted_iota(jnp.int32,(KV,T),1)
        ok=(kseg[...]==qseg[...])|(row==col)
        bias[...]=jnp.where(ok,0.0,-1e30)
    @pl.when(s+1<N)
    def _(): fetch(s+1,1-slot)
    pltpu.make_async_copy(W.at[slot],W.at[slot],sem.at[slot]).wait()
    n=C//128
    dob[...]=dot(dres[...],W[slot],1,0).astype(BF)
    for p in range(n):
        kp=k_in[0,:,p*128:(p+1)*128]; vp=v_in[0,:,p*128:(p+1)*128]
        qp=q_in[0,:,p*128:(p+1)*128]; dp_=dob[:,p*128:(p+1)*128]
        half=lax.broadcasted_iota(jnp.int32,qp.shape,1)<64
        parts=[]
        dvs=None
        for h in range(2):
            mk=half if h==0 else ~half
            qm=jnp.where(mk,qp,jnp.zeros_like(qp)); dm=jnp.where(mk,dp_,jnp.zeros_like(dp_))
            pt=jnp.exp(dot(kp,qm,1,1)+bias[...]-lse_in[0,2*p+h:2*p+h+1,:])
            dpt=dot(vp,dm,1,1)
            delta=jnp.sum(pt*dpt,axis=0,keepdims=True)
            ds=(pt*(dpt-delta)).astype(BF)
            dv=dot(pt.astype(BF),dm,1,0); dk=dot(ds,qm,1,0)
            dqt=dot(kp,ds,0,0)
            parts.append(dqt[h*64:(h+1)*64])
            if h==0: dva,dka=dv,dk
            else: dva,dka=dva+dv,dka+dk
        dqs[:,p*128:(p+1)*128]=jnp.concatenate(parts,axis=0).T*(1.0/math.sqrt(HEAD_DIM))
        dks[:,p*128:(p+1)*128]=dka
        dv_out[0,:,p*128:(p+1)*128]=dva.astype(BF)
    cw=wide(cos[...],n); sw=wide(sin[...],n)
    dq_out[0]=turn(dqs[...],cw[:T],-sw[:T],lower_lanes(T,C)).astype(BF)
    dk_out[0]=turn(dks[...],cw,-sw,lower_lanes(KV,C)).astype(BF)

def bwd_attn(perm,dres,cos,sin,kseg,qseg,q,k,v,lse,pieces,S0=0,N=None,carry=()):
    wps,metas,S,SLAB,C=pieces
    T,D=dres.shape; KV=k.shape[1]; HG=C//HEAD_DIM
    N=S if N is None else N
    ib=lambda rows:pl.BlockSpec((1,rows,C),lambda s,p:(s+S0,0,0))
    gs=pltpu.PrefetchScalarGridSpec(num_scalar_prefetch=1,grid=(N,),
        in_specs=[full((T,D)),full((KV,128)),full((KV,128)),full((KV,1)),full((1,T)),ib(T),ib(KV),ib(KV),pl.BlockSpec((1,HG,T),lambda s,p:(s+S0,0,0))]+[pl.BlockSpec(memory_space=ANY)]*(len(wps)+len(carry)),
        out_specs=[ib(T),ib(KV),ib(KV)],
        scratch_shapes=[pltpu.VMEM((2,D,C),BF),pltpu.VMEM((KV,T),F32),pltpu.VMEM((T,C),BF),pltpu.VMEM((T,C),F32),pltpu.VMEM((KV,C),F32),pltpu.SemaphoreType.DMA((2,))])
    sd=jax.ShapeDtypeStruct
    fl=(2*T*D*C+10*T*KV*C)*N
    return pl.pallas_call(functools.partial(bwd_attn_kernel,T=T,KV=KV,C=C,metas=metas,S=S,SLAB=SLAB,S0=S0,N=N),grid_spec=gs,
        out_shape=[sd((S,T,C),BF),sd((S,KV,C),BF),sd((S,KV,C),BF)],
        input_output_aliases={10+len(wps)+i:i for i in range(len(carry))},
        cost_estimate=pl.CostEstimate(flops=1,transcendentals=0,bytes_accessed=1),name="attn_bwd")(perm,dres,cos,sin,kseg,qseg,q,k,v,lse,*wps,*carry)

def grad_attn_kernel(perm, slots, a1T, dresT, xhat, o_in, dq_in, dk_in, dv_in, *rest, T, KV, C, R, metas, S, SLAB):
    wps = rest[:len(metas)]
    da_own, da_far, gg_out, d0, d1, W, stg, acc, sem, osem = rest[len(metas):]
    s=pl.program_id(0)
    slot=lax.rem(s,2)
    def fetch(step, sl):
        fetch_pieces(wps, metas, perm, step, lambda src, blk: pltpu.make_async_copy(src.at[pl.ds(0,3)], W.at[sl, :, pl.ds(pl.multiple_of(blk*SLAB,SLAB),SLAB), :], sem.at[sl]).start())
    @pl.when(s==0)
    def _(): fetch(0,0)
    @pl.when(s+1<S)
    def _(): fetch(s+1,1-slot)
    @pl.when(s>=2)
    def _(): pltpu.make_async_copy(stg.at[slot],stg.at[slot],osem.at[slot]).wait()
    stg[slot,0]=dot(a1T[:,:T],dq_in[0],1,0).astype(BF)
    stg[slot,1]=dot(a1T[...],dk_in[0],1,0).astype(BF)
    stg[slot,2]=dot(a1T[...],dv_in[0],1,0).astype(BF)
    stg[slot,3]=dot(dresT[...],o_in[0],1,0).astype(BF)
    for r in range(R):
        dst=(d0,d1)[r%2]
        pltpu.make_async_copy(stg.at[slot,:,pl.ds(pl.multiple_of(perm[R+r]*SLAB,SLAB),SLAB),:], dst.at[r//2, slots[s]], osem.at[slot]).start()
    pltpu.make_async_copy(W.at[slot],W.at[slot],sem.at[slot]).wait()
    c=dot(dk_in[0],W[slot,1],1,1)+dot(dv_in[0],W[slot,2],1,1)
    cq=dot(dq_in[0],W[slot,0],1,1)
    @pl.when(s==0)
    def _():
        acc[...]=c
        acc[:T,:]=acc[:T,:]+cq
    @pl.when(s>0)
    def _():
        acc[...]=acc[...]+c
        acc[:T,:]=acc[:T,:]+cq
    @pl.when(s==S-1)
    def _():
        gg_out[...]=jnp.sum(acc[...]*xhat[...].astype(F32),axis=0,keepdims=True)
        da_own[...]=acc[:T,:]
        da_far[...]=acc[T:,:].astype(BF)
        for sl in range(min(S,2)):
            pltpu.make_async_copy(stg.at[sl],stg.at[sl],osem.at[sl]).wait()

def grad_attn(perm2,slots,a1T,dresT,xhat,o,dq,dk,dv,pieces):
    wps,metas,S,SLAB,C=pieces
    R=perm2.shape[0]//2
    D,T=dresT.shape; KV=dk.shape[1]
    A=pl.BlockSpec(memory_space=ANY)
    ib=lambda rows:pl.BlockSpec((1,rows,C),lambda s,p,q:(s,0,0))
    gs=pltpu.PrefetchScalarGridSpec(num_scalar_prefetch=2,grid=(S,),
        in_specs=[full((D,KV)),full((D,T)),full((KV,D)),ib(T),ib(T),ib(KV),ib(KV)]+[A]*len(wps),
        out_specs=[full((T,D)),full((KV-T,D)),full((1,D)),A,A],
        scratch_shapes=[pltpu.VMEM((2,3,D,C),BF),pltpu.VMEM((2,4,D,C),BF),pltpu.VMEM((KV,D),F32),pltpu.SemaphoreType.DMA((2,)),pltpu.SemaphoreType.DMA((2,))])
    sd=jax.ShapeDtypeStruct
    piece=sd((R//2,S,4,SLAB,C),BF)
    return pl.pallas_call(functools.partial(grad_attn_kernel,T=T,KV=KV,C=C,R=R,metas=metas,S=S,SLAB=SLAB),grid_spec=gs,
        out_shape=[sd((T,D),F32),sd((KV-T,D),BF),sd((1,D),F32),piece,piece],
        cost_estimate=pl.CostEstimate(flops=1,transcendentals=0,bytes_accessed=1),name="attn_grad")(perm2,slots,a1T,dresT,xhat,o,dq,dk,dv,*wps)

def split3(x):
    hi=x.astype(BF)
    return hi,(x-hi.astype(F32)).astype(BF)

def dot3(a,b,ca,cb):
    ah,al=a; bh,bl=b
    return dot(ah,bh,ca,cb)+(dot(ah,bl,ca,cb)+dot(al,bh,ca,cb))

def soap_kernel(sc, g_in, first, second, left, right, *rest, turned):
    f_out, s_out, u_out, n_out = rest[-4:]
    step,b1,b2=sc[0],sc[1],sc[2]
    ql=split3(left[0]); qr=split3(right[0])
    if turned:
        x=dot3(split3(g_in[0]),ql,1,0)
        r=dot3(split3(x),qr,0,0).T
    else:
        x=dot3(ql,split3(g_in[0]),0,0)
        r=dot3(split3(x),qr,1,0)
    fn=b1*first[0]+(1.0-b1)*r
    sn=b2*second[0]+(1.0-b2)*r*r
    f_out[0]=fn; s_out[0]=sn
    n=fn/(jnp.sqrt(sn)+ADAM_EPS)
    if turned:
        t=dot3(split3(dot3(qr,split3(n),1,0)),ql,1,1)
    else:
        t=dot3(split3(dot3(ql,split3(n),1,0)),qr,1,1)
    size=n.shape[0]*n.shape[1]
    fac=jnp.sqrt(jnp.sum(n*n,keepdims=True)*(1.0/size))*lax.rsqrt(jnp.sum(t*t,keepdims=True)*(1.0/size)+SCALE_EPS)
    u_out[0]=(-step*fac)*t
    n_out[0]=jnp.broadcast_to(fac,(8,128))

def soap(scalars,g,first,second,left,right,turned,K0=0,N=None,carry=()):
    K=first.shape[0]
    N=K if N is None else N
    b=lambda x:pl.BlockSpec((1,)+x.shape[1:],lambda k,s:(k+K0,0,0))
    sd=jax.ShapeDtypeStruct
    o=sd(first.shape,F32)
    outs=[o,o,o,sd((K,8,128),F32)]
    gs=pltpu.PrefetchScalarGridSpec(num_scalar_prefetch=1,grid=(N,),
        in_specs=[b(x) for x in (g,first,second,left,right)]+[pl.BlockSpec(memory_space=ANY)]*len(carry),out_specs=[b(x) for x in outs])
    return pl.pallas_call(functools.partial(soap_kernel,turned=turned),grid_spec=gs,out_shape=outs,
        input_output_aliases={6+i:i for i in range(len(carry))},
        cost_estimate=pl.CostEstimate(flops=1,transcendentals=0,bytes_accessed=1),
        name="soap_"+("mlp" if turned else "attn"))(scalars,g,first,second,left,right,*carry)

def norm_kernel(own, far, gain, a1, a1T, xh, *, T):
    for lo,ref in ((0,own),(T,far)):
        v=ref[...].astype(F32)
        ce=v-jnp.mean(v,axis=1,keepdims=True)
        x=ce*lax.rsqrt(jnp.mean(ce*ce,axis=1,keepdims=True)+NORM_EPS)
        n=ref.shape[0]
        xh[lo:lo+n,:]=x.astype(BF)
        y=x*gain[...]
        a1[lo:lo+n,:]=y.astype(BF)
        a1T[:,lo:lo+n]=y.T.astype(BF)

def norm_first(own,far,gain):
    T,D=own.shape; KV=T+far.shape[0]
    sd=jax.ShapeDtypeStruct
    outs=[sd((KV,D),BF),sd((D,KV),BF),sd((KV,D),BF)]
    return pl.pallas_call(functools.partial(norm_kernel,T=T),grid=(1,),in_specs=[full(x.shape) for x in (own,far,gain)],
        out_specs=[full(o.shape) for o in outs],out_shape=outs,
        cost_estimate=pl.CostEstimate(flops=1,transcendentals=0,bytes_accessed=1),name="norm_first")(own,far,gain)

def input_kernel(hid, da, dres, gain, *rest):
    out=rest[-1]
    v=hid[...].astype(F32)
    ce=v-jnp.mean(v,axis=1,keepdims=True)
    rstd=lax.rsqrt(jnp.mean(ce*ce,axis=1,keepdims=True)+NORM_EPS)
    x=ce*rstd
    d=da[...]
    for r in rest[:-1]:
        d=d+r[...].astype(F32)
    e=d*gain[...]
    out[...]=(dres[...]+rstd*(e-jnp.mean(e,axis=1,keepdims=True)-x*jnp.mean(e*x,axis=1,keepdims=True))).astype(BF)

def input_back(hid,da,dres,gain,*back):
    args=(hid,da,dres,gain)+back
    return pl.pallas_call(input_kernel,grid=(1,),in_specs=[full(x.shape) for x in args],out_specs=full(hid.shape),
        out_shape=jax.ShapeDtypeStruct(hid.shape,BF),
        cost_estimate=pl.CostEstimate(flops=1,transcendentals=0,bytes_accessed=1),name="input_back")(*args)


def ring_order(count):
    return list(range(0, count, 2)) + list(range(1, count, 2))[::-1]


def swap_dp(value, bit, owners):
    return lax.ppermute(value, "dp", [(i, i ^ bit) for i in range(owners)])


def to_ring_pred(value, shards):
    ring = ring_order(shards)
    return lax.ppermute(
        value, "tensor", [(ring[p], ring[(p - 1) % shards]) for p in range(shards)]
    )


def to_ring_succ(value, shards):
    ring = ring_order(shards)
    return lax.ppermute(
        value, "tensor", [(ring[p], ring[(p + 1) % shards]) for p in range(shards)]
    )


def along_line(value, steps, shards):
    ring = ring_order(shards)
    return lax.ppermute(
        value, "tensor", [(ring[p], ring[(p + steps) % shards]) for p in range(shards)]
    )


def add_low(one, two):
    return (one.astype(F32) + two.astype(F32)).astype(BF)


def halve(pieces, bits, owners):
    for bit in bits:
        live = sorted(bits[bits.index(bit):], reverse=True)
        axis = live.index(bit)
        send = lax.index_in_dim(pieces, 1, axis, keepdims=False)
        keep = lax.index_in_dim(pieces, 0, axis, keepdims=False)
        pieces = add_low(keep, swap_dp(send, bit, owners))
    return pieces


def reduce_pieces(even, odd, cut, owners, shards):
    mine = add_low(even, swap_dp(odd, 1, owners))
    bits = [1 << b for b in range(1, owners.bit_length() - 1)]
    mine = mine.reshape((2,) * len(bits) + mine.shape[1:])
    low = halve(mine[..., :cut, :], bits[::-1], owners)
    high = halve(mine[..., cut:, :], bits, owners)
    both = jnp.concatenate([low, high], axis=-2)
    moving = both[shards - 1]
    for left in range(shards - 2, -1, -1):
        moving = to_ring_pred(moving, shards)
        moving = moving.astype(F32) + both[left].astype(F32)
        if left:
            moving = moving.astype(BF)
    return moving


def all_sum(value, owners, shards):
    for axis, count in (("dp", owners), ("tensor", shards)):
        step = 1
        while step < count:
            value = value + lax.ppermute(value, axis, [(i, i ^ step) for i in range(count)])
            step *= 2
    return value


def after(value, *earlier):
    return lax.optimization_barrier((value,) + earlier)[0]


def add_all(*values):
    total = values[0].astype(F32)
    for value in values[1:]:
        total = total + value.astype(F32)
    return total


def gather_stack(stacked, owners):
    half = stacked.shape[0] // 2
    by_x, by_y = swap_dp(stacked, 2, owners), swap_dp(stacked, 4, owners)
    return by_x, by_y, swap_dp(by_x[:half], 4, owners), swap_dp(by_y[half:], 2, owners)


def to_core(arrays, owners):
    return [swap_dp(a, 1, owners) for a in arrays]


def with_partner(arrays, metas, owners):
    return arrays + [swap_dp(a, 1, owners) for a in arrays], metas + tuple((m[0] + 1,) + m[1:] for m in metas)


def cross_sends(even, core, half):
    low = add_all(even[3, :half], core[3, :half]).astype(BF)
    high = add_all(even[3, half:], core[3, half:]).astype(BF)
    return low, high


def side_sends(even, core, from_y, from_x, half):
    to_x = jnp.concatenate(
        [add_all(even[1, :half], core[1, :half], from_y), add_all(even[1, half:], core[1, half:])]
    ).astype(BF)
    to_y = jnp.concatenate(
        [add_all(even[2, :half], core[2, :half]), add_all(even[2, half:], core[2, half:], from_x)]
    ).astype(BF)
    return to_x, to_y


def own_part(even, core, from_x, from_y, slot):
    return add_all(even[0, slot], core[0, slot], from_x[slot], from_y[slot])


def ring_sum(even, core, from_x, from_y, shards):
    moving = None
    for slot in list(range(1, shards)) + [0]:
        part = own_part(even, core, from_x, from_y, slot)
        if moving is not None:
            part = part + to_ring_succ(moving, shards).astype(F32)
        moving = part.astype(BF)
    return part


def per_device(
    hidden_in, out_grad, attn_weight, mlp_weight, norm_gain,
    attn_first, attn_second, attn_left, attn_right,
    mlp_first, mlp_second, mlp_left, mlp_right,
    gain_first, gain_second, owner_rows, segment_ids, positions, valid,
    step, learn_rate, beta_first, beta_second,
):
    owners = lax.axis_size("dp")
    shards = lax.axis_size("tensor")
    dp_index = lax.axis_index("dp")
    place = lax.axis_index("tensor")
    rows, width = hidden_in.shape
    slab = attn_weight.shape[1]
    hid_cols = mlp_weight.shape[2]
    span = SEQ_LEN // rows
    within = place % span
    base = place - within
    half = shards // 2
    gain_rows = norm_gain.astype(F32)

    def from_peer(value, ahead):
        pairs = [(g + (w + ahead) % span, g + w) for g in range(0, shards, span) for w in range(span)]
        return lax.ppermute(value, "tensor", pairs)

    def sequence_rows(column):
        return jnp.concatenate(
            [lax.dynamic_slice_in_dim(column, (base + (within + d) % span) * rows, rows, 0) for d in range(span)]
        )

    joined = 128 // slab if slab < 128 else 1
    fast = owners == 8 and joined == 1 and shards == 4 and span == 2
    both = ("dp", "tensor")
    mlp_turned = jnp.swapaxes(mlp_weight, 1, 2)
    if not fast:
        attn_all = lax.all_gather(attn_weight, both, axis=0, tiled=False).reshape((owners, shards) + attn_weight.shape)
        mlp_all = lax.all_gather(mlp_turned, both, axis=0, tiled=False).reshape((owners, shards) + mlp_turned.shape)

    slot_ids = jnp.arange(owners, dtype=jnp.int32)
    rel_owner = jnp.sum(
        jnp.where((slot_ids[:, None] ^ dp_index) == slot_ids[None, :], owner_rows[None, :], 0), axis=1
    )
    ring = ring_order(shards)
    ring_place = jnp.array([ring.index(z) for z in range(shards)], jnp.int32)
    my_place = jnp.sum(jnp.where(jnp.arange(shards) == place, ring_place, 0))
    slots = (my_place - ring_place) % shards
    attn_perm = jnp.concatenate([rel_owner if fast else owner_rows, rel_owner]).astype(jnp.int32)
    if fast:
        slots = jnp.arange(shards, dtype=jnp.int32)
    if joined == 1:
        mlp_perm = attn_perm
    else:
        inverse = jnp.sum(jnp.where(owner_rows[None, :] == slot_ids[:, None], slot_ids[None, :], 0), axis=1)
        mlp_all = jnp.take(mlp_all, inverse, axis=0).reshape((owners // joined, joined) + mlp_all.shape[1:])
        mlp_all = jnp.moveaxis(mlp_all, 1, 4)
        mlp_all = mlp_all.reshape(mlp_all.shape[:4] + (joined * slab,))
        blocks = jnp.arange(owners // joined, dtype=jnp.int32)
        mlp_perm = jnp.concatenate([blocks, blocks])

    seg = sequence_rows(segment_ids)
    keep_seq = sequence_rows(valid)
    pos = sequence_rows(positions)
    half_dim = HEAD_DIM // 2
    frequency = jnp.exp(jnp.arange(half_dim, dtype=F32) * (-2.0 * math.log(ROPE_BASE) / HEAD_DIM))
    angles = pos.astype(F32)[:, None] * frequency[None, :]
    cos_half, sin_half = jnp.cos(angles), jnp.sin(angles)
    cos_table = jnp.concatenate([cos_half] * 4, axis=1)
    sin_table = jnp.concatenate([-sin_half, sin_half] * 2, axis=1)
    key_seg = jnp.where(keep_seq > 0, seg, -1)[:, None]
    query_seg = seg[None, :rows]
    keep_own = keep_seq[:rows].astype(F32)[:, None]

    first_gain, second_gain = gain_rows[0:1], gain_rows[1:2]
    if fast:
        together = lax.optimization_barrier
        mlp_x, mlp_y, mlp_z = [None] * 4, [None] * 4, [None] * 4
        line_1 = along_line(attn_weight, 1, shards)
        mlp_x[0], mlp_y[0] = swap_dp(mlp_turned, 2, owners), swap_dp(mlp_turned, 4, owners)
        tables = (cos_table, sin_table, key_seg, query_seg, keep_own, attn_perm, mlp_perm, slots, first_gain, second_gain)
        line_1, mlp_x[0], mlp_y[0] = together((line_1, mlp_x[0], mlp_y[0]))
        pair_a = jnp.stack([attn_weight, line_1])
        x_a, y_a = swap_dp(pair_a, 2, owners), swap_dp(pair_a, 4, owners)
        far_rows = from_peer(after(hidden_in, line_1), 1)
        core_0 = to_core([after(a, line_1) for a in (mlp_turned, mlp_x[0])], owners)
        x_a, y_a, core_0, tables = together((x_a, y_a, core_0, tables))
        cos_table, sin_table, key_seg, query_seg, keep_own, attn_perm, mlp_perm, slots, first_gain, second_gain = tables
        z_a, mlp_z[0] = swap_dp(x_a, 4, owners), swap_dp(after(mlp_y[0], y_a), 2, owners)
        line_2, line_3 = along_line(after(line_1, x_a), 1, shards), along_line(after(attn_weight, x_a), 3, shards)
        normal = norm_first(hidden_in, far_rows, first_gain)
        z_a, mlp_z[0], normal, line_2, line_3 = together((z_a, mlp_z[0], tuple(normal), line_2, line_3))
        pair_b = jnp.stack([line_2, line_3])
        x_b, y_b = swap_dp(pair_b, 2, owners), swap_dp(pair_b, 4, owners)
        mlp_line = [mlp_turned, along_line(after(mlp_turned, line_3), 1, shards), None, None]
        core_a4 = to_core([after(a, z_a) for a in (pair_a, x_a, y_a, z_a)], owners)
        core_b = [swap_dp(after(pair_b, core_a4[1]), 1, owners)]
        normal, core_a4, mlp_line[1], core_b, x_b, y_b = together((tuple(normal), core_a4, mlp_line[1], core_b, x_b, y_b))
        z_b = swap_dp(y_b, 2, owners)
        mlp_x[1], mlp_y[1] = swap_dp(mlp_line[1], 2, owners), swap_dp(mlp_line[1], 4, owners)
        mlp_line[3] = along_line(after(mlp_turned, mlp_line[1]), 3, shards)
        mlp_line[2] = along_line(mlp_line[1], 1, shards)
        first_norm, first_turned, xhat_low = normal

        def attn_set(arrays, first):
            return arrays, tuple((r, first, 2, shards) for r in (0, 2, 4, 6, 1, 3, 5, 7))

        sizes = (shards, slab, attn_weight.shape[2])
        arrays_a, metas_a = attn_set([pair_a, x_a, y_a, z_a, *core_a4], 0)
        attn_part_a = (arrays_a, metas_a, *sizes)
    else:
        far_rows = [from_peer(hidden_in, d) for d in range(1, span)]
        attn_pieces = ([attn_all], (None,), shards, slab, attn_weight.shape[2])
        first_norm, first_turned, xhat_low = norm_first(hidden_in, jnp.concatenate(far_rows), first_gain)
    back_args = (cos_table, sin_table, key_seg, query_seg)
    fwd_args = (attn_perm, first_norm, hidden_in, second_gain, cos_table, sin_table, key_seg, query_seg, keep_own)
    if fast:
        carry = fwd_attn(*fwd_args, attn_part_a, S0=0, N=half)
        z_b, mlp_x[1], mlp_y[1], mlp_line[3], mlp_line[2], carry = together(
            (z_b, mlp_x[1], mlp_y[1], mlp_line[3], mlp_line[2], tuple(carry))
        )
        core_b = core_b + to_core([after(x_b, z_b), after(y_b, z_b)], owners)
        core_z_b = swap_dp(z_b, 1, owners)
        core_b, core_z_b, mlp_x[1], mlp_y[1], mlp_line[3], mlp_line[2] = together((core_b, core_z_b, mlp_x[1], mlp_y[1], mlp_line[3], mlp_line[2]))
        mlp_z[1] = swap_dp(mlp_y[1], 2, owners)
        mlp_y[2] = swap_dp(mlp_line[2], 4, owners)
        arrays_b, metas_b = attn_set([pair_b, x_b, y_b, z_b, *core_b, core_z_b], 2)
        attn_part_b = (arrays_b, metas_b, *sizes)
        attn_pieces = (arrays_a + arrays_b, metas_a + metas_b, *sizes)
        mlp_x[3], mlp_y[3] = swap_dp(mlp_line[3], 2, owners), swap_dp(mlp_line[3], 4, owners)
        out = fwd_attn(*fwd_args, attn_part_b, S0=half, N=half, carry=carry)
        mlp_x[3], mlp_y[3], mlp_z[1], mlp_y[2], out = together((mlp_x[3], mlp_y[3], mlp_z[1], mlp_y[2], tuple(out)))
        queries, keys, values, attended, log_sums, resid, second_norm, stat_a = out

        def mlp_set(slot):
            return [mlp_line[slot], mlp_x[slot], mlp_y[slot], mlp_z[slot]]

        def mlp_pieces(*slots_of):
            arrays, metas = [], []
            for slot, got in slots_of:
                arrays += [a[None] for a in got]
                metas += [(r, slot, 1, shards) for r in (0, 2, 4, 6, 1, 3, 5, 7)]
            return arrays, tuple(metas), shards, slab, hid_cols

        set_0, set_1 = mlp_set(0), mlp_set(1)
        core_1 = to_core([after(a, mlp_z[1]) for a in set_1], owners)
        core_0 = core_0 + to_core([after(a, core_1[1]) for a in (mlp_y[0], mlp_z[0])], owners)
        core_1, core_0, second_norm, mlp_x[3], mlp_y[2] = together((core_1, core_0, second_norm, mlp_x[3], mlp_y[2]))
        mlp_z[3], mlp_z[2] = swap_dp(mlp_x[3], 4, owners), swap_dp(mlp_y[2], 2, owners)
        mlp_x[2] = swap_dp(after(mlp_line[2], second_norm), 2, owners)
        core_3 = to_core([mlp_line[3], mlp_x[3]], owners)
        mlp_args = (mlp_perm, slots, second_norm, out_grad, resid, second_gain, keep_own)
        out = mlp(*mlp_args, mlp_pieces((0, set_0 + core_0), (1, set_1 + core_1)), S0=0, N=half)
        mlp_x[2], mlp_z[2], mlp_z[3], core_3, out = together((mlp_x[2], mlp_z[2], mlp_z[3], core_3, tuple(out)))
        *carry, even_a, odd_a = out
        set_2, set_3 = mlp_set(2), mlp_set(3)
        core_2 = to_core([after(a, odd_a) for a in set_2], owners)
        core_3 = core_3 + to_core([after(a, odd_a) for a in set_3[2:]], owners)
        core_a = swap_dp(odd_a, 1, owners)
        low, high = cross_sends(even_a, core_a, 1)
        low, high, core_2, core_3, carry = lax.optimization_barrier((low, high, core_2, core_3, carry))
        from_y, from_x = swap_dp(low, 4, owners), swap_dp(high, 2, owners)
        out = mlp(*mlp_args, mlp_pieces((2, set_2 + core_2), (3, set_3 + core_3)), S0=half, N=half, carry=carry)
        from_y, from_x, *out = lax.optimization_barrier((from_y, from_x, *out))
        output, dresid, dres_low, dres_turned, gain_two, stat_m, even_b, odd_b = out
        core_b2 = swap_dp(odd_b, 1, owners)
        to_x, to_y = side_sends(even_a, core_a, from_y, from_x, 1)
        to_x, to_y, dres_low = lax.optimization_barrier((to_x, to_y, dres_low))
        back_x, back_y = swap_dp(to_x, 2, owners), swap_dp(to_y, 4, owners)
        fwd_kept = (queries, keys, values, log_sums, attn_pieces)
        grads = bwd_attn(attn_perm, dres_low, *back_args, *fwd_kept, S0=0, N=half)
        back_x, back_y, core_b2, *grads = lax.optimization_barrier((back_x, back_y, core_b2, *grads))
        low, high = cross_sends(even_b, core_b2, 1)
        ring_1 = own_part(even_a, core_a, back_x, back_y, 1).astype(BF)
        low, high, ring_1, dres_low = lax.optimization_barrier((low, high, ring_1, dres_low))
        from_y, from_x = swap_dp(low, 4, owners), swap_dp(high, 2, owners)
        ring_1 = to_ring_succ(ring_1, shards)
        grads = bwd_attn(attn_perm, dres_low, *back_args, *fwd_kept, S0=half, N=half, carry=tuple(grads))
        from_y, from_x, ring_1, *grads = lax.optimization_barrier((from_y, from_x, ring_1, *grads))
        to_x, to_y = side_sends(even_b, core_b2, from_y, from_x, 1)
        to_x, to_y, dres_turned = lax.optimization_barrier((to_x, to_y, dres_turned))
        from_x, from_y = swap_dp(to_x, 2, owners), swap_dp(to_y, 4, owners)
        out = grad_attn(attn_perm, slots, first_turned, dres_turned, xhat_low, attended, *grads, attn_pieces)
        from_x, from_y, *out = lax.optimization_barrier((from_x, from_y, *out))
        da_own, da_far, gain_one, attn_even, attn_odd = out
    else:
        queries, keys, values, attended, log_sums, resid, second_norm, stat_a = fwd_attn(*fwd_args, attn_pieces)
        output, dresid, dres_low, dres_turned, gain_two, stat_m, mlp_even, mlp_odd = mlp(
            mlp_perm, slots, second_norm, out_grad, resid, second_gain, keep_own,
            ([mlp_all], (None,), shards, mlp_all.shape[-1], hid_cols),
        )
        if joined > 1:
            merged = jnp.stack([mlp_even, mlp_odd], axis=1).reshape((owners // joined,) + mlp_even.shape[1:])
            merged = merged.reshape(merged.shape[:-1] + (joined, slab))
            merged = jnp.moveaxis(merged, -2, 1).reshape((owners,) + mlp_even.shape[1:-1] + (slab,))
            merged = jnp.take(merged, rel_owner, axis=0)
            mlp_even, mlp_odd = merged[0::2], merged[1::2]
        mlp_sum = reduce_pieces(mlp_even, mlp_odd, -(-hid_cols // 32) * 16, owners, shards)
        grads = bwd_attn(attn_perm, dres_low, *back_args, queries, keys, values, log_sums, attn_pieces)
        da_own, da_far, gain_one, attn_even, attn_odd = grad_attn(
            attn_perm, slots, first_turned, dres_turned, xhat_low, attended, *grads, attn_pieces
        )
    def send_back(da_far):
        got = []
        for d in range(1, span):
            pairs = [(g + w, g + (w + d) % span) for g in range(0, shards, span) for w in range(span)]
            got.append(lax.ppermute(da_far[(d - 1) * rows : d * rows], "tensor", pairs))
        return got

    def swap_line(value, bit):
        return lax.ppermute(value, "tensor", [(i, i ^ bit) for i in range(shards)])

    def finish_input(da_back):
        return input_back(hidden_in, da_own, dresid, first_gain, *da_back)

    step_count = step.astype(F32)
    step_size = (
        learn_rate
        * jnp.sqrt(1.0 - jnp.power(beta_second, step_count))
        / (1.0 - jnp.power(beta_first, step_count))
    )
    scalars = jnp.stack([step_size, beta_first, beta_second])

    def flip(value):
        return jnp.swapaxes(value, 1, 2)

    def soap_mlp(total, *part):
        return soap(scalars, total, flip(mlp_first), flip(mlp_second), mlp_left, mlp_right, True, *part)

    sums = jnp.concatenate([jnp.sum(stat_a, axis=1), jnp.sum(stat_m, axis=1), jnp.sum(keep_own)[None]])
    small = jnp.concatenate([gain_one, gain_two, jnp.pad(sums, (0, width - 5))[None]], axis=0)
    if fast:
        attn_core = swap_dp(attn_odd, 1, owners)
        ring_2 = (own_part(even_b, core_b2, from_x, from_y, 0) + ring_1.astype(F32)).astype(BF)
        ring_2 = to_ring_succ(ring_2, shards)
        small = small + swap_dp(small, 1, owners)
        small, attn_core = lax.optimization_barrier((small, attn_core))
        low, high = cross_sends(attn_even, attn_core, half)
        low, high, small = lax.optimization_barrier((low, high, small))
        cross_y, cross_x = swap_dp(low, 4, owners), swap_dp(high, 2, owners)
        small = small + swap_dp(small, 2, owners)
        ring_3 = (own_part(even_b, core_b2, from_x, from_y, 1) + ring_2.astype(F32)).astype(BF)
        ring_3 = to_ring_succ(ring_3, shards)
        small, cross_x, cross_y = lax.optimization_barrier((small, cross_x, cross_y))
        to_x, to_y = side_sends(attn_even, attn_core, cross_y, cross_x, half)
        to_x, to_y, small, ring_3 = lax.optimization_barrier((to_x, to_y, small, ring_3))
        attn_x, attn_y = swap_dp(to_x, 2, owners), swap_dp(to_y, 4, owners)
        small = small + swap_dp(small, 4, owners)
        da_back = send_back(after(da_far, ring_3))
        mlp_sum = own_part(even_a, core_a, back_x, back_y, 0) + ring_3.astype(F32)
        mlp_new = soap_mlp(mlp_sum)
        attn_x, attn_y, mlp_sum, mlp_new = lax.optimization_barrier((attn_x, attn_y, mlp_sum, tuple(mlp_new)))
        moving = own_part(attn_even, attn_core, attn_x, attn_y, 1).astype(BF)
        for slot in range(1, shards):
            moving, small, da_back = lax.optimization_barrier((moving, small, da_back))
            moving = to_ring_succ(moving, shards)
            if slot < 3:
                small = small + swap_line(small, slot)
            if slot == 1:
                input_grad = finish_input(da_back)
                moving, input_grad = lax.optimization_barrier((moving, input_grad))
            moving, small = lax.optimization_barrier((moving, small))
            moving = moving.astype(F32) + own_part(attn_even, attn_core, attn_x, attn_y, (slot + 1) % shards)
            if slot + 1 < shards:
                moving = moving.astype(BF)
        attn_sum = moving
    else:
        attn_sum = reduce_pieces(attn_even, attn_odd, slab // 2, owners, shards)
        small = all_sum(small, owners, shards)
        mlp_new = soap_mlp(mlp_sum)
        input_grad = finish_input(send_back(da_far))
    gain_grad = small[:2]
    stat_sums = small[2]

    attn_grad = attn_sum
    attn_first_new, attn_second_new, attn_update, attn_scale = soap(
        scalars, attn_sum, attn_first, attn_second, attn_left, attn_right, False
    )
    mlp_grad, mlp_first_new, mlp_second_new, mlp_update = (flip(v) for v in (mlp_sum, *mlp_new[:3]))
    mlp_scale = mlp_new[3]
    gain_first_new = beta_first * gain_first + (1.0 - beta_first) * gain_grad
    gain_second_new = beta_second * gain_second + (1.0 - beta_second) * gain_grad * gain_grad
    gain_update = -step_size * gain_first_new / (jnp.sqrt(gain_second_new) + ADAM_EPS)
    root_means = jnp.sqrt(stat_sums[:4] / (stat_sums[4] * width))
    norm_scale = jnp.concatenate([attn_scale[:, :1, :1], mlp_scale[:, :1, :1]], axis=0)
    return (
        output, input_grad, attn_grad, mlp_grad, gain_grad,
        attn_first_new, attn_second_new, mlp_first_new, mlp_second_new,
        gain_first_new, gain_second_new, attn_update, mlp_update, gain_update,
        norm_scale, root_means,
    )


def solution(mesh):
    rows = P(("dp", "tensor"), None)
    block = P(None, "dp", "tensor")
    return jax.shard_map(
        per_device,
        mesh=mesh,
        in_specs=(rows, rows, block, block, P()) + (block,) * 8 + (P(),) * 3 + (P("dp"),) * 3 + (P(),) * 4,
        out_specs=(rows, rows, block, block, P(), block, block, block, block, P(), P(), block, block, P(), block, P()),
        check_vma=False,
    )
```

```python
import functools
import math

import jax
import jax.numpy as jnp
from jax import lax
from jax.experimental import pallas as pl
from jax.experimental.pallas import tpu as pltpu
from jax.sharding import PartitionSpec as P

HEAD_DIM = 64
SEQ_LEN = 1024
NORM_EPS = 1e-05
ROPE_BASE = 160000.0
ADAM_EPS = 1e-08
SCALE_EPS = 1e-06
PRECISE = lax.Precision.HIGHEST
BF = jnp.bfloat16
F32 = jnp.float32
ANY = pl.ANY


def dot(a,b,ca,cb):
    return lax.dot_general(a,b,(((ca,),(cb,)),((),())),preferred_element_type=F32)

def turn(x, cos, sin, lower):
    w=x.shape[1]
    sw=jnp.where(lower, pltpu.roll(x, w-32, 1), pltpu.roll(x, 32, 1))
    return x*cos+sw*sin

def lower_lanes(rows, cols):
    return lax.broadcasted_iota(jnp.int32,(rows,cols),1)%64<32

def wide(t, n):
    return t if n==1 else jnp.concatenate([t]*n,axis=1)

def fetch_pieces(refs, metas, perm, step, copy):
    for ref, meta in zip(refs, metas):
        if meta is None:
            for r in range(ref.shape[0]):
                copy(ref.at[r, step], perm[r])
        else:
            r, first, count, total = meta
            if count == total:
                copy(ref.at[step], perm[r])
            else:
                @pl.when((step >= first) & (step < first + count))
                def _(ref=ref, r=r, first=first):
                    copy(ref.at[jnp.clip(step - first, 0, ref.shape[0] - 1)], perm[r])

def fwd_attn_kernel(perm, a1, hid, gain, cos, sin, kseg, qseg, keep, *rest, T, KV, C, metas, S, SLAB, QB, S0, N):
    wps = rest[:len(metas)]
    rest = rest[len(metas):]
    if S0:
        acc_in, rest = rest[0], rest[6:]
    q_out, k_out, v_out, o_out, lse_out = rest[:5]
    if S0+N==S:
        resid_out, a2_out, stat_out, acc = rest[5:9]
    else:
        acc = rest[5]
    W, bias, osc, sem = rest[-4:]
    s=pl.program_id(0)
    def fetch(step, slot):
        fetch_pieces(wps, metas, perm, S0+step, lambda src, blk: pltpu.make_async_copy(src, W.at[slot, :, pl.ds(pl.multiple_of(blk*SLAB,SLAB),SLAB), :], sem.at[slot]).start())
    slot=lax.rem(s,2)
    @pl.when(s==0)
    def _():
        fetch(0,0)
        row=lax.broadcasted_iota(jnp.int32,(KV,T),0); col=lax.broadcasted_iota(jnp.int32,(KV,T),1)
        ok=(kseg[...]==qseg[...])|(row==col)
        bias[...]=jnp.where(ok,0.0,-1e30)
        acc[...]=acc_in[...] if S0 else jnp.zeros_like(acc)
    @pl.when(s+1<N)
    def _(): fetch(s+1,1-slot)
    pltpu.make_async_copy(W.at[slot],W.at[slot],sem.at[slot]).wait()
    n=C//128
    low_q=lower_lanes(T,C); low_k=lower_lanes(KV,C)
    cw=wide(cos[...],n); sw=wide(sin[...],n)
    q=dot(a1[:T,:],W[slot,0],1,0)
    q_out[0]=(turn(q,cw[:T],sw[:T],low_q).astype(BF)*BF(1/math.sqrt(HEAD_DIM))).astype(BF)
    k=dot(a1[...],W[slot,1],1,0)
    k_out[0]=turn(k,cw,sw,low_k).astype(BF)
    v_out[0]=dot(a1[...],W[slot,2],1,0).astype(BF)
    for p in range(n):
        kp=k_out[0,:,p*128:(p+1)*128]; vp=v_out[0,:,p*128:(p+1)*128]
        for b in range(T//QB):
            qp=q_out[0,b*QB:(b+1)*QB,p*128:(p+1)*128]
            half=lax.broadcasted_iota(jnp.int32,qp.shape,1)<64
            parts=[]
            for h in range(2):
                qm=jnp.where(half if h==0 else ~half,qp,jnp.zeros_like(qp))
                st=dot(kp,qm,1,1)+bias[:,b*QB:(b+1)*QB]
                m=jnp.max(st,axis=0,keepdims=True)
                e=jnp.exp(st-m)
                l=jnp.sum(e,axis=0,keepdims=True)
                ot=dot(vp,e.astype(BF),0,0)
                parts.append(ot[h*64:(h+1)*64]*(1.0/l))
                lse_out[0,pl.ds(2*p+h,1),b*QB:(b+1)*QB]=m+jnp.log(l)
            op=jnp.concatenate(parts,axis=0)
            osc[b*QB:(b+1)*QB,p*128:(p+1)*128]=op.T.astype(BF)
    o_out[0]=osc[...]
    acc[...]+=dot(osc[...],W[slot,3],1,1)
    if S0+N<S:
        return
    @pl.when(s==N-1)
    def _():
        at=acc[...]
        rs=hid[...].astype(F32)+at
        resid_out[...]=rs
        mu=jnp.mean(rs,axis=1,keepdims=True); ce=rs-mu
        var=jnp.mean(ce*ce,axis=1,keepdims=True)
        a2_out[...]=(ce*lax.rsqrt(var+NORM_EPS)*gain[...]).astype(BF)
        kp=keep[...]
        s1=jnp.sum(kp*at*at,axis=0,keepdims=True); s2=jnp.sum(kp*rs*rs,axis=0,keepdims=True)
        stat_out[...]=jnp.concatenate([s1,s2],axis=0)

def full(shape):
    nd=len(shape)
    return pl.BlockSpec(shape,lambda *a:(0,)*nd)

def fwd_attn(perm,a1,hid,gain,cos,sin,kseg,qseg,keep,pieces,S0=0,N=None,carry=(),QB=512):
    wps,metas,S,SLAB,C=pieces
    N=S if N is None else N
    KV,D=a1.shape; T=hid.shape[0]; HG=C//HEAD_DIM
    A=pl.BlockSpec(memory_space=ANY)
    sb=lambda rows:pl.BlockSpec((1,rows,C),lambda s,p:(s+S0,0,0))
    sd=jax.ShapeDtypeStruct
    last=S0+N==S
    tail=[sd((T,D),F32),sd((T,D),BF),sd((2,D),F32)] if last else [sd((T,D),F32)]
    gs=pltpu.PrefetchScalarGridSpec(num_scalar_prefetch=1,grid=(N,),
        in_specs=[full((KV,D)),full((T,D)),full((1,D)),full((KV,128)),full((KV,128)),full((KV,1)),full((1,T)),full((T,1))]+[A]*len(wps)+([full((T,D))]+[A]*5 if S0 else []),
        out_specs=[sb(T),sb(KV),sb(KV),sb(T),pl.BlockSpec((1,HG,T),lambda s,p:(s+S0,0,0))]+[full(t.shape) for t in tail],
        scratch_shapes=([pltpu.VMEM((T,D),F32)] if last else [])+[pltpu.VMEM((2,4,D,C),BF),pltpu.VMEM((KV,T),F32),pltpu.VMEM((T,C),BF),pltpu.SemaphoreType.DMA((2,))])
    return pl.pallas_call(functools.partial(fwd_attn_kernel,T=T,KV=KV,C=C,metas=metas,S=S,SLAB=SLAB,QB=min(QB,T),S0=S0,N=N),grid_spec=gs,
        out_shape=[sd((S,T,C),BF),sd((S,KV,C),BF),sd((S,KV,C),BF),sd((S,T,C),BF),sd((S,HG,T),F32)]+tail,
        input_output_aliases={10+len(wps)+i:i for i in range(5)} if S0 else {},
        cost_estimate=pl.CostEstimate(flops=1,transcendentals=0,bytes_accessed=1),name="attn_fwd")(perm,a1,hid,gain,cos,sin,kseg,qseg,keep,*wps,*((carry[5],)+tuple(carry[:5]) if S0 else ()))

def gelu_parts(x):
    phi=0.5*(1.0+lax.erf(x*(1.0/math.sqrt(2.0))))
    den=jnp.exp(-0.5*x*x)*(1.0/math.sqrt(2.0*math.pi))
    return phi,den

def mlp_kernel(perm, slots, a2, g, resid, gain, keep, *rest, T, D, HC, R, metas, S, SLAB, TB, S0, N):
    wps = rest[:len(metas)]
    rest = rest[len(metas):]
    if S0:
        y_in, da_in = rest[:2]
        rest = rest[2:]
    if S0+N==S:
        out, dres_out, dresb_out, dresT_out, gg_out, stat_out = rest[:6]
        rest = rest[6:]
        d0, d1, y, da = rest[:4]
    else:
        y, da, d0, d1 = rest[:4]
    W, stg, hT, dgT, duT, sem, osem = rest[4:]
    s=pl.program_id(0)
    slot=lax.rem(s,2)
    def fetch(step, sl):
        fetch_pieces(wps, metas, perm, S0+step, lambda src, blk: pltpu.make_async_copy(src, W.at[sl, :, :, pl.ds(pl.multiple_of(blk*SLAB,SLAB),SLAB)], sem.at[sl]).start())
    @pl.when(s==0)
    def _(): fetch(0,0)
    @pl.when(s+1<N)
    def _(): fetch(s+1,1-slot)
    pltpu.make_async_copy(W.at[slot],W.at[slot],sem.at[slot]).wait()
    for b in range(T//TB):
        lo,hi=b*TB,(b+1)*TB
        ga=dot(W[slot,0],a2[lo:hi,:],1,1)
        up=dot(W[slot,1],a2[lo:hi,:],1,1)
        dh=dot(W[slot,2],g[lo:hi,:],1,1)
        phi,den=gelu_parts(ga)
        ge=ga*phi
        hT[:,lo:hi]=(ge*up).astype(BF)
        dgT[:,lo:hi]=(dh*up*(phi+ga*den)).astype(BF)
        duT[:,lo:hi]=(dh*ge).astype(BF)
    yc=dot(hT[...],W[slot,2],0,0)
    dc=dot(dgT[...],W[slot,0],0,0)+dot(duT[...],W[slot,1],0,0)
    @pl.when(s==0)
    def _():
        y[...]=yc+y_in[...] if S0 else yc
        da[...]=dc+da_in[...] if S0 else dc
    @pl.when(s>0)
    def _():
        y[...]+=yc; da[...]+=dc
    @pl.when(s>=2)
    def _(): pltpu.make_async_copy(stg.at[slot],stg.at[slot],osem.at[slot]).wait()
    stg[slot,0]=dot(dgT[...],a2[...],1,0).astype(BF)
    stg[slot,1]=dot(duT[...],a2[...],1,0).astype(BF)
    stg[slot,2]=dot(hT[...],g[...],1,0).astype(BF)
    for r in range(R):
        dst=(d0,d1)[r%2]
        pltpu.make_async_copy(stg.at[slot,:,:,pl.ds(pl.multiple_of(perm[R+r]*SLAB,SLAB),SLAB)], dst.at[r//2, slots[S0+s]-S0], osem.at[slot]).start()
    if S0+N==S:
        @pl.when(s==N-1)
        def _():
            br=y[...]; rs=resid[...]; gf=g[...].astype(F32)
            res=rs+br
            out[...]=res.astype(BF)
            kp=keep[...]
            s1=jnp.sum(kp*br*br,axis=0,keepdims=True); s2=jnp.sum(kp*res*res,axis=0,keepdims=True)
            stat_out[...]=jnp.concatenate([s1,s2],axis=0)
            mu=jnp.mean(rs,axis=1,keepdims=True); ce=rs-mu
            rstd=lax.rsqrt(jnp.mean(ce*ce,axis=1,keepdims=True)+NORM_EPS)
            xh=ce*rstd
            d=da[...]
            gg_out[...]=jnp.sum(d*xh,axis=0,keepdims=True)
            e=d*gain[...]
            dr=gf+rstd*(e-jnp.mean(e,axis=1,keepdims=True)-xh*jnp.mean(e*xh,axis=1,keepdims=True))
            dres_out[...]=dr
            db=dr.astype(BF)
            dresb_out[...]=db
            dresT_out[...]=dr.T.astype(BF)
    @pl.when(s==N-1)
    def _():
        for sl in range(min(N,2)):
            pltpu.make_async_copy(stg.at[sl],stg.at[sl],osem.at[sl]).wait()

def mlp(perm2,slots,a2,g,resid,gain,keep,pieces,S0=0,N=None,carry=(),TB=256):
    wps,metas,S,SLAB,HC=pieces
    N=S if N is None else N
    R=perm2.shape[0]//2
    T,D=a2.shape
    A=pl.BlockSpec(memory_space=ANY)
    sd=jax.ShapeDtypeStruct
    last=S0+N==S
    outs=[sd((T,D),BF),sd((T,D),F32),sd((T,D),BF),sd((D,T),BF),sd((1,D),F32),sd((2,D),F32)] if last else [sd((T,D),F32)]*2
    gs=pltpu.PrefetchScalarGridSpec(num_scalar_prefetch=2,grid=(N,),
        in_specs=[full((T,D)),full((T,D)),full((T,D)),full((1,D)),full((T,1))]+[A]*len(wps)+[full((T,D))]*len(carry),
        out_specs=[full(o.shape) for o in outs]+[A,A],
        scratch_shapes=([pltpu.VMEM((T,D),F32)]*2 if last else [])+[pltpu.VMEM((2,3,HC,D),BF),pltpu.VMEM((2,3,HC,D),BF)]+[pltpu.VMEM((HC,T),BF)]*3+[pltpu.SemaphoreType.DMA((2,)),pltpu.SemaphoreType.DMA((2,))])
    piece=sd((R//2,N,3,HC,SLAB),BF)
    return pl.pallas_call(functools.partial(mlp_kernel,T=T,D=D,HC=HC,R=R,metas=metas,S=S,SLAB=SLAB,TB=min(TB,T),S0=S0,N=N),grid_spec=gs,
        out_shape=outs+[piece,piece],
        cost_estimate=pl.CostEstimate(flops=1,transcendentals=0,bytes_accessed=1),name="mlp_both")(perm2,slots,a2,g,resid,gain,keep,*wps,*carry)

def bwd_attn_kernel(perm, dres, cos, sin, kseg, qseg, q_in, k_in, v_in, lse_in, *rest, T, KV, C, metas, S, SLAB, S0, N):
    wps = rest[:len(metas)]
    dq_out, dk_out, dv_out, W, bias, dob, dqs, dks, sem = rest[-9:]
    s=pl.program_id(0)
    slot=lax.rem(s,2)
    def fetch(step, sl):
        fetch_pieces(wps, metas, perm, S0+step, lambda src, blk: pltpu.make_async_copy(src.at[3], W.at[sl, pl.ds(pl.multiple_of(blk*SLAB,SLAB),SLAB), :], sem.at[sl]).start())
    @pl.when(s==0)
    def _():
        fetch(0,0)
        row=lax.broadcasted_iota(jnp.int32,(KV,T),0); col=lax.broadcasted_iota(jnp.int32,(KV,T),1)
        ok=(kseg[...]==qseg[...])|(row==col)
        bias[...]=jnp.where(ok,0.0,-1e30)
    @pl.when(s+1<N)
    def _(): fetch(s+1,1-slot)
    pltpu.make_async_copy(W.at[slot],W.at[slot],sem.at[slot]).wait()
    n=C//128
    dob[...]=dot(dres[...],W[slot],1,0).astype(BF)
    for p in range(n):
        kp=k_in[0,:,p*128:(p+1)*128]; vp=v_in[0,:,p*128:(p+1)*128]
        qp=q_in[0,:,p*128:(p+1)*128]; dp_=dob[:,p*128:(p+1)*128]
        half=lax.broadcasted_iota(jnp.int32,qp.shape,1)<64
        parts=[]
        dvs=None
        for h in range(2):
            mk=half if h==0 else ~half
            qm=jnp.where(mk,qp,jnp.zeros_like(qp)); dm=jnp.where(mk,dp_,jnp.zeros_like(dp_))
            pt=jnp.exp(dot(kp,qm,1,1)+bias[...]-lse_in[0,2*p+h:2*p+h+1,:])
            dpt=dot(vp,dm,1,1)
            delta=jnp.sum(pt*dpt,axis=0,keepdims=True)
            ds=(pt*(dpt-delta)).astype(BF)
            dv=dot(pt.astype(BF),dm,1,0); dk=dot(ds,qm,1,0)
            dqt=dot(kp,ds,0,0)
            parts.append(dqt[h*64:(h+1)*64])
            if h==0: dva,dka=dv,dk
            else: dva,dka=dva+dv,dka+dk
        dqs[:,p*128:(p+1)*128]=jnp.concatenate(parts,axis=0).T*(1.0/math.sqrt(HEAD_DIM))
        dks[:,p*128:(p+1)*128]=dka
        dv_out[0,:,p*128:(p+1)*128]=dva.astype(BF)
    cw=wide(cos[...],n); sw=wide(sin[...],n)
    dq_out[0]=turn(dqs[...],cw[:T],-sw[:T],lower_lanes(T,C)).astype(BF)
    dk_out[0]=turn(dks[...],cw,-sw,lower_lanes(KV,C)).astype(BF)

def bwd_attn(perm,dres,cos,sin,kseg,qseg,q,k,v,lse,pieces,S0=0,N=None,carry=()):
    wps,metas,S,SLAB,C=pieces
    T,D=dres.shape; KV=k.shape[1]; HG=C//HEAD_DIM
    N=S if N is None else N
    ib=lambda rows:pl.BlockSpec((1,rows,C),lambda s,p:(s+S0,0,0))
    gs=pltpu.PrefetchScalarGridSpec(num_scalar_prefetch=1,grid=(N,),
        in_specs=[full((T,D)),full((KV,128)),full((KV,128)),full((KV,1)),full((1,T)),ib(T),ib(KV),ib(KV),pl.BlockSpec((1,HG,T),lambda s,p:(s+S0,0,0))]+[pl.BlockSpec(memory_space=ANY)]*(len(wps)+len(carry)),
        out_specs=[ib(T),ib(KV),ib(KV)],
        scratch_shapes=[pltpu.VMEM((2,D,C),BF),pltpu.VMEM((KV,T),F32),pltpu.VMEM((T,C),BF),pltpu.VMEM((T,C),F32),pltpu.VMEM((KV,C),F32),pltpu.SemaphoreType.DMA((2,))])
    sd=jax.ShapeDtypeStruct
    fl=(2*T*D*C+10*T*KV*C)*N
    return pl.pallas_call(functools.partial(bwd_attn_kernel,T=T,KV=KV,C=C,metas=metas,S=S,SLAB=SLAB,S0=S0,N=N),grid_spec=gs,
        out_shape=[sd((S,T,C),BF),sd((S,KV,C),BF),sd((S,KV,C),BF)],
        input_output_aliases={10+len(wps)+i:i for i in range(len(carry))},
        cost_estimate=pl.CostEstimate(flops=1,transcendentals=0,bytes_accessed=1),name="attn_bwd")(perm,dres,cos,sin,kseg,qseg,q,k,v,lse,*wps,*carry)

def grad_attn_kernel(perm, slots, a1T, dresT, xhat, o_in, dq_in, dk_in, dv_in, *rest, T, KV, C, R, metas, S, SLAB):
    wps = rest[:len(metas)]
    da_own, da_far, gg_out, d0, d1, W, stg, acc, sem, osem = rest[len(metas):]
    s=pl.program_id(0)
    slot=lax.rem(s,2)
    def fetch(step, sl):
        fetch_pieces(wps, metas, perm, step, lambda src, blk: pltpu.make_async_copy(src.at[pl.ds(0,3)], W.at[sl, :, pl.ds(pl.multiple_of(blk*SLAB,SLAB),SLAB), :], sem.at[sl]).start())
    @pl.when(s==0)
    def _(): fetch(0,0)
    @pl.when(s+1<S)
    def _(): fetch(s+1,1-slot)
    @pl.when(s>=2)
    def _(): pltpu.make_async_copy(stg.at[slot],stg.at[slot],osem.at[slot]).wait()
    stg[slot,0]=dot(a1T[:,:T],dq_in[0],1,0).astype(BF)
    stg[slot,1]=dot(a1T[...],dk_in[0],1,0).astype(BF)
    stg[slot,2]=dot(a1T[...],dv_in[0],1,0).astype(BF)
    stg[slot,3]=dot(dresT[...],o_in[0],1,0).astype(BF)
    for r in range(R):
        dst=(d0,d1)[r%2]
        pltpu.make_async_copy(stg.at[slot,:,pl.ds(pl.multiple_of(perm[R+r]*SLAB,SLAB),SLAB),:], dst.at[r//2, slots[s]], osem.at[slot]).start()
    pltpu.make_async_copy(W.at[slot],W.at[slot],sem.at[slot]).wait()
    c=dot(dk_in[0],W[slot,1],1,1)+dot(dv_in[0],W[slot,2],1,1)
    cq=dot(dq_in[0],W[slot,0],1,1)
    @pl.when(s==0)
    def _():
        acc[...]=c
        acc[:T,:]=acc[:T,:]+cq
    @pl.when(s>0)
    def _():
        acc[...]=acc[...]+c
        acc[:T,:]=acc[:T,:]+cq
    @pl.when(s==S-1)
    def _():
        gg_out[...]=jnp.sum(acc[...]*xhat[...].astype(F32),axis=0,keepdims=True)
        da_own[...]=acc[:T,:]
        da_far[...]=acc[T:,:].astype(BF)
        for sl in range(min(S,2)):
            pltpu.make_async_copy(stg.at[sl],stg.at[sl],osem.at[sl]).wait()

def grad_attn(perm2,slots,a1T,dresT,xhat,o,dq,dk,dv,pieces):
    wps,metas,S,SLAB,C=pieces
    R=perm2.shape[0]//2
    D,T=dresT.shape; KV=dk.shape[1]
    A=pl.BlockSpec(memory_space=ANY)
    ib=lambda rows:pl.BlockSpec((1,rows,C),lambda s,p,q:(s,0,0))
    gs=pltpu.PrefetchScalarGridSpec(num_scalar_prefetch=2,grid=(S,),
        in_specs=[full((D,KV)),full((D,T)),full((KV,D)),ib(T),ib(T),ib(KV),ib(KV)]+[A]*len(wps),
        out_specs=[full((T,D)),full((KV-T,D)),full((1,D)),A,A],
        scratch_shapes=[pltpu.VMEM((2,3,D,C),BF),pltpu.VMEM((2,4,D,C),BF),pltpu.VMEM((KV,D),F32),pltpu.SemaphoreType.DMA((2,)),pltpu.SemaphoreType.DMA((2,))])
    sd=jax.ShapeDtypeStruct
    piece=sd((R//2,S,4,SLAB,C),BF)
    return pl.pallas_call(functools.partial(grad_attn_kernel,T=T,KV=KV,C=C,R=R,metas=metas,S=S,SLAB=SLAB),grid_spec=gs,
        out_shape=[sd((T,D),F32),sd((KV-T,D),BF),sd((1,D),F32),piece,piece],
        cost_estimate=pl.CostEstimate(flops=1,transcendentals=0,bytes_accessed=1),name="attn_grad")(perm2,slots,a1T,dresT,xhat,o,dq,dk,dv,*wps)

def split3(x):
    hi=x.astype(BF)
    return hi,(x-hi.astype(F32)).astype(BF)

def dot3(a,b,ca,cb):
    ah,al=a; bh,bl=b
    return dot(ah,bh,ca,cb)+(dot(ah,bl,ca,cb)+dot(al,bh,ca,cb))

def soap_kernel(sc, g_in, first, second, left, right, *rest, turned):
    f_out, s_out, u_out, n_out = rest[-4:]
    step,b1,b2=sc[0],sc[1],sc[2]
    ql=split3(left[0]); qr=split3(right[0])
    if turned:
        x=dot3(split3(g_in[0]),ql,1,0)
        r=dot3(split3(x),qr,0,0).T
    else:
        x=dot3(ql,split3(g_in[0]),0,0)
        r=dot3(split3(x),qr,1,0)
    fn=b1*first[0]+(1.0-b1)*r
    sn=b2*second[0]+(1.0-b2)*r*r
    f_out[0]=fn; s_out[0]=sn
    n=fn/(jnp.sqrt(sn)+ADAM_EPS)
    if turned:
        t=dot3(split3(dot3(qr,split3(n),1,0)),ql,1,1)
    else:
        t=dot3(split3(dot3(ql,split3(n),1,0)),qr,1,1)
    size=n.shape[0]*n.shape[1]
    fac=jnp.sqrt(jnp.sum(n*n,keepdims=True)*(1.0/size))*lax.rsqrt(jnp.sum(t*t,keepdims=True)*(1.0/size)+SCALE_EPS)
    u_out[0]=(-step*fac)*t
    n_out[0]=jnp.broadcast_to(fac,(8,128))

def soap(scalars,g,first,second,left,right,turned,K0=0,N=None,carry=()):
    K=first.shape[0]
    N=K if N is None else N
    b=lambda x:pl.BlockSpec((1,)+x.shape[1:],lambda k,s:(k+K0,0,0))
    sd=jax.ShapeDtypeStruct
    o=sd(first.shape,F32)
    outs=[o,o,o,sd((K,8,128),F32)]
    gs=pltpu.PrefetchScalarGridSpec(num_scalar_prefetch=1,grid=(N,),
        in_specs=[b(x) for x in (g,first,second,left,right)]+[pl.BlockSpec(memory_space=ANY)]*len(carry),out_specs=[b(x) for x in outs])
    return pl.pallas_call(functools.partial(soap_kernel,turned=turned),grid_spec=gs,out_shape=outs,
        input_output_aliases={6+i:i for i in range(len(carry))},
        cost_estimate=pl.CostEstimate(flops=1,transcendentals=0,bytes_accessed=1),
        name="soap_"+("mlp" if turned else "attn"))(scalars,g,first,second,left,right,*carry)

def norm_kernel(own, far, gain, a1, a1T, xh, *, T):
    for lo,ref in ((0,own),(T,far)):
        v=ref[...].astype(F32)
        ce=v-jnp.mean(v,axis=1,keepdims=True)
        x=ce*lax.rsqrt(jnp.mean(ce*ce,axis=1,keepdims=True)+NORM_EPS)
        n=ref.shape[0]
        xh[lo:lo+n,:]=x.astype(BF)
        y=x*gain[...]
        a1[lo:lo+n,:]=y.astype(BF)
        a1T[:,lo:lo+n]=y.T.astype(BF)

def norm_first(own,far,gain):
    T,D=own.shape; KV=T+far.shape[0]
    sd=jax.ShapeDtypeStruct
    outs=[sd((KV,D),BF),sd((D,KV),BF),sd((KV,D),BF)]
    return pl.pallas_call(functools.partial(norm_kernel,T=T),grid=(1,),in_specs=[full(x.shape) for x in (own,far,gain)],
        out_specs=[full(o.shape) for o in outs],out_shape=outs,
        cost_estimate=pl.CostEstimate(flops=1,transcendentals=0,bytes_accessed=1),name="norm_first")(own,far,gain)

def input_kernel(hid, da, dres, gain, *rest):
    out=rest[-1]
    v=hid[...].astype(F32)
    ce=v-jnp.mean(v,axis=1,keepdims=True)
    rstd=lax.rsqrt(jnp.mean(ce*ce,axis=1,keepdims=True)+NORM_EPS)
    x=ce*rstd
    d=da[...]
    for r in rest[:-1]:
        d=d+r[...].astype(F32)
    e=d*gain[...]
    out[...]=(dres[...]+rstd*(e-jnp.mean(e,axis=1,keepdims=True)-x*jnp.mean(e*x,axis=1,keepdims=True))).astype(BF)

def input_back(hid,da,dres,gain,*back):
    args=(hid,da,dres,gain)+back
    return pl.pallas_call(input_kernel,grid=(1,),in_specs=[full(x.shape) for x in args],out_specs=full(hid.shape),
        out_shape=jax.ShapeDtypeStruct(hid.shape,BF),
        cost_estimate=pl.CostEstimate(flops=1,transcendentals=0,bytes_accessed=1),name="input_back")(*args)


def ring_order(count):
    return list(range(0, count, 2)) + list(range(1, count, 2))[::-1]


def swap_dp(value, bit, owners):
    return lax.ppermute(value, "dp", [(i, i ^ bit) for i in range(owners)])


def to_ring_pred(value, shards):
    ring = ring_order(shards)
    return lax.ppermute(
        value, "tensor", [(ring[p], ring[(p - 1) % shards]) for p in range(shards)]
    )


def to_ring_succ(value, shards):
    ring = ring_order(shards)
    return lax.ppermute(
        value, "tensor", [(ring[p], ring[(p + 1) % shards]) for p in range(shards)]
    )


def along_line(value, steps, shards):
    ring = ring_order(shards)
    return lax.ppermute(
        value, "tensor", [(ring[p], ring[(p + steps) % shards]) for p in range(shards)]
    )


def add_low(one, two):
    return (one.astype(F32) + two.astype(F32)).astype(BF)


def halve(pieces, bits, owners):
    for bit in bits:
        live = sorted(bits[bits.index(bit):], reverse=True)
        axis = live.index(bit)
        send = lax.index_in_dim(pieces, 1, axis, keepdims=False)
        keep = lax.index_in_dim(pieces, 0, axis, keepdims=False)
        pieces = add_low(keep, swap_dp(send, bit, owners))
    return pieces


def reduce_pieces(even, odd, cut, owners, shards):
    mine = add_low(even, swap_dp(odd, 1, owners))
    bits = [1 << b for b in range(1, owners.bit_length() - 1)]
    mine = mine.reshape((2,) * len(bits) + mine.shape[1:])
    low = halve(mine[..., :cut, :], bits[::-1], owners)
    high = halve(mine[..., cut:, :], bits, owners)
    both = jnp.concatenate([low, high], axis=-2)
    moving = both[shards - 1]
    for left in range(shards - 2, -1, -1):
        moving = to_ring_pred(moving, shards)
        moving = moving.astype(F32) + both[left].astype(F32)
        if left:
            moving = moving.astype(BF)
    return moving


def all_sum(value, owners, shards):
    for axis, count in (("dp", owners), ("tensor", shards)):
        step = 1
        while step < count:
            value = value + lax.ppermute(value, axis, [(i, i ^ step) for i in range(count)])
            step *= 2
    return value


def after(value, *earlier):
    return lax.optimization_barrier((value,) + earlier)[0]


def add_all(*values):
    total = values[0].astype(F32)
    for value in values[1:]:
        total = total + value.astype(F32)
    return total


def gather_stack(stacked, owners):
    half = stacked.shape[0] // 2
    by_x, by_y = swap_dp(stacked, 2, owners), swap_dp(stacked, 4, owners)
    return by_x, by_y, swap_dp(by_x[:half], 4, owners), swap_dp(by_y[half:], 2, owners)


def to_core(arrays, owners):
    return [swap_dp(a, 1, owners) for a in arrays]


def with_partner(arrays, metas, owners):
    return arrays + [swap_dp(a, 1, owners) for a in arrays], metas + tuple((m[0] + 1,) + m[1:] for m in metas)


def cross_sends(even, core, half):
    low = add_all(even[3, :half], core[3, :half]).astype(BF)
    high = add_all(even[3, half:], core[3, half:]).astype(BF)
    return low, high


def side_sends(even, core, from_y, from_x, half):
    to_x = jnp.concatenate(
        [add_all(even[1, :half], core[1, :half], from_y), add_all(even[1, half:], core[1, half:])]
    ).astype(BF)
    to_y = jnp.concatenate(
        [add_all(even[2, :half], core[2, :half]), add_all(even[2, half:], core[2, half:], from_x)]
    ).astype(BF)
    return to_x, to_y


def own_part(even, core, from_x, from_y, slot):
    return add_all(even[0, slot], core[0, slot], from_x[slot], from_y[slot])


def ring_sum(even, core, from_x, from_y, shards):
    moving = None
    for slot in list(range(1, shards)) + [0]:
        part = own_part(even, core, from_x, from_y, slot)
        if moving is not None:
            part = part + to_ring_succ(moving, shards).astype(F32)
        moving = part.astype(BF)
    return part


def per_device(
    hidden_in, out_grad, attn_weight, mlp_weight, norm_gain,
    attn_first, attn_second, attn_left, attn_right,
    mlp_first, mlp_second, mlp_left, mlp_right,
    gain_first, gain_second, owner_rows, segment_ids, positions, valid,
    step, learn_rate, beta_first, beta_second,
):
    owners = lax.axis_size("dp")
    shards = lax.axis_size("tensor")
    dp_index = lax.axis_index("dp")
    place = lax.axis_index("tensor")
    rows, width = hidden_in.shape
    slab = attn_weight.shape[1]
    hid_cols = mlp_weight.shape[2]
    span = SEQ_LEN // rows
    within = place % span
    base = place - within
    half = shards // 2
    gain_rows = norm_gain.astype(F32)

    def from_peer(value, ahead):
        pairs = [(g + (w + ahead) % span, g + w) for g in range(0, shards, span) for w in range(span)]
        return lax.ppermute(value, "tensor", pairs)

    def sequence_rows(column):
        return jnp.concatenate(
            [lax.dynamic_slice_in_dim(column, (base + (within + d) % span) * rows, rows, 0) for d in range(span)]
        )

    joined = 128 // slab if slab < 128 else 1
    fast = owners == 8 and joined == 1 and shards == 4 and span == 2
    both = ("dp", "tensor")
    mlp_turned = jnp.swapaxes(mlp_weight, 1, 2)
    if not fast:
        attn_all = lax.all_gather(attn_weight, both, axis=0, tiled=False).reshape((owners, shards) + attn_weight.shape)
        mlp_all = lax.all_gather(mlp_turned, both, axis=0, tiled=False).reshape((owners, shards) + mlp_turned.shape)

    slot_ids = jnp.arange(owners, dtype=jnp.int32)
    rel_owner = jnp.sum(
        jnp.where((slot_ids[:, None] ^ dp_index) == slot_ids[None, :], owner_rows[None, :], 0), axis=1
    )
    ring = ring_order(shards)
    ring_place = jnp.array([ring.index(z) for z in range(shards)], jnp.int32)
    my_place = jnp.sum(jnp.where(jnp.arange(shards) == place, ring_place, 0))
    slots = (my_place - ring_place) % shards
    attn_perm = jnp.concatenate([rel_owner if fast else owner_rows, rel_owner]).astype(jnp.int32)
    if fast:
        slots = jnp.arange(shards, dtype=jnp.int32)
    if joined == 1:
        mlp_perm = attn_perm
    else:
        inverse = jnp.sum(jnp.where(owner_rows[None, :] == slot_ids[:, None], slot_ids[None, :], 0), axis=1)
        mlp_all = jnp.take(mlp_all, inverse, axis=0).reshape((owners // joined, joined) + mlp_all.shape[1:])
        mlp_all = jnp.moveaxis(mlp_all, 1, 4)
        mlp_all = mlp_all.reshape(mlp_all.shape[:4] + (joined * slab,))
        blocks = jnp.arange(owners // joined, dtype=jnp.int32)
        mlp_perm = jnp.concatenate([blocks, blocks])

    seg = sequence_rows(segment_ids)
    keep_seq = sequence_rows(valid)
    pos = sequence_rows(positions)
    half_dim = HEAD_DIM // 2
    frequency = jnp.exp(jnp.arange(half_dim, dtype=F32) * (-2.0 * math.log(ROPE_BASE) / HEAD_DIM))
    angles = pos.astype(F32)[:, None] * frequency[None, :]
    cos_half, sin_half = jnp.cos(angles), jnp.sin(angles)
    cos_table = jnp.concatenate([cos_half] * 4, axis=1)
    sin_table = jnp.concatenate([-sin_half, sin_half] * 2, axis=1)
    key_seg = jnp.where(keep_seq > 0, seg, -1)[:, None]
    query_seg = seg[None, :rows]
    keep_own = keep_seq[:rows].astype(F32)[:, None]

    first_gain, second_gain = gain_rows[0:1], gain_rows[1:2]
    if fast:
        together = lax.optimization_barrier
        mlp_x, mlp_y, mlp_z = [None] * 4, [None] * 4, [None] * 4
        line_1 = along_line(attn_weight, 1, shards)
        mlp_x[0], mlp_y[0] = swap_dp(mlp_turned, 2, owners), swap_dp(mlp_turned, 4, owners)
        tables = (cos_table, sin_table, key_seg, query_seg, keep_own, attn_perm, mlp_perm, slots, first_gain, second_gain)
        line_1, mlp_x[0], mlp_y[0] = together((line_1, mlp_x[0], mlp_y[0]))
        pair_a = jnp.stack([attn_weight, line_1])
        x_a, y_a = swap_dp(pair_a, 2, owners), swap_dp(pair_a, 4, owners)
        far_rows = from_peer(after(hidden_in, line_1), 1)
        core_0 = to_core([after(a, line_1) for a in (mlp_turned, mlp_x[0])], owners)
        x_a, y_a, core_0, tables = together((x_a, y_a, core_0, tables))
        cos_table, sin_table, key_seg, query_seg, keep_own, attn_perm, mlp_perm, slots, first_gain, second_gain = tables
        z_a, mlp_z[0] = swap_dp(x_a, 4, owners), swap_dp(after(mlp_y[0], y_a), 2, owners)
        line_2, line_3 = along_line(after(line_1, x_a), 1, shards), along_line(after(attn_weight, x_a), 3, shards)
        normal = norm_first(hidden_in, far_rows, first_gain)
        z_a, mlp_z[0], normal, line_2, line_3 = together((z_a, mlp_z[0], tuple(normal), line_2, line_3))
        pair_b = jnp.stack([line_2, line_3])
        x_b, y_b = swap_dp(pair_b, 2, owners), swap_dp(pair_b, 4, owners)
        mlp_line = [mlp_turned, along_line(after(mlp_turned, line_3), 1, shards), None, None]
        core_a4 = to_core([after(a, z_a) for a in (pair_a, x_a, y_a, z_a)], owners)
        core_b = [swap_dp(after(pair_b, core_a4[1]), 1, owners)]
        normal, core_a4, mlp_line[1], core_b, x_b, y_b = together((tuple(normal), core_a4, mlp_line[1], core_b, x_b, y_b))
        z_b = swap_dp(y_b, 2, owners)
        mlp_x[1], mlp_y[1] = swap_dp(mlp_line[1], 2, owners), swap_dp(mlp_line[1], 4, owners)
        mlp_line[3] = along_line(after(mlp_turned, mlp_line[1]), 3, shards)
        mlp_line[2] = along_line(mlp_line[1], 1, shards)
        first_norm, first_turned, xhat_low = normal

        def attn_set(arrays, first):
            return arrays, tuple((r, first, 2, shards) for r in (0, 2, 4, 6, 1, 3, 5, 7))

        sizes = (shards, slab, attn_weight.shape[2])
        arrays_a, metas_a = attn_set([pair_a, x_a, y_a, z_a, *core_a4], 0)
        attn_part_a = (arrays_a, metas_a, *sizes)
    else:
        far_rows = [from_peer(hidden_in, d) for d in range(1, span)]
        attn_pieces = ([attn_all], (None,), shards, slab, attn_weight.shape[2])
        first_norm, first_turned, xhat_low = norm_first(hidden_in, jnp.concatenate(far_rows), first_gain)
    back_args = (cos_table, sin_table, key_seg, query_seg)
    fwd_args = (attn_perm, first_norm, hidden_in, second_gain, cos_table, sin_table, key_seg, query_seg, keep_own)
    if fast:
        carry = fwd_attn(*fwd_args, attn_part_a, S0=0, N=half)
        z_b, mlp_x[1], mlp_y[1], mlp_line[3], mlp_line[2], carry = together(
            (z_b, mlp_x[1], mlp_y[1], mlp_line[3], mlp_line[2], tuple(carry))
        )
        core_b = core_b + to_core([after(x_b, z_b), after(y_b, z_b)], owners)
        core_z_b = swap_dp(z_b, 1, owners)
        core_b, core_z_b, mlp_x[1], mlp_y[1], mlp_line[3], mlp_line[2] = together((core_b, core_z_b, mlp_x[1], mlp_y[1], mlp_line[3], mlp_line[2]))
        mlp_z[1] = swap_dp(mlp_y[1], 2, owners)
        mlp_y[2] = swap_dp(mlp_line[2], 4, owners)
        arrays_b, metas_b = attn_set([pair_b, x_b, y_b, z_b, *core_b, core_z_b], 2)
        attn_part_b = (arrays_b, metas_b, *sizes)
        attn_pieces = (arrays_a + arrays_b, metas_a + metas_b, *sizes)
        mlp_x[3], mlp_y[3] = swap_dp(mlp_line[3], 2, owners), swap_dp(mlp_line[3], 4, owners)
        out = fwd_attn(*fwd_args, attn_part_b, S0=half, N=half, carry=carry)
        mlp_x[3], mlp_y[3], mlp_z[1], mlp_y[2], out = together((mlp_x[3], mlp_y[3], mlp_z[1], mlp_y[2], tuple(out)))
        queries, keys, values, attended, log_sums, resid, second_norm, stat_a = out

        def mlp_set(slot):
            return [mlp_line[slot], mlp_x[slot], mlp_y[slot], mlp_z[slot]]

        def mlp_pieces(*slots_of):
            arrays, metas = [], []
            for slot, got in slots_of:
                arrays += [a[None] for a in got]
                metas += [(r, slot, 1, shards) for r in (0, 2, 4, 6, 1, 3, 5, 7)]
            return arrays, tuple(metas), shards, slab, hid_cols

        set_0, set_1 = mlp_set(0), mlp_set(1)
        core_1 = to_core([after(a, mlp_z[1]) for a in set_1], owners)
        core_0 = core_0 + to_core([after(a, core_1[1]) for a in (mlp_y[0], mlp_z[0])], owners)
        core_1, core_0, second_norm, mlp_x[3], mlp_y[2] = together((core_1, core_0, second_norm, mlp_x[3], mlp_y[2]))
        mlp_z[3], mlp_z[2] = swap_dp(mlp_x[3], 4, owners), swap_dp(mlp_y[2], 2, owners)
        mlp_x[2] = swap_dp(after(mlp_line[2], second_norm), 2, owners)
        core_3 = to_core([mlp_line[3], mlp_x[3]], owners)
        mlp_args = (mlp_perm, slots, second_norm, out_grad, resid, second_gain, keep_own)
        out = mlp(*mlp_args, mlp_pieces((0, set_0 + core_0), (1, set_1 + core_1)), S0=0, N=half)
        mlp_x[2], mlp_z[2], mlp_z[3], core_3, out = together((mlp_x[2], mlp_z[2], mlp_z[3], core_3, tuple(out)))
        *carry, even_a, odd_a = out
        set_2, set_3 = mlp_set(2), mlp_set(3)
        core_2 = to_core([after(a, odd_a) for a in set_2], owners)
        core_3 = core_3 + to_core([after(a, odd_a) for a in set_3[2:]], owners)
        core_2, core_3, carry = together((core_2, core_3, carry))
        core_a = swap_dp(after(odd_a, core_2[3]), 1, owners)
        out = mlp(*mlp_args, mlp_pieces((2, set_2 + core_2), (3, set_3 + core_3)), S0=half, N=half, carry=carry)
        core_a, out = together((core_a, tuple(out)))
        output, dresid, dres_low, dres_turned, gain_two, stat_m, even_b, odd_b = out
        low, high = cross_sends(even_a, core_a, 1)
        low, high, dres_low = together((low, high, dres_low))
        from_y, from_x = swap_dp(low, 4, owners), swap_dp(high, 2, owners)
        core_b2 = swap_dp(odd_b, 1, owners)
        fwd_kept = (queries, keys, values, log_sums, attn_pieces)
        grads = bwd_attn(attn_perm, dres_low, *back_args, *fwd_kept, S0=0, N=half)
        from_y, from_x, core_b2, *grads = together((from_y, from_x, core_b2, *grads))
        low, high = cross_sends(even_b, core_b2, 1)
        to_x, to_y = side_sends(even_a, core_a, from_y, from_x, 1)
        low, high, to_x, to_y, dres_low = together((low, high, to_x, to_y, dres_low))
        from_y, from_x = swap_dp(low, 4, owners), swap_dp(high, 2, owners)
        back_x, back_y = swap_dp(to_x, 2, owners), swap_dp(to_y, 4, owners)
        grads = bwd_attn(attn_perm, dres_low, *back_args, *fwd_kept, S0=half, N=half, carry=tuple(grads))
        from_y, from_x, *grads = together((from_y, from_x, *grads))
        to_x, to_y = side_sends(even_b, core_b2, from_y, from_x, 1)
        to_x, to_y, back_x, back_y = together((to_x, to_y, back_x, back_y))
        from_x, from_y = swap_dp(to_x, 2, owners), swap_dp(to_y, 4, owners)
        ring_1 = own_part(even_a, core_a, back_x, back_y, 1).astype(BF)
        ring_1, dres_turned = together((ring_1, dres_turned))
        ring_1 = to_ring_succ(ring_1, shards)
        out = grad_attn(attn_perm, slots, first_turned, dres_turned, xhat_low, attended, *grads, attn_pieces)
        from_x, from_y, ring_1, *out = lax.optimization_barrier((from_x, from_y, ring_1, *out))
        da_own, da_far, gain_one, attn_even, attn_odd = out
    else:
        queries, keys, values, attended, log_sums, resid, second_norm, stat_a = fwd_attn(*fwd_args, attn_pieces)
        output, dresid, dres_low, dres_turned, gain_two, stat_m, mlp_even, mlp_odd = mlp(
            mlp_perm, slots, second_norm, out_grad, resid, second_gain, keep_own,
            ([mlp_all], (None,), shards, mlp_all.shape[-1], hid_cols),
        )
        if joined > 1:
            merged = jnp.stack([mlp_even, mlp_odd], axis=1).reshape((owners // joined,) + mlp_even.shape[1:])
            merged = merged.reshape(merged.shape[:-1] + (joined, slab))
            merged = jnp.moveaxis(merged, -2, 1).reshape((owners,) + mlp_even.shape[1:-1] + (slab,))
            merged = jnp.take(merged, rel_owner, axis=0)
            mlp_even, mlp_odd = merged[0::2], merged[1::2]
        mlp_sum = reduce_pieces(mlp_even, mlp_odd, -(-hid_cols // 32) * 16, owners, shards)
        grads = bwd_attn(attn_perm, dres_low, *back_args, queries, keys, values, log_sums, attn_pieces)
        da_own, da_far, gain_one, attn_even, attn_odd = grad_attn(
            attn_perm, slots, first_turned, dres_turned, xhat_low, attended, *grads, attn_pieces
        )
    def send_back(da_far):
        got = []
        for d in range(1, span):
            pairs = [(g + w, g + (w + d) % span) for g in range(0, shards, span) for w in range(span)]
            got.append(lax.ppermute(da_far[(d - 1) * rows : d * rows], "tensor", pairs))
        return got

    def swap_line(value, bit):
        return lax.ppermute(value, "tensor", [(i, i ^ bit) for i in range(shards)])

    def finish_input(da_back):
        return input_back(hidden_in, da_own, dresid, first_gain, *da_back)

    step_count = step.astype(F32)
    step_size = (
        learn_rate
        * jnp.sqrt(1.0 - jnp.power(beta_second, step_count))
        / (1.0 - jnp.power(beta_first, step_count))
    )
    scalars = jnp.stack([step_size, beta_first, beta_second])

    def flip(value):
        return jnp.swapaxes(value, 1, 2)

    def soap_mlp(total, *part):
        return soap(scalars, total, flip(mlp_first), flip(mlp_second), mlp_left, mlp_right, True, *part)

    sums = jnp.concatenate([jnp.sum(stat_a, axis=1), jnp.sum(stat_m, axis=1), jnp.sum(keep_own)[None]])
    small = jnp.concatenate([gain_one, gain_two, jnp.pad(sums, (0, width - 5))[None]], axis=0)
    if fast:
        attn_core = swap_dp(attn_odd, 1, owners)
        ring_2 = (own_part(even_b, core_b2, from_x, from_y, 0) + ring_1.astype(F32)).astype(BF)
        ring_2 = to_ring_succ(ring_2, shards)
        small = small + swap_dp(small, 1, owners)
        small, attn_core = lax.optimization_barrier((small, attn_core))
        low, high = cross_sends(attn_even, attn_core, half)
        low, high, small = lax.optimization_barrier((low, high, small))
        cross_y, cross_x = swap_dp(low, 4, owners), swap_dp(high, 2, owners)
        small = small + swap_dp(small, 2, owners)
        ring_3 = (own_part(even_b, core_b2, from_x, from_y, 1) + ring_2.astype(F32)).astype(BF)
        ring_3 = to_ring_succ(ring_3, shards)
        small, cross_x, cross_y = lax.optimization_barrier((small, cross_x, cross_y))
        to_x, to_y = side_sends(attn_even, attn_core, cross_y, cross_x, half)
        to_x, to_y, small = lax.optimization_barrier((to_x, to_y, small))
        attn_x, attn_y = swap_dp(to_x, 2, owners), swap_dp(to_y, 4, owners)
        small = small + swap_dp(small, 4, owners)
        da_back = send_back(after(da_far, ring_3))
        mlp_sum = own_part(even_a, core_a, back_x, back_y, 0) + ring_3.astype(F32)
        mlp_new = soap_mlp(mlp_sum)
        attn_x, attn_y, mlp_sum, mlp_new = lax.optimization_barrier((attn_x, attn_y, mlp_sum, tuple(mlp_new)))
        moving = own_part(attn_even, attn_core, attn_x, attn_y, 1).astype(BF)
        for slot in range(1, shards):
            moving, small, da_back = lax.optimization_barrier((moving, small, da_back))
            moving = to_ring_succ(moving, shards)
            if slot < 3:
                small = small + swap_line(small, slot)
            if slot == 1:
                input_grad = finish_input(da_back)
                moving, input_grad = lax.optimization_barrier((moving, input_grad))
            moving, small = lax.optimization_barrier((moving, small))
            moving = moving.astype(F32) + own_part(attn_even, attn_core, attn_x, attn_y, (slot + 1) % shards)
            if slot + 1 < shards:
                moving = moving.astype(BF)
        attn_sum = moving
    else:
        attn_sum = reduce_pieces(attn_even, attn_odd, slab // 2, owners, shards)
        small = all_sum(small, owners, shards)
        mlp_new = soap_mlp(mlp_sum)
        input_grad = finish_input(send_back(da_far))
    gain_grad = small[:2]
    stat_sums = small[2]

    attn_grad = attn_sum
    attn_first_new, attn_second_new, attn_update, attn_scale = soap(
        scalars, attn_sum, attn_first, attn_second, attn_left, attn_right, False
    )
    mlp_grad, mlp_first_new, mlp_second_new, mlp_update = (flip(v) for v in (mlp_sum, *mlp_new[:3]))
    mlp_scale = mlp_new[3]
    gain_first_new = beta_first * gain_first + (1.0 - beta_first) * gain_grad
    gain_second_new = beta_second * gain_second + (1.0 - beta_second) * gain_grad * gain_grad
    gain_update = -step_size * gain_first_new / (jnp.sqrt(gain_second_new) + ADAM_EPS)
    root_means = jnp.sqrt(stat_sums[:4] / (stat_sums[4] * width))
    norm_scale = jnp.concatenate([attn_scale[:, :1, :1], mlp_scale[:, :1, :1]], axis=0)
    return (
        output, input_grad, attn_grad, mlp_grad, gain_grad,
        attn_first_new, attn_second_new, mlp_first_new, mlp_second_new,
        gain_first_new, gain_second_new, attn_update, mlp_update, gain_update,
        norm_scale, root_means,
    )


def solution(mesh):
    rows = P(("dp", "tensor"), None)
    block = P(None, "dp", "tensor")
    return jax.shard_map(
        per_device,
        mesh=mesh,
        in_specs=(rows, rows, block, block, P()) + (block,) * 8 + (P(),) * 3 + (P("dp"),) * 3 + (P(),) * 4,
        out_specs=(rows, rows, block, block, P(), block, block, block, block, P(), P(), block, block, P(), block, P()),
        check_vma=False,
    )
```

```python
import functools
import math

import jax
import jax.numpy as jnp
from jax import lax
from jax.experimental import pallas as pl
from jax.experimental.pallas import tpu as pltpu
from jax.sharding import PartitionSpec as P

HEAD_DIM = 64
SEQ_LEN = 1024
NORM_EPS = 1e-05
ROPE_BASE = 160000.0
ADAM_EPS = 1e-08
SCALE_EPS = 1e-06
PRECISE = lax.Precision.HIGHEST
BF = jnp.bfloat16
F32 = jnp.float32
ANY = pl.ANY


def dot(a,b,ca,cb):
    return lax.dot_general(a,b,(((ca,),(cb,)),((),())),preferred_element_type=F32)

def turn(x, cos, sin, lower):
    w=x.shape[1]
    sw=jnp.where(lower, pltpu.roll(x, w-32, 1), pltpu.roll(x, 32, 1))
    return x*cos+sw*sin

def lower_lanes(rows, cols):
    return lax.broadcasted_iota(jnp.int32,(rows,cols),1)%64<32

def wide(t, n):
    return t if n==1 else jnp.concatenate([t]*n,axis=1)

def fetch_pieces(refs, metas, perm, step, copy):
    for ref, meta in zip(refs, metas):
        if meta is None:
            for r in range(ref.shape[0]):
                copy(ref.at[r, step], perm[r])
        else:
            r, first, count, total = meta
            if count == total:
                copy(ref.at[step], perm[r])
            else:
                @pl.when((step >= first) & (step < first + count))
                def _(ref=ref, r=r, first=first):
                    copy(ref.at[jnp.clip(step - first, 0, ref.shape[0] - 1)], perm[r])

def fwd_attn_kernel(perm, a1, hid, gain, cos, sin, kseg, qseg, keep, *rest, T, KV, C, metas, S, SLAB, QB, S0, N):
    wps = rest[:len(metas)]
    rest = rest[len(metas):]
    if S0:
        acc_in, rest = rest[0], rest[6:]
    q_out, k_out, v_out, o_out, lse_out = rest[:5]
    if S0+N==S:
        resid_out, a2_out, stat_out, acc = rest[5:9]
    else:
        acc = rest[5]
    W, bias, osc, sem = rest[-4:]
    s=pl.program_id(0)
    def fetch(step, slot):
        fetch_pieces(wps, metas, perm, S0+step, lambda src, blk: pltpu.make_async_copy(src, W.at[slot, :, pl.ds(pl.multiple_of(blk*SLAB,SLAB),SLAB), :], sem.at[slot]).start())
    slot=lax.rem(s,2)
    @pl.when(s==0)
    def _():
        fetch(0,0)
        row=lax.broadcasted_iota(jnp.int32,(KV,T),0); col=lax.broadcasted_iota(jnp.int32,(KV,T),1)
        ok=(kseg[...]==qseg[...])|(row==col)
        bias[...]=jnp.where(ok,0.0,-1e30)
        acc[...]=acc_in[...] if S0 else jnp.zeros_like(acc)
    @pl.when(s+1<N)
    def _(): fetch(s+1,1-slot)
    pltpu.make_async_copy(W.at[slot],W.at[slot],sem.at[slot]).wait()
    n=C//128
    low_q=lower_lanes(T,C); low_k=lower_lanes(KV,C)
    cw=wide(cos[...],n); sw=wide(sin[...],n)
    q=dot(a1[:T,:],W[slot,0],1,0)
    q_out[0]=(turn(q,cw[:T],sw[:T],low_q).astype(BF)*BF(1/math.sqrt(HEAD_DIM))).astype(BF)
    k=dot(a1[...],W[slot,1],1,0)
    k_out[0]=turn(k,cw,sw,low_k).astype(BF)
    v_out[0]=dot(a1[...],W[slot,2],1,0).astype(BF)
    for p in range(n):
        kp=k_out[0,:,p*128:(p+1)*128]; vp=v_out[0,:,p*128:(p+1)*128]
        for b in range(T//QB):
            qp=q_out[0,b*QB:(b+1)*QB,p*128:(p+1)*128]
            half=lax.broadcasted_iota(jnp.int32,qp.shape,1)<64
            parts=[]
            for h in range(2):
                qm=jnp.where(half if h==0 else ~half,qp,jnp.zeros_like(qp))
                st=dot(kp,qm,1,1)+bias[:,b*QB:(b+1)*QB]
                m=jnp.max(st,axis=0,keepdims=True)
                e=jnp.exp(st-m)
                l=jnp.sum(e,axis=0,keepdims=True)
                ot=dot(vp,e.astype(BF),0,0)
                parts.append(ot[h*64:(h+1)*64]*(1.0/l))
                lse_out[0,pl.ds(2*p+h,1),b*QB:(b+1)*QB]=m+jnp.log(l)
            op=jnp.concatenate(parts,axis=0)
            osc[b*QB:(b+1)*QB,p*128:(p+1)*128]=op.T.astype(BF)
    o_out[0]=osc[...]
    acc[...]+=dot(osc[...],W[slot,3],1,1)
    if S0+N<S:
        return
    @pl.when(s==N-1)
    def _():
        at=acc[...]
        rs=hid[...].astype(F32)+at
        resid_out[...]=rs
        mu=jnp.mean(rs,axis=1,keepdims=True); ce=rs-mu
        var=jnp.mean(ce*ce,axis=1,keepdims=True)
        a2_out[...]=(ce*lax.rsqrt(var+NORM_EPS)*gain[...]).astype(BF)
        kp=keep[...]
        s1=jnp.sum(kp*at*at,axis=0,keepdims=True); s2=jnp.sum(kp*rs*rs,axis=0,keepdims=True)
        stat_out[...]=jnp.concatenate([s1,s2],axis=0)

def full(shape):
    nd=len(shape)
    return pl.BlockSpec(shape,lambda *a:(0,)*nd)

def fwd_attn(perm,a1,hid,gain,cos,sin,kseg,qseg,keep,pieces,S0=0,N=None,carry=(),QB=512):
    wps,metas,S,SLAB,C=pieces
    N=S if N is None else N
    KV,D=a1.shape; T=hid.shape[0]; HG=C//HEAD_DIM
    A=pl.BlockSpec(memory_space=ANY)
    sb=lambda rows:pl.BlockSpec((1,rows,C),lambda s,p:(s+S0,0,0))
    sd=jax.ShapeDtypeStruct
    last=S0+N==S
    tail=[sd((T,D),F32),sd((T,D),BF),sd((2,D),F32)] if last else [sd((T,D),F32)]
    gs=pltpu.PrefetchScalarGridSpec(num_scalar_prefetch=1,grid=(N,),
        in_specs=[full((KV,D)),full((T,D)),full((1,D)),full((KV,128)),full((KV,128)),full((KV,1)),full((1,T)),full((T,1))]+[A]*len(wps)+([full((T,D))]+[A]*5 if S0 else []),
        out_specs=[sb(T),sb(KV),sb(KV),sb(T),pl.BlockSpec((1,HG,T),lambda s,p:(s+S0,0,0))]+[full(t.shape) for t in tail],
        scratch_shapes=([pltpu.VMEM((T,D),F32)] if last else [])+[pltpu.VMEM((2,4,D,C),BF),pltpu.VMEM((KV,T),F32),pltpu.VMEM((T,C),BF),pltpu.SemaphoreType.DMA((2,))])
    return pl.pallas_call(functools.partial(fwd_attn_kernel,T=T,KV=KV,C=C,metas=metas,S=S,SLAB=SLAB,QB=min(QB,T),S0=S0,N=N),grid_spec=gs,
        out_shape=[sd((S,T,C),BF),sd((S,KV,C),BF),sd((S,KV,C),BF),sd((S,T,C),BF),sd((S,HG,T),F32)]+tail,
        input_output_aliases={10+len(wps)+i:i for i in range(5)} if S0 else {},
        cost_estimate=pl.CostEstimate(flops=1,transcendentals=0,bytes_accessed=1),name="attn_fwd")(perm,a1,hid,gain,cos,sin,kseg,qseg,keep,*wps,*((carry[5],)+tuple(carry[:5]) if S0 else ()))

def gelu_parts(x):
    phi=0.5*(1.0+lax.erf(x*(1.0/math.sqrt(2.0))))
    den=jnp.exp(-0.5*x*x)*(1.0/math.sqrt(2.0*math.pi))
    return phi,den

def mlp_kernel(perm, slots, a2, g, resid, gain, keep, *rest, T, D, HC, R, metas, S, SLAB, TB, S0, N):
    wps = rest[:len(metas)]
    rest = rest[len(metas):]
    if S0:
        y_in, da_in = rest[:2]
        rest = rest[2:]
    if S0+N==S:
        out, dres_out, dresb_out, dresT_out, gg_out, stat_out = rest[:6]
        rest = rest[6:]
        d0, d1, y, da = rest[:4]
    else:
        y, da, d0, d1 = rest[:4]
    W, stg, hT, dgT, duT, sem, osem = rest[4:]
    s=pl.program_id(0)
    slot=lax.rem(s,2)
    def fetch(step, sl):
        fetch_pieces(wps, metas, perm, S0+step, lambda src, blk: pltpu.make_async_copy(src, W.at[sl, :, :, pl.ds(pl.multiple_of(blk*SLAB,SLAB),SLAB)], sem.at[sl]).start())
    @pl.when(s==0)
    def _(): fetch(0,0)
    @pl.when(s+1<N)
    def _(): fetch(s+1,1-slot)
    pltpu.make_async_copy(W.at[slot],W.at[slot],sem.at[slot]).wait()
    for b in range(T//TB):
        lo,hi=b*TB,(b+1)*TB
        ga=dot(W[slot,0],a2[lo:hi,:],1,1)
        up=dot(W[slot,1],a2[lo:hi,:],1,1)
        dh=dot(W[slot,2],g[lo:hi,:],1,1)
        phi,den=gelu_parts(ga)
        ge=ga*phi
        hT[:,lo:hi]=(ge*up).astype(BF)
        dgT[:,lo:hi]=(dh*up*(phi+ga*den)).astype(BF)
        duT[:,lo:hi]=(dh*ge).astype(BF)
    yc=dot(hT[...],W[slot,2],0,0)
    dc=dot(dgT[...],W[slot,0],0,0)+dot(duT[...],W[slot,1],0,0)
    @pl.when(s==0)
    def _():
        y[...]=yc+y_in[...] if S0 else yc
        da[...]=dc+da_in[...] if S0 else dc
    @pl.when(s>0)
    def _():
        y[...]+=yc; da[...]+=dc
    @pl.when(s>=2)
    def _(): pltpu.make_async_copy(stg.at[slot],stg.at[slot],osem.at[slot]).wait()
    stg[slot,0]=dot(dgT[...],a2[...],1,0).astype(BF)
    stg[slot,1]=dot(duT[...],a2[...],1,0).astype(BF)
    stg[slot,2]=dot(hT[...],g[...],1,0).astype(BF)
    for r in range(R):
        dst=(d0,d1)[r%2]
        pltpu.make_async_copy(stg.at[slot,:,:,pl.ds(pl.multiple_of(perm[R+r]*SLAB,SLAB),SLAB)], dst.at[r//2, slots[S0+s]-S0], osem.at[slot]).start()
    if S0+N==S:
        @pl.when(s==N-1)
        def _():
            br=y[...]; rs=resid[...]; gf=g[...].astype(F32)
            res=rs+br
            out[...]=res.astype(BF)
            kp=keep[...]
            s1=jnp.sum(kp*br*br,axis=0,keepdims=True); s2=jnp.sum(kp*res*res,axis=0,keepdims=True)
            stat_out[...]=jnp.concatenate([s1,s2],axis=0)
            mu=jnp.mean(rs,axis=1,keepdims=True); ce=rs-mu
            rstd=lax.rsqrt(jnp.mean(ce*ce,axis=1,keepdims=True)+NORM_EPS)
            xh=ce*rstd
            d=da[...]
            gg_out[...]=jnp.sum(d*xh,axis=0,keepdims=True)
            e=d*gain[...]
            dr=gf+rstd*(e-jnp.mean(e,axis=1,keepdims=True)-xh*jnp.mean(e*xh,axis=1,keepdims=True))
            dres_out[...]=dr
            db=dr.astype(BF)
            dresb_out[...]=db
            dresT_out[...]=dr.T.astype(BF)
    @pl.when(s==N-1)
    def _():
        for sl in range(min(N,2)):
            pltpu.make_async_copy(stg.at[sl],stg.at[sl],osem.at[sl]).wait()

def mlp(perm2,slots,a2,g,resid,gain,keep,pieces,S0=0,N=None,carry=(),TB=256):
    wps,metas,S,SLAB,HC=pieces
    N=S if N is None else N
    R=perm2.shape[0]//2
    T,D=a2.shape
    A=pl.BlockSpec(memory_space=ANY)
    sd=jax.ShapeDtypeStruct
    last=S0+N==S
    outs=[sd((T,D),BF),sd((T,D),F32),sd((T,D),BF),sd((D,T),BF),sd((1,D),F32),sd((2,D),F32)] if last else [sd((T,D),F32)]*2
    gs=pltpu.PrefetchScalarGridSpec(num_scalar_prefetch=2,grid=(N,),
        in_specs=[full((T,D)),full((T,D)),full((T,D)),full((1,D)),full((T,1))]+[A]*len(wps)+[full((T,D))]*len(carry),
        out_specs=[full(o.shape) for o in outs]+[A,A],
        scratch_shapes=([pltpu.VMEM((T,D),F32)]*2 if last else [])+[pltpu.VMEM((2,3,HC,D),BF),pltpu.VMEM((2,3,HC,D),BF)]+[pltpu.VMEM((HC,T),BF)]*3+[pltpu.SemaphoreType.DMA((2,)),pltpu.SemaphoreType.DMA((2,))])
    piece=sd((R//2,N,3,HC,SLAB),BF)
    return pl.pallas_call(functools.partial(mlp_kernel,T=T,D=D,HC=HC,R=R,metas=metas,S=S,SLAB=SLAB,TB=min(TB,T),S0=S0,N=N),grid_spec=gs,
        out_shape=outs+[piece,piece],
        cost_estimate=pl.CostEstimate(flops=1,transcendentals=0,bytes_accessed=1),name="mlp_both")(perm2,slots,a2,g,resid,gain,keep,*wps,*carry)

def bwd_attn_kernel(perm, dres, cos, sin, kseg, qseg, q_in, k_in, v_in, lse_in, *rest, T, KV, C, metas, S, SLAB, S0, N):
    wps = rest[:len(metas)]
    dq_out, dk_out, dv_out, W, bias, dob, dqs, dks, sem = rest[-9:]
    s=pl.program_id(0)
    slot=lax.rem(s,2)
    def fetch(step, sl):
        fetch_pieces(wps, metas, perm, S0+step, lambda src, blk: pltpu.make_async_copy(src.at[3], W.at[sl, pl.ds(pl.multiple_of(blk*SLAB,SLAB),SLAB), :], sem.at[sl]).start())
    @pl.when(s==0)
    def _():
        fetch(0,0)
        row=lax.broadcasted_iota(jnp.int32,(KV,T),0); col=lax.broadcasted_iota(jnp.int32,(KV,T),1)
        ok=(kseg[...]==qseg[...])|(row==col)
        bias[...]=jnp.where(ok,0.0,-1e30)
    @pl.when(s+1<N)
    def _(): fetch(s+1,1-slot)
    pltpu.make_async_copy(W.at[slot],W.at[slot],sem.at[slot]).wait()
    n=C//128
    dob[...]=dot(dres[...],W[slot],1,0).astype(BF)
    for p in range(n):
        kp=k_in[0,:,p*128:(p+1)*128]; vp=v_in[0,:,p*128:(p+1)*128]
        qp=q_in[0,:,p*128:(p+1)*128]; dp_=dob[:,p*128:(p+1)*128]
        half=lax.broadcasted_iota(jnp.int32,qp.shape,1)<64
        parts=[]
        dvs=None
        for h in range(2):
            mk=half if h==0 else ~half
            qm=jnp.where(mk,qp,jnp.zeros_like(qp)); dm=jnp.where(mk,dp_,jnp.zeros_like(dp_))
            pt=jnp.exp(dot(kp,qm,1,1)+bias[...]-lse_in[0,2*p+h:2*p+h+1,:])
            dpt=dot(vp,dm,1,1)
            delta=jnp.sum(pt*dpt,axis=0,keepdims=True)
            ds=(pt*(dpt-delta)).astype(BF)
            dv=dot(pt.astype(BF),dm,1,0); dk=dot(ds,qm,1,0)
            dqt=dot(kp,ds,0,0)
            parts.append(dqt[h*64:(h+1)*64])
            if h==0: dva,dka=dv,dk
            else: dva,dka=dva+dv,dka+dk
        dqs[:,p*128:(p+1)*128]=jnp.concatenate(parts,axis=0).T*(1.0/math.sqrt(HEAD_DIM))
        dks[:,p*128:(p+1)*128]=dka
        dv_out[0,:,p*128:(p+1)*128]=dva.astype(BF)
    cw=wide(cos[...],n); sw=wide(sin[...],n)
    dq_out[0]=turn(dqs[...],cw[:T],-sw[:T],lower_lanes(T,C)).astype(BF)
    dk_out[0]=turn(dks[...],cw,-sw,lower_lanes(KV,C)).astype(BF)

def bwd_attn(perm,dres,cos,sin,kseg,qseg,q,k,v,lse,pieces,S0=0,N=None,carry=()):
    wps,metas,S,SLAB,C=pieces
    T,D=dres.shape; KV=k.shape[1]; HG=C//HEAD_DIM
    N=S if N is None else N
    ib=lambda rows:pl.BlockSpec((1,rows,C),lambda s,p:(s+S0,0,0))
    gs=pltpu.PrefetchScalarGridSpec(num_scalar_prefetch=1,grid=(N,),
        in_specs=[full((T,D)),full((KV,128)),full((KV,128)),full((KV,1)),full((1,T)),ib(T),ib(KV),ib(KV),pl.BlockSpec((1,HG,T),lambda s,p:(s+S0,0,0))]+[pl.BlockSpec(memory_space=ANY)]*(len(wps)+len(carry)),
        out_specs=[ib(T),ib(KV),ib(KV)],
        scratch_shapes=[pltpu.VMEM((2,D,C),BF),pltpu.VMEM((KV,T),F32),pltpu.VMEM((T,C),BF),pltpu.VMEM((T,C),F32),pltpu.VMEM((KV,C),F32),pltpu.SemaphoreType.DMA((2,))])
    sd=jax.ShapeDtypeStruct
    fl=(2*T*D*C+10*T*KV*C)*N
    return pl.pallas_call(functools.partial(bwd_attn_kernel,T=T,KV=KV,C=C,metas=metas,S=S,SLAB=SLAB,S0=S0,N=N),grid_spec=gs,
        out_shape=[sd((S,T,C),BF),sd((S,KV,C),BF),sd((S,KV,C),BF)],
        input_output_aliases={10+len(wps)+i:i for i in range(len(carry))},
        cost_estimate=pl.CostEstimate(flops=1,transcendentals=0,bytes_accessed=1),name="attn_bwd")(perm,dres,cos,sin,kseg,qseg,q,k,v,lse,*wps,*carry)

def grad_attn_kernel(perm, slots, a1T, dresT, xhat, o_in, dq_in, dk_in, dv_in, *rest, T, KV, C, R, metas, S, SLAB):
    wps = rest[:len(metas)]
    da_own, da_far, gg_out, d0, d1, W, stg, acc, sem, osem = rest[len(metas):]
    s=pl.program_id(0)
    slot=lax.rem(s,2)
    def fetch(step, sl):
        fetch_pieces(wps, metas, perm, step, lambda src, blk: pltpu.make_async_copy(src.at[pl.ds(0,3)], W.at[sl, :, pl.ds(pl.multiple_of(blk*SLAB,SLAB),SLAB), :], sem.at[sl]).start())
    @pl.when(s==0)
    def _(): fetch(0,0)
    @pl.when(s+1<S)
    def _(): fetch(s+1,1-slot)
    @pl.when(s>=2)
    def _(): pltpu.make_async_copy(stg.at[slot],stg.at[slot],osem.at[slot]).wait()
    stg[slot,0]=dot(a1T[:,:T],dq_in[0],1,0).astype(BF)
    stg[slot,1]=dot(a1T[...],dk_in[0],1,0).astype(BF)
    stg[slot,2]=dot(a1T[...],dv_in[0],1,0).astype(BF)
    stg[slot,3]=dot(dresT[...],o_in[0],1,0).astype(BF)
    for r in range(R):
        dst=(d0,d1)[r%2]
        pltpu.make_async_copy(stg.at[slot,:,pl.ds(pl.multiple_of(perm[R+r]*SLAB,SLAB),SLAB),:], dst.at[r//2, slots[s]], osem.at[slot]).start()
    pltpu.make_async_copy(W.at[slot],W.at[slot],sem.at[slot]).wait()
    c=dot(dk_in[0],W[slot,1],1,1)+dot(dv_in[0],W[slot,2],1,1)
    cq=dot(dq_in[0],W[slot,0],1,1)
    @pl.when(s==0)
    def _():
        acc[...]=c
        acc[:T,:]=acc[:T,:]+cq
    @pl.when(s>0)
    def _():
        acc[...]=acc[...]+c
        acc[:T,:]=acc[:T,:]+cq
    @pl.when(s==S-1)
    def _():
        gg_out[...]=jnp.sum(acc[...]*xhat[...].astype(F32),axis=0,keepdims=True)
        da_own[...]=acc[:T,:]
        da_far[...]=acc[T:,:].astype(BF)
        for sl in range(min(S,2)):
            pltpu.make_async_copy(stg.at[sl],stg.at[sl],osem.at[sl]).wait()

def grad_attn(perm2,slots,a1T,dresT,xhat,o,dq,dk,dv,pieces):
    wps,metas,S,SLAB,C=pieces
    R=perm2.shape[0]//2
    D,T=dresT.shape; KV=dk.shape[1]
    A=pl.BlockSpec(memory_space=ANY)
    ib=lambda rows:pl.BlockSpec((1,rows,C),lambda s,p,q:(s,0,0))
    gs=pltpu.PrefetchScalarGridSpec(num_scalar_prefetch=2,grid=(S,),
        in_specs=[full((D,KV)),full((D,T)),full((KV,D)),ib(T),ib(T),ib(KV),ib(KV)]+[A]*len(wps),
        out_specs=[full((T,D)),full((KV-T,D)),full((1,D)),A,A],
        scratch_shapes=[pltpu.VMEM((2,3,D,C),BF),pltpu.VMEM((2,4,D,C),BF),pltpu.VMEM((KV,D),F32),pltpu.SemaphoreType.DMA((2,)),pltpu.SemaphoreType.DMA((2,))])
    sd=jax.ShapeDtypeStruct
    piece=sd((R//2,S,4,SLAB,C),BF)
    return pl.pallas_call(functools.partial(grad_attn_kernel,T=T,KV=KV,C=C,R=R,metas=metas,S=S,SLAB=SLAB),grid_spec=gs,
        out_shape=[sd((T,D),F32),sd((KV-T,D),BF),sd((1,D),F32),piece,piece],
        cost_estimate=pl.CostEstimate(flops=1,transcendentals=0,bytes_accessed=1),name="attn_grad")(perm2,slots,a1T,dresT,xhat,o,dq,dk,dv,*wps)

def split3(x):
    hi=x.astype(BF)
    return hi,(x-hi.astype(F32)).astype(BF)

def dot3(a,b,ca,cb):
    ah,al=a; bh,bl=b
    return dot(ah,bh,ca,cb)+(dot(ah,bl,ca,cb)+dot(al,bh,ca,cb))

def soap_kernel(sc, g_in, first, second, left, right, *rest, turned, each):
    f_out, s_out, u_out, n_out = rest[-4:]
    step,b1,b2=sc[0],sc[1],sc[2]
    for i in range(each):
        ql=split3(left[i]); qr=split3(right[i])
        if turned:
            x=dot3(split3(g_in[i]),ql,1,0)
            r=dot3(split3(x),qr,0,0).T
        else:
            x=dot3(ql,split3(g_in[i]),0,0)
            r=dot3(split3(x),qr,1,0)
        fn=b1*first[i]+(1.0-b1)*r
        sn=b2*second[i]+(1.0-b2)*r*r
        f_out[i]=fn; s_out[i]=sn
        n=fn/(jnp.sqrt(sn)+ADAM_EPS)
        if turned:
            t=dot3(split3(dot3(qr,split3(n),1,0)),ql,1,1)
        else:
            t=dot3(split3(dot3(ql,split3(n),1,0)),qr,1,1)
        size=n.shape[0]*n.shape[1]
        fac=jnp.sqrt(jnp.sum(n*n,keepdims=True)*(1.0/size))*lax.rsqrt(jnp.sum(t*t,keepdims=True)*(1.0/size)+SCALE_EPS)
        u_out[i]=(-step*fac)*t
        n_out[i]=jnp.broadcast_to(fac,(8,128))

def soap(scalars,g,first,second,left,right,turned,each=1,K0=0,N=None,carry=()):
    K=first.shape[0]
    N=K if N is None else N
    b=lambda x:pl.BlockSpec((each,)+x.shape[1:],lambda k,s:(k+K0,0,0))
    sd=jax.ShapeDtypeStruct
    o=sd(first.shape,F32)
    outs=[o,o,o,sd((K,8,128),F32)]
    gs=pltpu.PrefetchScalarGridSpec(num_scalar_prefetch=1,grid=(N//each,),
        in_specs=[b(x) for x in (g,first,second,left,right)]+[pl.BlockSpec(memory_space=ANY)]*len(carry),out_specs=[b(x) for x in outs])
    return pl.pallas_call(functools.partial(soap_kernel,turned=turned,each=each),grid_spec=gs,out_shape=outs,
        input_output_aliases={6+i:i for i in range(len(carry))},
        cost_estimate=pl.CostEstimate(flops=1,transcendentals=0,bytes_accessed=1),
        name="soap_"+("mlp" if turned else "attn"))(scalars,g,first,second,left,right,*carry)

def norm_kernel(own, far, gain, a1, a1T, xh, *, T):
    for lo,ref in ((0,own),(T,far)):
        v=ref[...].astype(F32)
        ce=v-jnp.mean(v,axis=1,keepdims=True)
        x=ce*lax.rsqrt(jnp.mean(ce*ce,axis=1,keepdims=True)+NORM_EPS)
        n=ref.shape[0]
        xh[lo:lo+n,:]=x.astype(BF)
        y=x*gain[...]
        a1[lo:lo+n,:]=y.astype(BF)
        a1T[:,lo:lo+n]=y.T.astype(BF)

def norm_first(own,far,gain):
    T,D=own.shape; KV=T+far.shape[0]
    sd=jax.ShapeDtypeStruct
    outs=[sd((KV,D),BF),sd((D,KV),BF),sd((KV,D),BF)]
    return pl.pallas_call(functools.partial(norm_kernel,T=T),grid=(1,),in_specs=[full(x.shape) for x in (own,far,gain)],
        out_specs=[full(o.shape) for o in outs],out_shape=outs,
        cost_estimate=pl.CostEstimate(flops=1,transcendentals=0,bytes_accessed=1),name="norm_first")(own,far,gain)

def input_kernel(hid, da, dres, gain, *rest):
    out=rest[-1]
    v=hid[...].astype(F32)
    ce=v-jnp.mean(v,axis=1,keepdims=True)
    rstd=lax.rsqrt(jnp.mean(ce*ce,axis=1,keepdims=True)+NORM_EPS)
    x=ce*rstd
    d=da[...]
    for r in rest[:-1]:
        d=d+r[...].astype(F32)
    e=d*gain[...]
    out[...]=(dres[...]+rstd*(e-jnp.mean(e,axis=1,keepdims=True)-x*jnp.mean(e*x,axis=1,keepdims=True))).astype(BF)

def input_back(hid,da,dres,gain,*back):
    args=(hid,da,dres,gain)+back
    return pl.pallas_call(input_kernel,grid=(1,),in_specs=[full(x.shape) for x in args],out_specs=full(hid.shape),
        out_shape=jax.ShapeDtypeStruct(hid.shape,BF),
        cost_estimate=pl.CostEstimate(flops=1,transcendentals=0,bytes_accessed=1),name="input_back")(*args)


def ring_order(count):
    return list(range(0, count, 2)) + list(range(1, count, 2))[::-1]


def swap_dp(value, bit, owners):
    return lax.ppermute(value, "dp", [(i, i ^ bit) for i in range(owners)])


def to_ring_pred(value, shards):
    ring = ring_order(shards)
    return lax.ppermute(
        value, "tensor", [(ring[p], ring[(p - 1) % shards]) for p in range(shards)]
    )


def to_ring_succ(value, shards):
    ring = ring_order(shards)
    return lax.ppermute(
        value, "tensor", [(ring[p], ring[(p + 1) % shards]) for p in range(shards)]
    )


def along_line(value, steps, shards):
    ring = ring_order(shards)
    return lax.ppermute(
        value, "tensor", [(ring[p], ring[(p + steps) % shards]) for p in range(shards)]
    )


def add_low(one, two):
    return (one.astype(F32) + two.astype(F32)).astype(BF)


def halve(pieces, bits, owners):
    for bit in bits:
        live = sorted(bits[bits.index(bit):], reverse=True)
        axis = live.index(bit)
        send = lax.index_in_dim(pieces, 1, axis, keepdims=False)
        keep = lax.index_in_dim(pieces, 0, axis, keepdims=False)
        pieces = add_low(keep, swap_dp(send, bit, owners))
    return pieces


def reduce_pieces(even, odd, cut, owners, shards):
    mine = add_low(even, swap_dp(odd, 1, owners))
    bits = [1 << b for b in range(1, owners.bit_length() - 1)]
    mine = mine.reshape((2,) * len(bits) + mine.shape[1:])
    low = halve(mine[..., :cut, :], bits[::-1], owners)
    high = halve(mine[..., cut:, :], bits, owners)
    both = jnp.concatenate([low, high], axis=-2)
    moving = both[shards - 1]
    for left in range(shards - 2, -1, -1):
        moving = to_ring_pred(moving, shards)
        moving = moving.astype(F32) + both[left].astype(F32)
        if left:
            moving = moving.astype(BF)
    return moving


def all_sum(value, owners, shards):
    for axis, count in (("dp", owners), ("tensor", shards)):
        step = 1
        while step < count:
            value = value + lax.ppermute(value, axis, [(i, i ^ step) for i in range(count)])
            step *= 2
    return value


def after(value, *earlier):
    return lax.optimization_barrier((value,) + earlier)[0]


def add_all(*values):
    total = values[0].astype(F32)
    for value in values[1:]:
        total = total + value.astype(F32)
    return total


def gather_stack(stacked, owners):
    half = stacked.shape[0] // 2
    by_x, by_y = swap_dp(stacked, 2, owners), swap_dp(stacked, 4, owners)
    return by_x, by_y, swap_dp(by_x[:half], 4, owners), swap_dp(by_y[half:], 2, owners)


def to_core(arrays, owners):
    return [swap_dp(a, 1, owners) for a in arrays]


def with_partner(arrays, metas, owners):
    return arrays + [swap_dp(a, 1, owners) for a in arrays], metas + tuple((m[0] + 1,) + m[1:] for m in metas)


def cross_sends(even, core, half):
    low = add_all(even[3, :half], core[3, :half]).astype(BF)
    high = add_all(even[3, half:], core[3, half:]).astype(BF)
    return low, high


def side_sends(even, core, from_y, from_x, half):
    to_x = jnp.concatenate(
        [add_all(even[1, :half], core[1, :half], from_y), add_all(even[1, half:], core[1, half:])]
    ).astype(BF)
    to_y = jnp.concatenate(
        [add_all(even[2, :half], core[2, :half]), add_all(even[2, half:], core[2, half:], from_x)]
    ).astype(BF)
    return to_x, to_y


def own_part(even, core, from_x, from_y, slot):
    return add_all(even[0, slot], core[0, slot], from_x[slot], from_y[slot])


def ring_sum(even, core, from_x, from_y, shards):
    moving = None
    for slot in list(range(1, shards)) + [0]:
        part = own_part(even, core, from_x, from_y, slot)
        if moving is not None:
            part = part + to_ring_succ(moving, shards).astype(F32)
        moving = part.astype(BF)
    return part


def per_device(
    hidden_in, out_grad, attn_weight, mlp_weight, norm_gain,
    attn_first, attn_second, attn_left, attn_right,
    mlp_first, mlp_second, mlp_left, mlp_right,
    gain_first, gain_second, owner_rows, segment_ids, positions, valid,
    step, learn_rate, beta_first, beta_second,
):
    owners = lax.axis_size("dp")
    shards = lax.axis_size("tensor")
    dp_index = lax.axis_index("dp")
    place = lax.axis_index("tensor")
    rows, width = hidden_in.shape
    slab = attn_weight.shape[1]
    hid_cols = mlp_weight.shape[2]
    span = SEQ_LEN // rows
    within = place % span
    base = place - within
    half = shards // 2
    gain_rows = norm_gain.astype(F32)

    def from_peer(value, ahead):
        pairs = [(g + (w + ahead) % span, g + w) for g in range(0, shards, span) for w in range(span)]
        return lax.ppermute(value, "tensor", pairs)

    def sequence_rows(column):
        return jnp.concatenate(
            [lax.dynamic_slice_in_dim(column, (base + (within + d) % span) * rows, rows, 0) for d in range(span)]
        )

    joined = 128 // slab if slab < 128 else 1
    fast = owners == 8 and joined == 1 and shards == 4 and span == 2
    both = ("dp", "tensor")
    mlp_turned = jnp.swapaxes(mlp_weight, 1, 2)
    if not fast:
        attn_all = lax.all_gather(attn_weight, both, axis=0, tiled=False).reshape((owners, shards) + attn_weight.shape)
        mlp_all = lax.all_gather(mlp_turned, both, axis=0, tiled=False).reshape((owners, shards) + mlp_turned.shape)

    slot_ids = jnp.arange(owners, dtype=jnp.int32)
    rel_owner = jnp.sum(
        jnp.where((slot_ids[:, None] ^ dp_index) == slot_ids[None, :], owner_rows[None, :], 0), axis=1
    )
    ring = ring_order(shards)
    ring_place = jnp.array([ring.index(z) for z in range(shards)], jnp.int32)
    my_place = jnp.sum(jnp.where(jnp.arange(shards) == place, ring_place, 0))
    slots = (my_place - ring_place) % shards
    attn_perm = jnp.concatenate([rel_owner if fast else owner_rows, rel_owner]).astype(jnp.int32)
    if fast:
        slots = jnp.arange(shards, dtype=jnp.int32)
    if joined == 1:
        mlp_perm = attn_perm
    else:
        inverse = jnp.sum(jnp.where(owner_rows[None, :] == slot_ids[:, None], slot_ids[None, :], 0), axis=1)
        mlp_all = jnp.take(mlp_all, inverse, axis=0).reshape((owners // joined, joined) + mlp_all.shape[1:])
        mlp_all = jnp.moveaxis(mlp_all, 1, 4)
        mlp_all = mlp_all.reshape(mlp_all.shape[:4] + (joined * slab,))
        blocks = jnp.arange(owners // joined, dtype=jnp.int32)
        mlp_perm = jnp.concatenate([blocks, blocks])

    seg = sequence_rows(segment_ids)
    keep_seq = sequence_rows(valid)
    pos = sequence_rows(positions)
    half_dim = HEAD_DIM // 2
    frequency = jnp.exp(jnp.arange(half_dim, dtype=F32) * (-2.0 * math.log(ROPE_BASE) / HEAD_DIM))
    angles = pos.astype(F32)[:, None] * frequency[None, :]
    cos_half, sin_half = jnp.cos(angles), jnp.sin(angles)
    cos_table = jnp.concatenate([cos_half] * 4, axis=1)
    sin_table = jnp.concatenate([-sin_half, sin_half] * 2, axis=1)
    key_seg = jnp.where(keep_seq > 0, seg, -1)[:, None]
    query_seg = seg[None, :rows]
    keep_own = keep_seq[:rows].astype(F32)[:, None]

    first_gain, second_gain = gain_rows[0:1], gain_rows[1:2]
    if fast:
        together = lax.optimization_barrier
        mlp_x, mlp_y, mlp_z = [None] * 4, [None] * 4, [None] * 4
        line_1 = along_line(attn_weight, 1, shards)
        mlp_x[0], mlp_y[0] = swap_dp(mlp_turned, 2, owners), swap_dp(mlp_turned, 4, owners)
        tables = (cos_table, sin_table, key_seg, query_seg, keep_own, attn_perm, mlp_perm, slots, first_gain, second_gain)
        line_1, mlp_x[0], mlp_y[0] = together((line_1, mlp_x[0], mlp_y[0]))
        pair_a = jnp.stack([attn_weight, line_1])
        x_a, y_a = swap_dp(pair_a, 2, owners), swap_dp(pair_a, 4, owners)
        far_rows = from_peer(after(hidden_in, line_1), 1)
        core_0 = to_core([after(a, line_1) for a in (mlp_turned, mlp_x[0])], owners)
        x_a, y_a, core_0, tables = together((x_a, y_a, core_0, tables))
        cos_table, sin_table, key_seg, query_seg, keep_own, attn_perm, mlp_perm, slots, first_gain, second_gain = tables
        z_a, mlp_z[0] = swap_dp(x_a, 4, owners), swap_dp(after(mlp_y[0], y_a), 2, owners)
        line_2, line_3 = along_line(after(line_1, x_a), 1, shards), along_line(after(attn_weight, x_a), 3, shards)
        normal = norm_first(hidden_in, far_rows, first_gain)
        z_a, mlp_z[0], normal, line_2, line_3 = together((z_a, mlp_z[0], tuple(normal), line_2, line_3))
        pair_b = jnp.stack([line_2, line_3])
        x_b, y_b = swap_dp(pair_b, 2, owners), swap_dp(pair_b, 4, owners)
        mlp_line = [mlp_turned, along_line(after(mlp_turned, line_3), 1, shards), None, None]
        core_a4 = to_core([after(a, z_a) for a in (pair_a, x_a, y_a, z_a)], owners)
        core_b = [swap_dp(after(pair_b, core_a4[1]), 1, owners)]
        core_0 = core_0 + to_core([after(a, core_b[0]) for a in (mlp_y[0], mlp_z[0])], owners)
        normal, core_a4, mlp_line[1], core_b, x_b, y_b, core_0 = together(
            (tuple(normal), core_a4, mlp_line[1], core_b, x_b, y_b, core_0)
        )
        z_b = swap_dp(y_b, 2, owners)
        mlp_x[1], mlp_y[1] = swap_dp(mlp_line[1], 2, owners), swap_dp(mlp_line[1], 4, owners)
        mlp_line[3] = along_line(after(mlp_turned, mlp_line[1]), 3, shards)
        mlp_line[2] = along_line(mlp_line[1], 1, shards)
        first_norm, first_turned, xhat_low = normal

        def attn_set(arrays, first):
            return arrays, tuple((r, first, 2, shards) for r in (0, 2, 4, 6, 1, 3, 5, 7))

        sizes = (shards, slab, attn_weight.shape[2])
        arrays_a, metas_a = attn_set([pair_a, x_a, y_a, z_a, *core_a4], 0)
        attn_part_a = (arrays_a, metas_a, *sizes)
    else:
        far_rows = [from_peer(hidden_in, d) for d in range(1, span)]
        attn_pieces = ([attn_all], (None,), shards, slab, attn_weight.shape[2])
        first_norm, first_turned, xhat_low = norm_first(hidden_in, jnp.concatenate(far_rows), first_gain)
    back_args = (cos_table, sin_table, key_seg, query_seg)
    fwd_args = (attn_perm, first_norm, hidden_in, second_gain, cos_table, sin_table, key_seg, query_seg, keep_own)
    if fast:
        carry = fwd_attn(*fwd_args, attn_part_a, S0=0, N=half)
        z_b, mlp_x[1], mlp_y[1], mlp_line[3], mlp_line[2], carry = together(
            (z_b, mlp_x[1], mlp_y[1], mlp_line[3], mlp_line[2], tuple(carry))
        )
        core_b = core_b + to_core([after(x_b, z_b), after(y_b, z_b)], owners)
        core_z_b = swap_dp(z_b, 1, owners)
        core_b, core_z_b, mlp_x[1], mlp_y[1], mlp_line[3], mlp_line[2] = together((core_b, core_z_b, mlp_x[1], mlp_y[1], mlp_line[3], mlp_line[2]))
        mlp_z[1] = swap_dp(mlp_y[1], 2, owners)
        mlp_y[2] = swap_dp(mlp_line[2], 4, owners)
        arrays_b, metas_b = attn_set([pair_b, x_b, y_b, z_b, *core_b, core_z_b], 2)
        attn_part_b = (arrays_b, metas_b, *sizes)
        attn_pieces = (arrays_a + arrays_b, metas_a + metas_b, *sizes)
        mlp_x[3], mlp_y[3] = swap_dp(mlp_line[3], 2, owners), swap_dp(mlp_line[3], 4, owners)
        out = fwd_attn(*fwd_args, attn_part_b, S0=half, N=half, carry=carry)
        mlp_x[3], mlp_y[3], mlp_z[1], mlp_y[2], out = together((mlp_x[3], mlp_y[3], mlp_z[1], mlp_y[2], tuple(out)))
        queries, keys, values, attended, log_sums, resid, second_norm, stat_a = out

        def mlp_set(slot):
            return [mlp_line[slot], mlp_x[slot], mlp_y[slot], mlp_z[slot]]

        def mlp_pieces(*slots_of):
            arrays, metas = [], []
            for slot, got in slots_of:
                arrays += [a[None] for a in got]
                metas += [(r, slot, 1, shards) for r in (0, 2, 4, 6, 1, 3, 5, 7)]
            return arrays, tuple(metas), shards, slab, hid_cols

        set_0, set_1 = mlp_set(0), mlp_set(1)
        core_1 = to_core([after(a, mlp_z[1]) for a in set_1], owners)
        core_1, second_norm, mlp_x[3], mlp_y[2] = together((core_1, second_norm, mlp_x[3], mlp_y[2]))
        mlp_z[3], mlp_z[2] = swap_dp(mlp_x[3], 4, owners), swap_dp(mlp_y[2], 2, owners)
        mlp_x[2] = swap_dp(after(mlp_line[2], second_norm), 2, owners)
        core_3 = to_core([mlp_line[3], mlp_x[3]], owners)
        mlp_args = (mlp_perm, slots, second_norm, out_grad, resid, second_gain, keep_own)
        out = mlp(*mlp_args, mlp_pieces((0, set_0 + core_0), (1, set_1 + core_1)), S0=0, N=half)
        mlp_x[2], mlp_z[2], mlp_z[3], core_3, out = together((mlp_x[2], mlp_z[2], mlp_z[3], core_3, tuple(out)))
        *carry, even_a, odd_a = out
        set_2, set_3 = mlp_set(2), mlp_set(3)
        core_2 = to_core([after(a, odd_a) for a in set_2], owners)
        core_3 = core_3 + to_core([after(a, odd_a) for a in set_3[2:]], owners)
        core_2, core_3, carry = together((core_2, core_3, carry))
        core_a = swap_dp(after(odd_a, core_2[3]), 1, owners)
        out = mlp(*mlp_args, mlp_pieces((2, set_2 + core_2), (3, set_3 + core_3)), S0=half, N=half, carry=carry)
        core_a, out = together((core_a, tuple(out)))
        output, dresid, dres_low, dres_turned, gain_two, stat_m, even_b, odd_b = out
        low, high = cross_sends(even_a, core_a, 1)
        low, high, dres_low = together((low, high, dres_low))
        from_y, from_x = swap_dp(low, 4, owners), swap_dp(high, 2, owners)
        core_b2 = swap_dp(odd_b, 1, owners)
        fwd_kept = (queries, keys, values, log_sums, attn_pieces)
        grads = bwd_attn(attn_perm, dres_low, *back_args, *fwd_kept, S0=0, N=half)
        from_y, from_x, core_b2, *grads = together((from_y, from_x, core_b2, *grads))
        low, high = cross_sends(even_b, core_b2, 1)
        to_x, to_y = side_sends(even_a, core_a, from_y, from_x, 1)
        low, high, to_x, to_y, dres_low = together((low, high, to_x, to_y, dres_low))
        from_y, from_x = swap_dp(low, 4, owners), swap_dp(high, 2, owners)
        back_x, back_y = swap_dp(to_x, 2, owners), swap_dp(to_y, 4, owners)
        grads = bwd_attn(attn_perm, dres_low, *back_args, *fwd_kept, S0=half, N=half, carry=tuple(grads))
        from_y, from_x, *grads = together((from_y, from_x, *grads))
        to_x, to_y = side_sends(even_b, core_b2, from_y, from_x, 1)
        to_x, to_y, back_x, back_y = together((to_x, to_y, back_x, back_y))
        from_x, from_y = swap_dp(to_x, 2, owners), swap_dp(to_y, 4, owners)
        ring_1 = own_part(even_a, core_a, back_x, back_y, 1).astype(BF)
        ring_1, dres_turned = together((ring_1, dres_turned))
        ring_1 = to_ring_succ(ring_1, shards)
        out = grad_attn(attn_perm, slots, first_turned, dres_turned, xhat_low, attended, *grads, attn_pieces)
        from_x, from_y, ring_1, *out = lax.optimization_barrier((from_x, from_y, ring_1, *out))
        da_own, da_far, gain_one, attn_even, attn_odd = out
    else:
        queries, keys, values, attended, log_sums, resid, second_norm, stat_a = fwd_attn(*fwd_args, attn_pieces)
        output, dresid, dres_low, dres_turned, gain_two, stat_m, mlp_even, mlp_odd = mlp(
            mlp_perm, slots, second_norm, out_grad, resid, second_gain, keep_own,
            ([mlp_all], (None,), shards, mlp_all.shape[-1], hid_cols),
        )
        if joined > 1:
            merged = jnp.stack([mlp_even, mlp_odd], axis=1).reshape((owners // joined,) + mlp_even.shape[1:])
            merged = merged.reshape(merged.shape[:-1] + (joined, slab))
            merged = jnp.moveaxis(merged, -2, 1).reshape((owners,) + mlp_even.shape[1:-1] + (slab,))
            merged = jnp.take(merged, rel_owner, axis=0)
            mlp_even, mlp_odd = merged[0::2], merged[1::2]
        mlp_sum = reduce_pieces(mlp_even, mlp_odd, -(-hid_cols // 32) * 16, owners, shards)
        grads = bwd_attn(attn_perm, dres_low, *back_args, queries, keys, values, log_sums, attn_pieces)
        da_own, da_far, gain_one, attn_even, attn_odd = grad_attn(
            attn_perm, slots, first_turned, dres_turned, xhat_low, attended, *grads, attn_pieces
        )
    def send_back(da_far):
        got = []
        for d in range(1, span):
            pairs = [(g + w, g + (w + d) % span) for g in range(0, shards, span) for w in range(span)]
            got.append(lax.ppermute(da_far[(d - 1) * rows : d * rows], "tensor", pairs))
        return got

    def swap_line(value, bit):
        return lax.ppermute(value, "tensor", [(i, i ^ bit) for i in range(shards)])

    def finish_input(da_back):
        return input_back(hidden_in, da_own, dresid, first_gain, *da_back)

    step_count = step.astype(F32)
    step_size = (
        learn_rate
        * jnp.sqrt(1.0 - jnp.power(beta_second, step_count))
        / (1.0 - jnp.power(beta_first, step_count))
    )
    scalars = jnp.stack([step_size, beta_first, beta_second])

    def flip(value):
        return jnp.swapaxes(value, 1, 2)

    def soap_mlp(total, *part):
        return soap(scalars, total, flip(mlp_first), flip(mlp_second), mlp_left, mlp_right, True, *part)

    sums = jnp.concatenate([jnp.sum(stat_a, axis=1), jnp.sum(stat_m, axis=1), jnp.sum(keep_own)[None]])
    small = jnp.concatenate([gain_one, gain_two, jnp.pad(sums, (0, width - 5))[None]], axis=0)
    if fast:
        attn_core = swap_dp(attn_odd, 1, owners)
        ring_2 = (own_part(even_b, core_b2, from_x, from_y, 0) + ring_1.astype(F32)).astype(BF)
        ring_2 = to_ring_succ(ring_2, shards)
        small = small + swap_dp(small, 1, owners)
        small, attn_core = lax.optimization_barrier((small, attn_core))
        low, high = cross_sends(attn_even, attn_core, half)
        low, high, small = lax.optimization_barrier((low, high, small))
        cross_y, cross_x = swap_dp(low, 4, owners), swap_dp(high, 2, owners)
        small = small + swap_dp(small, 2, owners)
        ring_3 = (own_part(even_b, core_b2, from_x, from_y, 1) + ring_2.astype(F32)).astype(BF)
        ring_3 = to_ring_succ(ring_3, shards)
        small, cross_x, cross_y = lax.optimization_barrier((small, cross_x, cross_y))
        to_x, to_y = side_sends(attn_even, attn_core, cross_y, cross_x, half)
        to_x, to_y, small = lax.optimization_barrier((to_x, to_y, small))
        attn_x, attn_y = swap_dp(to_x, 2, owners), swap_dp(to_y, 4, owners)
        small = small + swap_dp(small, 4, owners)
        da_back = send_back(after(da_far, ring_3))
        mlp_sum = own_part(even_a, core_a, back_x, back_y, 0) + ring_3.astype(F32)
        mlp_new = soap_mlp(mlp_sum)
        attn_x, attn_y, mlp_sum, mlp_new = lax.optimization_barrier((attn_x, attn_y, mlp_sum, tuple(mlp_new)))
        moving = own_part(attn_even, attn_core, attn_x, attn_y, 1).astype(BF)
        for slot in range(1, shards):
            moving, small, da_back = lax.optimization_barrier((moving, small, da_back))
            moving = to_ring_succ(moving, shards)
            if slot < 3:
                small = small + swap_line(small, slot)
            if slot == 1:
                input_grad = finish_input(da_back)
                moving, input_grad = lax.optimization_barrier((moving, input_grad))
            moving, small = lax.optimization_barrier((moving, small))
            moving = moving.astype(F32) + own_part(attn_even, attn_core, attn_x, attn_y, (slot + 1) % shards)
            if slot + 1 < shards:
                moving = moving.astype(BF)
        attn_sum = moving
    else:
        attn_sum = reduce_pieces(attn_even, attn_odd, slab // 2, owners, shards)
        small = all_sum(small, owners, shards)
        mlp_new = soap_mlp(mlp_sum)
        input_grad = finish_input(send_back(da_far))
    gain_grad = small[:2]
    stat_sums = small[2]

    attn_grad = attn_sum
    attn_first_new, attn_second_new, attn_update, attn_scale = soap(
        scalars, attn_sum, attn_first, attn_second, attn_left, attn_right, False, 2
    )
    mlp_grad, mlp_first_new, mlp_second_new, mlp_update = (flip(v) for v in (mlp_sum, *mlp_new[:3]))
    mlp_scale = mlp_new[3]
    gain_first_new = beta_first * gain_first + (1.0 - beta_first) * gain_grad
    gain_second_new = beta_second * gain_second + (1.0 - beta_second) * gain_grad * gain_grad
    gain_update = -step_size * gain_first_new / (jnp.sqrt(gain_second_new) + ADAM_EPS)
    root_means = jnp.sqrt(stat_sums[:4] / (stat_sums[4] * width))
    norm_scale = jnp.concatenate([attn_scale[:, :1, :1], mlp_scale[:, :1, :1]], axis=0)
    return (
        output, input_grad, attn_grad, mlp_grad, gain_grad,
        attn_first_new, attn_second_new, mlp_first_new, mlp_second_new,
        gain_first_new, gain_second_new, attn_update, mlp_update, gain_update,
        norm_scale, root_means,
    )


def solution(mesh):
    rows = P(("dp", "tensor"), None)
    block = P(None, "dp", "tensor")
    return jax.shard_map(
        per_device,
        mesh=mesh,
        in_specs=(rows, rows, block, block, P()) + (block,) * 8 + (P(),) * 3 + (P("dp"),) * 3 + (P(),) * 4,
        out_specs=(rows, rows, block, block, P(), block, block, block, block, P(), P(), block, block, P(), block, P()),
        check_vma=False,
    )
```

```python
import functools
import math

import jax
import jax.numpy as jnp
from jax import lax
from jax.experimental import pallas as pl
from jax.experimental.pallas import tpu as pltpu
from jax.sharding import PartitionSpec as P

HEAD_DIM = 64
SEQ_LEN = 1024
NORM_EPS = 1e-05
ROPE_BASE = 160000.0
ADAM_EPS = 1e-08
SCALE_EPS = 1e-06
PRECISE = lax.Precision.HIGHEST
BF = jnp.bfloat16
F32 = jnp.float32
ANY = pl.ANY


def dot(a,b,ca,cb):
    return lax.dot_general(a,b,(((ca,),(cb,)),((),())),preferred_element_type=F32)

def turn(x, cos, sin, lower):
    w=x.shape[1]
    sw=jnp.where(lower, pltpu.roll(x, w-32, 1), pltpu.roll(x, 32, 1))
    return x*cos+sw*sin

def lower_lanes(rows, cols):
    return lax.broadcasted_iota(jnp.int32,(rows,cols),1)%64<32

def wide(t, n):
    return t if n==1 else jnp.concatenate([t]*n,axis=1)

def fetch_pieces(refs, metas, perm, step, copy):
    for ref, meta in zip(refs, metas):
        if meta is None:
            for r in range(ref.shape[0]):
                copy(ref.at[r, step], perm[r])
        else:
            r, first, count, total = meta
            if count == total:
                copy(ref.at[step], perm[r])
            else:
                @pl.when((step >= first) & (step < first + count))
                def _(ref=ref, r=r, first=first):
                    copy(ref.at[jnp.clip(step - first, 0, ref.shape[0] - 1)], perm[r])

def fwd_attn_kernel(perm, a1, hid, gain, cos, sin, kseg, qseg, keep, *rest, T, KV, C, metas, S, SLAB, QB, S0, N):
    wps = rest[:len(metas)]
    rest = rest[len(metas):]
    if S0:
        acc_in, rest = rest[0], rest[6:]
    q_out, k_out, v_out, o_out, lse_out = rest[:5]
    if S0+N==S:
        resid_out, a2_out, stat_out, acc = rest[5:9]
    else:
        acc = rest[5]
    W, bias, osc, sem = rest[-4:]
    s=pl.program_id(0)
    def fetch(step, slot):
        fetch_pieces(wps, metas, perm, S0+step, lambda src, blk: pltpu.make_async_copy(src, W.at[slot, :, pl.ds(pl.multiple_of(blk*SLAB,SLAB),SLAB), :], sem.at[slot]).start())
    slot=lax.rem(s,2)
    @pl.when(s==0)
    def _():
        fetch(0,0)
        row=lax.broadcasted_iota(jnp.int32,(KV,T),0); col=lax.broadcasted_iota(jnp.int32,(KV,T),1)
        ok=(kseg[...]==qseg[...])|(row==col)
        bias[...]=jnp.where(ok,0.0,-1e30)
        acc[...]=acc_in[...] if S0 else jnp.zeros_like(acc)
    @pl.when(s+1<N)
    def _(): fetch(s+1,1-slot)
    pltpu.make_async_copy(W.at[slot],W.at[slot],sem.at[slot]).wait()
    n=C//128
    low_q=lower_lanes(T,C); low_k=lower_lanes(KV,C)
    cw=wide(cos[...],n); sw=wide(sin[...],n)
    q=dot(a1[:T,:],W[slot,0],1,0)
    q_out[0]=(turn(q,cw[:T],sw[:T],low_q).astype(BF)*BF(1/math.sqrt(HEAD_DIM))).astype(BF)
    k=dot(a1[...],W[slot,1],1,0)
    k_out[0]=turn(k,cw,sw,low_k).astype(BF)
    v_out[0]=dot(a1[...],W[slot,2],1,0).astype(BF)
    for p in range(n):
        kp=k_out[0,:,p*128:(p+1)*128]; vp=v_out[0,:,p*128:(p+1)*128]
        for b in range(T//QB):
            qp=q_out[0,b*QB:(b+1)*QB,p*128:(p+1)*128]
            half=lax.broadcasted_iota(jnp.int32,qp.shape,1)<64
            parts=[]
            for h in range(2):
                qm=jnp.where(half if h==0 else ~half,qp,jnp.zeros_like(qp))
                st=dot(kp,qm,1,1)+bias[:,b*QB:(b+1)*QB]
                m=jnp.max(st,axis=0,keepdims=True)
                e=jnp.exp(st-m)
                l=jnp.sum(e,axis=0,keepdims=True)
                ot=dot(vp,e.astype(BF),0,0)
                parts.append(ot[h*64:(h+1)*64]*(1.0/l))
                lse_out[0,pl.ds(2*p+h,1),b*QB:(b+1)*QB]=m+jnp.log(l)
            op=jnp.concatenate(parts,axis=0)
            osc[b*QB:(b+1)*QB,p*128:(p+1)*128]=op.T.astype(BF)
    o_out[0]=osc[...]
    acc[...]+=dot(osc[...],W[slot,3],1,1)
    if S0+N<S:
        return
    @pl.when(s==N-1)
    def _():
        at=acc[...]
        rs=hid[...].astype(F32)+at
        resid_out[...]=rs
        mu=jnp.mean(rs,axis=1,keepdims=True); ce=rs-mu
        var=jnp.mean(ce*ce,axis=1,keepdims=True)
        a2_out[...]=(ce*lax.rsqrt(var+NORM_EPS)*gain[...]).astype(BF)
        kp=keep[...]
        s1=jnp.sum(kp*at*at,axis=0,keepdims=True); s2=jnp.sum(kp*rs*rs,axis=0,keepdims=True)
        stat_out[...]=jnp.concatenate([s1,s2],axis=0)

def full(shape):
    nd=len(shape)
    return pl.BlockSpec(shape,lambda *a:(0,)*nd)

def fwd_attn(perm,a1,hid,gain,cos,sin,kseg,qseg,keep,pieces,S0=0,N=None,carry=(),QB=512):
    wps,metas,S,SLAB,C=pieces
    N=S if N is None else N
    KV,D=a1.shape; T=hid.shape[0]; HG=C//HEAD_DIM
    A=pl.BlockSpec(memory_space=ANY)
    sb=lambda rows:pl.BlockSpec((1,rows,C),lambda s,p:(s+S0,0,0))
    sd=jax.ShapeDtypeStruct
    last=S0+N==S
    tail=[sd((T,D),F32),sd((T,D),BF),sd((2,D),F32)] if last else [sd((T,D),F32)]
    gs=pltpu.PrefetchScalarGridSpec(num_scalar_prefetch=1,grid=(N,),
        in_specs=[full((KV,D)),full((T,D)),full((1,D)),full((KV,128)),full((KV,128)),full((KV,1)),full((1,T)),full((T,1))]+[A]*len(wps)+([full((T,D))]+[A]*5 if S0 else []),
        out_specs=[sb(T),sb(KV),sb(KV),sb(T),pl.BlockSpec((1,HG,T),lambda s,p:(s+S0,0,0))]+[full(t.shape) for t in tail],
        scratch_shapes=([pltpu.VMEM((T,D),F32)] if last else [])+[pltpu.VMEM((2,4,D,C),BF),pltpu.VMEM((KV,T),F32),pltpu.VMEM((T,C),BF),pltpu.SemaphoreType.DMA((2,))])
    return pl.pallas_call(functools.partial(fwd_attn_kernel,T=T,KV=KV,C=C,metas=metas,S=S,SLAB=SLAB,QB=min(QB,T),S0=S0,N=N),grid_spec=gs,
        out_shape=[sd((S,T,C),BF),sd((S,KV,C),BF),sd((S,KV,C),BF),sd((S,T,C),BF),sd((S,HG,T),F32)]+tail,
        input_output_aliases={10+len(wps)+i:i for i in range(5)} if S0 else {},
        cost_estimate=pl.CostEstimate(flops=1,transcendentals=0,bytes_accessed=1),name="attn_fwd")(perm,a1,hid,gain,cos,sin,kseg,qseg,keep,*wps,*((carry[5],)+tuple(carry[:5]) if S0 else ()))

def gelu_parts(x):
    phi=0.5*(1.0+lax.erf(x*(1.0/math.sqrt(2.0))))
    den=jnp.exp(-0.5*x*x)*(1.0/math.sqrt(2.0*math.pi))
    return phi,den

def mlp_kernel(perm, slots, a2, g, resid, gain, keep, *rest, T, D, HC, R, metas, S, SLAB, TB, S0, N):
    wps = rest[:len(metas)]
    rest = rest[len(metas):]
    if S0:
        y_in, da_in = rest[:2]
        rest = rest[2:]
    if S0+N==S:
        out, dres_out, dresb_out, dresT_out, gg_out, stat_out = rest[:6]
        rest = rest[6:]
        d0, d1, y, da = rest[:4]
    else:
        y, da, d0, d1 = rest[:4]
    W, stg, hT, dgT, duT, sem, osem = rest[4:]
    s=pl.program_id(0)
    slot=lax.rem(s,2)
    def fetch(step, sl):
        fetch_pieces(wps, metas, perm, S0+step, lambda src, blk: pltpu.make_async_copy(src, W.at[sl, :, :, pl.ds(pl.multiple_of(blk*SLAB,SLAB),SLAB)], sem.at[sl]).start())
    @pl.when(s==0)
    def _(): fetch(0,0)
    @pl.when(s+1<N)
    def _(): fetch(s+1,1-slot)
    pltpu.make_async_copy(W.at[slot],W.at[slot],sem.at[slot]).wait()
    for b in range(T//TB):
        lo,hi=b*TB,(b+1)*TB
        ga=dot(W[slot,0],a2[lo:hi,:],1,1)
        up=dot(W[slot,1],a2[lo:hi,:],1,1)
        dh=dot(W[slot,2],g[lo:hi,:],1,1)
        phi,den=gelu_parts(ga)
        ge=ga*phi
        hT[:,lo:hi]=(ge*up).astype(BF)
        dgT[:,lo:hi]=(dh*up*(phi+ga*den)).astype(BF)
        duT[:,lo:hi]=(dh*ge).astype(BF)
    yc=dot(hT[...],W[slot,2],0,0)
    dc=dot(dgT[...],W[slot,0],0,0)+dot(duT[...],W[slot,1],0,0)
    @pl.when(s==0)
    def _():
        y[...]=yc+y_in[...] if S0 else yc
        da[...]=dc+da_in[...] if S0 else dc
    @pl.when(s>0)
    def _():
        y[...]+=yc; da[...]+=dc
    @pl.when(s>=2)
    def _(): pltpu.make_async_copy(stg.at[slot],stg.at[slot],osem.at[slot]).wait()
    stg[slot,0]=dot(dgT[...],a2[...],1,0).astype(BF)
    stg[slot,1]=dot(duT[...],a2[...],1,0).astype(BF)
    stg[slot,2]=dot(hT[...],g[...],1,0).astype(BF)
    for r in range(R):
        dst=(d0,d1)[r%2]
        pltpu.make_async_copy(stg.at[slot,:,:,pl.ds(pl.multiple_of(perm[R+r]*SLAB,SLAB),SLAB)], dst.at[r//2, slots[S0+s]-S0], osem.at[slot]).start()
    if S0+N==S:
        @pl.when(s==N-1)
        def _():
            br=y[...]; rs=resid[...]; gf=g[...].astype(F32)
            res=rs+br
            out[...]=res.astype(BF)
            kp=keep[...]
            s1=jnp.sum(kp*br*br,axis=0,keepdims=True); s2=jnp.sum(kp*res*res,axis=0,keepdims=True)
            stat_out[...]=jnp.concatenate([s1,s2],axis=0)
            mu=jnp.mean(rs,axis=1,keepdims=True); ce=rs-mu
            rstd=lax.rsqrt(jnp.mean(ce*ce,axis=1,keepdims=True)+NORM_EPS)
            xh=ce*rstd
            d=da[...]
            gg_out[...]=jnp.sum(d*xh,axis=0,keepdims=True)
            e=d*gain[...]
            dr=gf+rstd*(e-jnp.mean(e,axis=1,keepdims=True)-xh*jnp.mean(e*xh,axis=1,keepdims=True))
            dres_out[...]=dr
            db=dr.astype(BF)
            dresb_out[...]=db
            dresT_out[...]=dr.T.astype(BF)
    @pl.when(s==N-1)
    def _():
        for sl in range(min(N,2)):
            pltpu.make_async_copy(stg.at[sl],stg.at[sl],osem.at[sl]).wait()

def mlp(perm2,slots,a2,g,resid,gain,keep,pieces,S0=0,N=None,carry=(),TB=256):
    wps,metas,S,SLAB,HC=pieces
    N=S if N is None else N
    R=perm2.shape[0]//2
    T,D=a2.shape
    A=pl.BlockSpec(memory_space=ANY)
    sd=jax.ShapeDtypeStruct
    last=S0+N==S
    outs=[sd((T,D),BF),sd((T,D),F32),sd((T,D),BF),sd((D,T),BF),sd((1,D),F32),sd((2,D),F32)] if last else [sd((T,D),F32)]*2
    gs=pltpu.PrefetchScalarGridSpec(num_scalar_prefetch=2,grid=(N,),
        in_specs=[full((T,D)),full((T,D)),full((T,D)),full((1,D)),full((T,1))]+[A]*len(wps)+[full((T,D))]*len(carry),
        out_specs=[full(o.shape) for o in outs]+[A,A],
        scratch_shapes=([pltpu.VMEM((T,D),F32)]*2 if last else [])+[pltpu.VMEM((2,3,HC,D),BF),pltpu.VMEM((2,3,HC,D),BF)]+[pltpu.VMEM((HC,T),BF)]*3+[pltpu.SemaphoreType.DMA((2,)),pltpu.SemaphoreType.DMA((2,))])
    piece=sd((R//2,N,3,HC,SLAB),BF)
    return pl.pallas_call(functools.partial(mlp_kernel,T=T,D=D,HC=HC,R=R,metas=metas,S=S,SLAB=SLAB,TB=min(TB,T),S0=S0,N=N),grid_spec=gs,
        out_shape=outs+[piece,piece],
        cost_estimate=pl.CostEstimate(flops=1,transcendentals=0,bytes_accessed=1),name="mlp_both")(perm2,slots,a2,g,resid,gain,keep,*wps,*carry)

def bwd_attn_kernel(perm, dres, cos, sin, kseg, qseg, q_in, k_in, v_in, lse_in, *rest, T, KV, C, metas, S, SLAB, S0, N):
    wps = rest[:len(metas)]
    dq_out, dk_out, dv_out, W, bias, dob, dqs, dks, sem = rest[-9:]
    s=pl.program_id(0)
    slot=lax.rem(s,2)
    def fetch(step, sl):
        fetch_pieces(wps, metas, perm, S0+step, lambda src, blk: pltpu.make_async_copy(src.at[3], W.at[sl, pl.ds(pl.multiple_of(blk*SLAB,SLAB),SLAB), :], sem.at[sl]).start())
    @pl.when(s==0)
    def _():
        fetch(0,0)
        row=lax.broadcasted_iota(jnp.int32,(KV,T),0); col=lax.broadcasted_iota(jnp.int32,(KV,T),1)
        ok=(kseg[...]==qseg[...])|(row==col)
        bias[...]=jnp.where(ok,0.0,-1e30)
    @pl.when(s+1<N)
    def _(): fetch(s+1,1-slot)
    pltpu.make_async_copy(W.at[slot],W.at[slot],sem.at[slot]).wait()
    n=C//128
    dob[...]=dot(dres[...],W[slot],1,0).astype(BF)
    for p in range(n):
        kp=k_in[0,:,p*128:(p+1)*128]; vp=v_in[0,:,p*128:(p+1)*128]
        qp=q_in[0,:,p*128:(p+1)*128]; dp_=dob[:,p*128:(p+1)*128]
        half=lax.broadcasted_iota(jnp.int32,qp.shape,1)<64
        parts=[]
        dvs=None
        for h in range(2):
            mk=half if h==0 else ~half
            qm=jnp.where(mk,qp,jnp.zeros_like(qp)); dm=jnp.where(mk,dp_,jnp.zeros_like(dp_))
            pt=jnp.exp(dot(kp,qm,1,1)+bias[...]-lse_in[0,2*p+h:2*p+h+1,:])
            dpt=dot(vp,dm,1,1)
            delta=jnp.sum(pt*dpt,axis=0,keepdims=True)
            ds=(pt*(dpt-delta)).astype(BF)
            dv=dot(pt.astype(BF),dm,1,0); dk=dot(ds,qm,1,0)
            dqt=dot(kp,ds,0,0)
            parts.append(dqt[h*64:(h+1)*64])
            if h==0: dva,dka=dv,dk
            else: dva,dka=dva+dv,dka+dk
        dqs[:,p*128:(p+1)*128]=jnp.concatenate(parts,axis=0).T*(1.0/math.sqrt(HEAD_DIM))
        dks[:,p*128:(p+1)*128]=dka
        dv_out[0,:,p*128:(p+1)*128]=dva.astype(BF)
    cw=wide(cos[...],n); sw=wide(sin[...],n)
    dq_out[0]=turn(dqs[...],cw[:T],-sw[:T],lower_lanes(T,C)).astype(BF)
    dk_out[0]=turn(dks[...],cw,-sw,lower_lanes(KV,C)).astype(BF)

def bwd_attn(perm,dres,cos,sin,kseg,qseg,q,k,v,lse,pieces,S0=0,N=None,carry=()):
    wps,metas,S,SLAB,C=pieces
    T,D=dres.shape; KV=k.shape[1]; HG=C//HEAD_DIM
    N=S if N is None else N
    ib=lambda rows:pl.BlockSpec((1,rows,C),lambda s,p:(s+S0,0,0))
    gs=pltpu.PrefetchScalarGridSpec(num_scalar_prefetch=1,grid=(N,),
        in_specs=[full((T,D)),full((KV,128)),full((KV,128)),full((KV,1)),full((1,T)),ib(T),ib(KV),ib(KV),pl.BlockSpec((1,HG,T),lambda s,p:(s+S0,0,0))]+[pl.BlockSpec(memory_space=ANY)]*(len(wps)+len(carry)),
        out_specs=[ib(T),ib(KV),ib(KV)],
        scratch_shapes=[pltpu.VMEM((2,D,C),BF),pltpu.VMEM((KV,T),F32),pltpu.VMEM((T,C),BF),pltpu.VMEM((T,C),F32),pltpu.VMEM((KV,C),F32),pltpu.SemaphoreType.DMA((2,))])
    sd=jax.ShapeDtypeStruct
    fl=(2*T*D*C+10*T*KV*C)*N
    return pl.pallas_call(functools.partial(bwd_attn_kernel,T=T,KV=KV,C=C,metas=metas,S=S,SLAB=SLAB,S0=S0,N=N),grid_spec=gs,
        out_shape=[sd((S,T,C),BF),sd((S,KV,C),BF),sd((S,KV,C),BF)],
        input_output_aliases={10+len(wps)+i:i for i in range(len(carry))},
        cost_estimate=pl.CostEstimate(flops=1,transcendentals=0,bytes_accessed=1),name="attn_bwd")(perm,dres,cos,sin,kseg,qseg,q,k,v,lse,*wps,*carry)

def grad_attn_kernel(perm, slots, a1T, dresT, xhat, o_in, dq_in, dk_in, dv_in, *rest, T, KV, C, R, metas, S, SLAB):
    wps = rest[:len(metas)]
    da_own, da_far, gg_out, d0, d1, W, stg, acc, sem, osem = rest[len(metas):]
    s=pl.program_id(0)
    slot=lax.rem(s,2)
    def fetch(step, sl):
        fetch_pieces(wps, metas, perm, step, lambda src, blk: pltpu.make_async_copy(src.at[pl.ds(0,3)], W.at[sl, :, pl.ds(pl.multiple_of(blk*SLAB,SLAB),SLAB), :], sem.at[sl]).start())
    @pl.when(s==0)
    def _(): fetch(0,0)
    @pl.when(s+1<S)
    def _(): fetch(s+1,1-slot)
    @pl.when(s>=2)
    def _(): pltpu.make_async_copy(stg.at[slot],stg.at[slot],osem.at[slot]).wait()
    stg[slot,0]=dot(a1T[:,:T],dq_in[0],1,0).astype(BF)
    stg[slot,1]=dot(a1T[...],dk_in[0],1,0).astype(BF)
    stg[slot,2]=dot(a1T[...],dv_in[0],1,0).astype(BF)
    stg[slot,3]=dot(dresT[...],o_in[0],1,0).astype(BF)
    for r in range(R):
        dst=(d0,d1)[r%2]
        pltpu.make_async_copy(stg.at[slot,:,pl.ds(pl.multiple_of(perm[R+r]*SLAB,SLAB),SLAB),:], dst.at[r//2, slots[s]], osem.at[slot]).start()
    pltpu.make_async_copy(W.at[slot],W.at[slot],sem.at[slot]).wait()
    c=dot(dk_in[0],W[slot,1],1,1)+dot(dv_in[0],W[slot,2],1,1)
    cq=dot(dq_in[0],W[slot,0],1,1)
    @pl.when(s==0)
    def _():
        acc[...]=c
        acc[:T,:]=acc[:T,:]+cq
    @pl.when(s>0)
    def _():
        acc[...]=acc[...]+c
        acc[:T,:]=acc[:T,:]+cq
    @pl.when(s==S-1)
    def _():
        gg_out[...]=jnp.sum(acc[...]*xhat[...].astype(F32),axis=0,keepdims=True)
        da_own[...]=acc[:T,:]
        da_far[...]=acc[T:,:].astype(BF)
        for sl in range(min(S,2)):
            pltpu.make_async_copy(stg.at[sl],stg.at[sl],osem.at[sl]).wait()

def grad_attn(perm2,slots,a1T,dresT,xhat,o,dq,dk,dv,pieces):
    wps,metas,S,SLAB,C=pieces
    R=perm2.shape[0]//2
    D,T=dresT.shape; KV=dk.shape[1]
    A=pl.BlockSpec(memory_space=ANY)
    ib=lambda rows:pl.BlockSpec((1,rows,C),lambda s,p,q:(s,0,0))
    gs=pltpu.PrefetchScalarGridSpec(num_scalar_prefetch=2,grid=(S,),
        in_specs=[full((D,KV)),full((D,T)),full((KV,D)),ib(T),ib(T),ib(KV),ib(KV)]+[A]*len(wps),
        out_specs=[full((T,D)),full((KV-T,D)),full((1,D)),A,A],
        scratch_shapes=[pltpu.VMEM((2,3,D,C),BF),pltpu.VMEM((2,4,D,C),BF),pltpu.VMEM((KV,D),F32),pltpu.SemaphoreType.DMA((2,)),pltpu.SemaphoreType.DMA((2,))])
    sd=jax.ShapeDtypeStruct
    piece=sd((R//2,S,4,SLAB,C),BF)
    return pl.pallas_call(functools.partial(grad_attn_kernel,T=T,KV=KV,C=C,R=R,metas=metas,S=S,SLAB=SLAB),grid_spec=gs,
        out_shape=[sd((T,D),F32),sd((KV-T,D),BF),sd((1,D),F32),piece,piece],
        cost_estimate=pl.CostEstimate(flops=1,transcendentals=0,bytes_accessed=1),name="attn_grad")(perm2,slots,a1T,dresT,xhat,o,dq,dk,dv,*wps)

def split3(x):
    hi=x.astype(BF)
    return hi,(x-hi.astype(F32)).astype(BF)

def dot3(a,b,ca,cb):
    ah,al=a; bh,bl=b
    return dot(ah,bh,ca,cb)+(dot(ah,bl,ca,cb)+dot(al,bh,ca,cb))

def soap_kernel(sc, g_in, first, second, left, right, *rest, turned, each):
    f_out, s_out, u_out, n_out = rest[-4:]
    step,b1,b2=sc[0],sc[1],sc[2]
    for i in range(each):
        ql=split3(left[i]); qr=split3(right[i])
        if turned:
            x=dot3(split3(g_in[i]),ql,1,0)
            r=dot3(split3(x),qr,0,0).T
        else:
            x=dot3(ql,split3(g_in[i]),0,0)
            r=dot3(split3(x),qr,1,0)
        fn=b1*first[i]+(1.0-b1)*r
        sn=b2*second[i]+(1.0-b2)*r*r
        f_out[i]=fn; s_out[i]=sn
        n=fn/(jnp.sqrt(sn)+ADAM_EPS)
        if turned:
            t=dot3(split3(dot3(qr,split3(n),1,0)),ql,1,1)
        else:
            t=dot3(split3(dot3(ql,split3(n),1,0)),qr,1,1)
        size=n.shape[0]*n.shape[1]
        fac=jnp.sqrt(jnp.sum(n*n,keepdims=True)*(1.0/size))*lax.rsqrt(jnp.sum(t*t,keepdims=True)*(1.0/size)+SCALE_EPS)
        u_out[i]=(-step*fac)*t
        n_out[i]=jnp.broadcast_to(fac,(8,128))

def soap(scalars,g,first,second,left,right,turned,each=1,K0=0,N=None,carry=()):
    K=first.shape[0]
    N=K if N is None else N
    b=lambda x:pl.BlockSpec((each,)+x.shape[1:],lambda k,s:(k+K0,0,0))
    sd=jax.ShapeDtypeStruct
    o=sd(first.shape,F32)
    outs=[o,o,o,sd((K,8,128),F32)]
    gs=pltpu.PrefetchScalarGridSpec(num_scalar_prefetch=1,grid=(N//each,),
        in_specs=[b(x) for x in (g,first,second,left,right)]+[pl.BlockSpec(memory_space=ANY)]*len(carry),out_specs=[b(x) for x in outs])
    return pl.pallas_call(functools.partial(soap_kernel,turned=turned,each=each),grid_spec=gs,out_shape=outs,
        input_output_aliases={6+i:i for i in range(len(carry))},
        cost_estimate=pl.CostEstimate(flops=1,transcendentals=0,bytes_accessed=1),
        name="soap_"+("mlp" if turned else "attn"))(scalars,g,first,second,left,right,*carry)

def norm_kernel(own, far, gain, a1, a1T, xh, *, T):
    for lo,ref in ((0,own),(T,far)):
        v=ref[...].astype(F32)
        ce=v-jnp.mean(v,axis=1,keepdims=True)
        x=ce*lax.rsqrt(jnp.mean(ce*ce,axis=1,keepdims=True)+NORM_EPS)
        n=ref.shape[0]
        xh[lo:lo+n,:]=x.astype(BF)
        y=x*gain[...]
        a1[lo:lo+n,:]=y.astype(BF)
        a1T[:,lo:lo+n]=y.T.astype(BF)

def norm_first(own,far,gain):
    T,D=own.shape; KV=T+far.shape[0]
    sd=jax.ShapeDtypeStruct
    outs=[sd((KV,D),BF),sd((D,KV),BF),sd((KV,D),BF)]
    return pl.pallas_call(functools.partial(norm_kernel,T=T),grid=(1,),in_specs=[full(x.shape) for x in (own,far,gain)],
        out_specs=[full(o.shape) for o in outs],out_shape=outs,
        cost_estimate=pl.CostEstimate(flops=1,transcendentals=0,bytes_accessed=1),name="norm_first")(own,far,gain)

def input_kernel(hid, da, dres, gain, *rest):
    out=rest[-1]
    v=hid[...].astype(F32)
    ce=v-jnp.mean(v,axis=1,keepdims=True)
    rstd=lax.rsqrt(jnp.mean(ce*ce,axis=1,keepdims=True)+NORM_EPS)
    x=ce*rstd
    d=da[...]
    for r in rest[:-1]:
        d=d+r[...].astype(F32)
    e=d*gain[...]
    out[...]=(dres[...]+rstd*(e-jnp.mean(e,axis=1,keepdims=True)-x*jnp.mean(e*x,axis=1,keepdims=True))).astype(BF)

def input_back(hid,da,dres,gain,*back):
    args=(hid,da,dres,gain)+back
    return pl.pallas_call(input_kernel,grid=(1,),in_specs=[full(x.shape) for x in args],out_specs=full(hid.shape),
        out_shape=jax.ShapeDtypeStruct(hid.shape,BF),
        cost_estimate=pl.CostEstimate(flops=1,transcendentals=0,bytes_accessed=1),name="input_back")(*args)


def ring_order(count):
    return list(range(0, count, 2)) + list(range(1, count, 2))[::-1]


def swap_dp(value, bit, owners):
    return lax.ppermute(value, "dp", [(i, i ^ bit) for i in range(owners)])


def to_ring_pred(value, shards):
    ring = ring_order(shards)
    return lax.ppermute(
        value, "tensor", [(ring[p], ring[(p - 1) % shards]) for p in range(shards)]
    )


def to_ring_succ(value, shards):
    ring = ring_order(shards)
    return lax.ppermute(
        value, "tensor", [(ring[p], ring[(p + 1) % shards]) for p in range(shards)]
    )


def along_line(value, steps, shards):
    ring = ring_order(shards)
    return lax.ppermute(
        value, "tensor", [(ring[p], ring[(p + steps) % shards]) for p in range(shards)]
    )


def add_low(one, two):
    return (one.astype(F32) + two.astype(F32)).astype(BF)


def halve(pieces, bits, owners):
    for bit in bits:
        live = sorted(bits[bits.index(bit):], reverse=True)
        axis = live.index(bit)
        send = lax.index_in_dim(pieces, 1, axis, keepdims=False)
        keep = lax.index_in_dim(pieces, 0, axis, keepdims=False)
        pieces = add_low(keep, swap_dp(send, bit, owners))
    return pieces


def reduce_pieces(even, odd, cut, owners, shards):
    mine = add_low(even, swap_dp(odd, 1, owners))
    bits = [1 << b for b in range(1, owners.bit_length() - 1)]
    mine = mine.reshape((2,) * len(bits) + mine.shape[1:])
    low = halve(mine[..., :cut, :], bits[::-1], owners)
    high = halve(mine[..., cut:, :], bits, owners)
    both = jnp.concatenate([low, high], axis=-2)
    moving = both[shards - 1]
    for left in range(shards - 2, -1, -1):
        moving = to_ring_pred(moving, shards)
        moving = moving.astype(F32) + both[left].astype(F32)
        if left:
            moving = moving.astype(BF)
    return moving


def all_sum(value, owners, shards):
    for axis, count in (("dp", owners), ("tensor", shards)):
        step = 1
        while step < count:
            value = value + lax.ppermute(value, axis, [(i, i ^ step) for i in range(count)])
            step *= 2
    return value


def after(value, *earlier):
    return lax.optimization_barrier((value,) + earlier)[0]


def add_all(*values):
    total = values[0].astype(F32)
    for value in values[1:]:
        total = total + value.astype(F32)
    return total


def gather_stack(stacked, owners):
    half = stacked.shape[0] // 2
    by_x, by_y = swap_dp(stacked, 2, owners), swap_dp(stacked, 4, owners)
    return by_x, by_y, swap_dp(by_x[:half], 4, owners), swap_dp(by_y[half:], 2, owners)


def to_core(arrays, owners):
    return [swap_dp(a, 1, owners) for a in arrays]


def with_partner(arrays, metas, owners):
    return arrays + [swap_dp(a, 1, owners) for a in arrays], metas + tuple((m[0] + 1,) + m[1:] for m in metas)


def cross_sends(even, core, half):
    low = add_all(even[3, :half], core[3, :half]).astype(BF)
    high = add_all(even[3, half:], core[3, half:]).astype(BF)
    return low, high


def side_sends(even, core, from_y, from_x, half):
    def widen(part, before):
        after_it = even.shape[1] - before - part.shape[0]
        return jnp.pad(part.astype(F32), [(before, after_it)] + [(0, 0)] * (part.ndim - 1))

    to_x = (add_all(even[1], core[1]) + widen(from_y, 0)).astype(BF)
    to_y = (add_all(even[2], core[2]) + widen(from_x, half)).astype(BF)
    return to_x, to_y


def own_part(even, core, from_x, from_y, slot):
    return add_all(even[0, slot], core[0, slot], from_x[slot], from_y[slot])


def ring_sum(even, core, from_x, from_y, shards):
    moving = None
    for slot in list(range(1, shards)) + [0]:
        part = own_part(even, core, from_x, from_y, slot)
        if moving is not None:
            part = part + to_ring_succ(moving, shards).astype(F32)
        moving = part.astype(BF)
    return part


def per_device(
    hidden_in, out_grad, attn_weight, mlp_weight, norm_gain,
    attn_first, attn_second, attn_left, attn_right,
    mlp_first, mlp_second, mlp_left, mlp_right,
    gain_first, gain_second, owner_rows, segment_ids, positions, valid,
    step, learn_rate, beta_first, beta_second,
):
    owners = lax.axis_size("dp")
    shards = lax.axis_size("tensor")
    dp_index = lax.axis_index("dp")
    place = lax.axis_index("tensor")
    rows, width = hidden_in.shape
    slab = attn_weight.shape[1]
    hid_cols = mlp_weight.shape[2]
    span = SEQ_LEN // rows
    within = place % span
    base = place - within
    half = shards // 2
    gain_rows = norm_gain.astype(F32)

    def from_peer(value, ahead):
        pairs = [(g + (w + ahead) % span, g + w) for g in range(0, shards, span) for w in range(span)]
        return lax.ppermute(value, "tensor", pairs)

    def sequence_rows(column):
        return jnp.concatenate(
            [lax.dynamic_slice_in_dim(column, (base + (within + d) % span) * rows, rows, 0) for d in range(span)]
        )

    joined = 128 // slab if slab < 128 else 1
    fast = owners == 8 and joined == 1 and shards == 4 and span == 2
    both = ("dp", "tensor")
    mlp_turned = jnp.swapaxes(mlp_weight, 1, 2)
    if not fast:
        attn_all = lax.all_gather(attn_weight, both, axis=0, tiled=False).reshape((owners, shards) + attn_weight.shape)
        mlp_all = lax.all_gather(mlp_turned, both, axis=0, tiled=False).reshape((owners, shards) + mlp_turned.shape)

    slot_ids = jnp.arange(owners, dtype=jnp.int32)
    rel_owner = jnp.sum(
        jnp.where((slot_ids[:, None] ^ dp_index) == slot_ids[None, :], owner_rows[None, :], 0), axis=1
    )
    ring = ring_order(shards)
    ring_place = jnp.array([ring.index(z) for z in range(shards)], jnp.int32)
    my_place = jnp.sum(jnp.where(jnp.arange(shards) == place, ring_place, 0))
    slots = (my_place - ring_place) % shards
    attn_perm = jnp.concatenate([rel_owner if fast else owner_rows, rel_owner]).astype(jnp.int32)
    if fast:
        slots = jnp.arange(shards, dtype=jnp.int32)
    if joined == 1:
        mlp_perm = attn_perm
    else:
        inverse = jnp.sum(jnp.where(owner_rows[None, :] == slot_ids[:, None], slot_ids[None, :], 0), axis=1)
        mlp_all = jnp.take(mlp_all, inverse, axis=0).reshape((owners // joined, joined) + mlp_all.shape[1:])
        mlp_all = jnp.moveaxis(mlp_all, 1, 4)
        mlp_all = mlp_all.reshape(mlp_all.shape[:4] + (joined * slab,))
        blocks = jnp.arange(owners // joined, dtype=jnp.int32)
        mlp_perm = jnp.concatenate([blocks, blocks])

    seg = sequence_rows(segment_ids)
    keep_seq = sequence_rows(valid)
    pos = sequence_rows(positions)
    half_dim = HEAD_DIM // 2
    frequency = jnp.exp(jnp.arange(half_dim, dtype=F32) * (-2.0 * math.log(ROPE_BASE) / HEAD_DIM))
    angles = pos.astype(F32)[:, None] * frequency[None, :]
    cos_half, sin_half = jnp.cos(angles), jnp.sin(angles)
    cos_table = jnp.concatenate([cos_half] * 4, axis=1)
    sin_table = jnp.concatenate([-sin_half, sin_half] * 2, axis=1)
    key_seg = jnp.where(keep_seq > 0, seg, -1)[:, None]
    query_seg = seg[None, :rows]
    keep_own = keep_seq[:rows].astype(F32)[:, None]

    first_gain, second_gain = gain_rows[0:1], gain_rows[1:2]
    if fast:
        together = lax.optimization_barrier
        mlp_x, mlp_y, mlp_z = [None] * 4, [None] * 4, [None] * 4
        line_1 = along_line(attn_weight, 1, shards)
        mlp_x[0], mlp_y[0] = swap_dp(mlp_turned, 2, owners), swap_dp(mlp_turned, 4, owners)
        tables = (cos_table, sin_table, key_seg, query_seg, keep_own, attn_perm, mlp_perm, slots, first_gain, second_gain)
        line_1, mlp_x[0], mlp_y[0] = together((line_1, mlp_x[0], mlp_y[0]))
        pair_a = jnp.stack([attn_weight, line_1])
        x_a, y_a = swap_dp(pair_a, 2, owners), swap_dp(pair_a, 4, owners)
        far_rows = from_peer(after(hidden_in, line_1), 1)
        core_0 = to_core([after(a, line_1) for a in (mlp_turned, mlp_x[0])], owners)
        x_a, y_a, core_0, tables = together((x_a, y_a, core_0, tables))
        cos_table, sin_table, key_seg, query_seg, keep_own, attn_perm, mlp_perm, slots, first_gain, second_gain = tables
        z_a, mlp_z[0] = swap_dp(x_a, 4, owners), swap_dp(after(mlp_y[0], y_a), 2, owners)
        line_2, line_3 = along_line(after(line_1, x_a), 1, shards), along_line(after(attn_weight, x_a), 3, shards)
        normal = norm_first(hidden_in, far_rows, first_gain)
        z_a, mlp_z[0], normal, line_2, line_3 = together((z_a, mlp_z[0], tuple(normal), line_2, line_3))
        pair_b = jnp.stack([line_2, line_3])
        x_b, y_b = swap_dp(pair_b, 2, owners), swap_dp(pair_b, 4, owners)
        mlp_line = [mlp_turned, along_line(after(mlp_turned, line_3), 1, shards), None, None]
        core_a4 = to_core([after(a, z_a) for a in (pair_a, x_a, y_a, z_a)], owners)
        core_b = [swap_dp(after(pair_b, core_a4[1]), 1, owners)]
        core_0 = core_0 + to_core([after(a, core_b[0]) for a in (mlp_y[0], mlp_z[0])], owners)
        normal, core_a4, mlp_line[1], core_b, x_b, y_b, core_0 = together(
            (tuple(normal), core_a4, mlp_line[1], core_b, x_b, y_b, core_0)
        )
        z_b = swap_dp(y_b, 2, owners)
        mlp_x[1], mlp_y[1] = swap_dp(mlp_line[1], 2, owners), swap_dp(mlp_line[1], 4, owners)
        mlp_line[3] = along_line(after(mlp_turned, mlp_line[1]), 3, shards)
        mlp_line[2] = along_line(mlp_line[1], 1, shards)
        first_norm, first_turned, xhat_low = normal

        def attn_set(arrays, first):
            return arrays, tuple((r, first, 2, shards) for r in (0, 2, 4, 6, 1, 3, 5, 7))

        sizes = (shards, slab, attn_weight.shape[2])
        arrays_a, metas_a = attn_set([pair_a, x_a, y_a, z_a, *core_a4], 0)
        attn_part_a = (arrays_a, metas_a, *sizes)
    else:
        far_rows = [from_peer(hidden_in, d) for d in range(1, span)]
        attn_pieces = ([attn_all], (None,), shards, slab, attn_weight.shape[2])
        first_norm, first_turned, xhat_low = norm_first(hidden_in, jnp.concatenate(far_rows), first_gain)
    back_args = (cos_table, sin_table, key_seg, query_seg)
    fwd_args = (attn_perm, first_norm, hidden_in, second_gain, cos_table, sin_table, key_seg, query_seg, keep_own)
    if fast:
        carry = fwd_attn(*fwd_args, attn_part_a, S0=0, N=half)
        z_b, mlp_x[1], mlp_y[1], mlp_line[3], mlp_line[2], carry = together(
            (z_b, mlp_x[1], mlp_y[1], mlp_line[3], mlp_line[2], tuple(carry))
        )
        core_b = core_b + to_core([after(x_b, z_b), after(y_b, z_b)], owners)
        core_z_b = swap_dp(z_b, 1, owners)
        core_b, core_z_b, mlp_x[1], mlp_y[1], mlp_line[3], mlp_line[2] = together((core_b, core_z_b, mlp_x[1], mlp_y[1], mlp_line[3], mlp_line[2]))
        mlp_z[1] = swap_dp(mlp_y[1], 2, owners)
        mlp_y[2] = swap_dp(mlp_line[2], 4, owners)
        arrays_b, metas_b = attn_set([pair_b, x_b, y_b, z_b, *core_b, core_z_b], 2)
        attn_part_b = (arrays_b, metas_b, *sizes)
        attn_pieces = (arrays_a + arrays_b, metas_a + metas_b, *sizes)
        mlp_x[3], mlp_y[3] = swap_dp(mlp_line[3], 2, owners), swap_dp(mlp_line[3], 4, owners)
        out = fwd_attn(*fwd_args, attn_part_b, S0=half, N=half, carry=carry)
        mlp_x[3], mlp_y[3], mlp_z[1], mlp_y[2], out = together((mlp_x[3], mlp_y[3], mlp_z[1], mlp_y[2], tuple(out)))
        queries, keys, values, attended, log_sums, resid, second_norm, stat_a = out

        def mlp_set(slot):
            return [mlp_line[slot], mlp_x[slot], mlp_y[slot], mlp_z[slot]]

        def mlp_pieces(*slots_of):
            arrays, metas = [], []
            for slot, got in slots_of:
                arrays += [a[None] for a in got]
                metas += [(r, slot, 1, shards) for r in (0, 2, 4, 6, 1, 3, 5, 7)]
            return arrays, tuple(metas), shards, slab, hid_cols

        set_0, set_1 = mlp_set(0), mlp_set(1)
        core_1 = to_core([after(a, mlp_z[1]) for a in set_1], owners)
        core_1, second_norm, mlp_x[3], mlp_y[2] = together((core_1, second_norm, mlp_x[3], mlp_y[2]))
        mlp_z[3], mlp_z[2] = swap_dp(mlp_x[3], 4, owners), swap_dp(mlp_y[2], 2, owners)
        mlp_x[2] = swap_dp(after(mlp_line[2], second_norm), 2, owners)
        core_3 = to_core([mlp_line[3], mlp_x[3]], owners)
        mlp_args = (mlp_perm, slots, second_norm, out_grad, resid, second_gain, keep_own)
        out = mlp(*mlp_args, mlp_pieces((0, set_0 + core_0), (1, set_1 + core_1)), S0=0, N=half)
        mlp_x[2], mlp_z[2], mlp_z[3], core_3, out = together((mlp_x[2], mlp_z[2], mlp_z[3], core_3, tuple(out)))
        *carry, even_a, odd_a = out
        set_2, set_3 = mlp_set(2), mlp_set(3)
        core_2 = to_core([after(a, odd_a) for a in set_2], owners)
        core_3 = core_3 + to_core([after(a, odd_a) for a in set_3[2:]], owners)
        core_2, core_3, carry = together((core_2, core_3, carry))
        core_a = swap_dp(after(odd_a, core_2[3]), 1, owners)
        out = mlp(*mlp_args, mlp_pieces((2, set_2 + core_2), (3, set_3 + core_3)), S0=half, N=half, carry=carry)
        core_a, out = together((core_a, tuple(out)))
        output, dresid, dres_low, dres_turned, gain_two, stat_m, even_b, odd_b = out
        low, high = cross_sends(even_a, core_a, 1)
        low, high, dres_low = together((low, high, dres_low))
        from_y, from_x = swap_dp(low, 4, owners), swap_dp(high, 2, owners)
        core_b2 = swap_dp(odd_b, 1, owners)
        fwd_kept = (queries, keys, values, log_sums, attn_pieces)
        grads = bwd_attn(attn_perm, dres_low, *back_args, *fwd_kept, S0=0, N=half)
        from_y, from_x, core_b2, *grads = together((from_y, from_x, core_b2, *grads))
        low, high = cross_sends(even_b, core_b2, 1)
        to_x, to_y = side_sends(even_a, core_a, from_y, from_x, 1)
        low, high, to_x, to_y, dres_low = together((low, high, to_x, to_y, dres_low))
        from_y, from_x = swap_dp(low, 4, owners), swap_dp(high, 2, owners)
        back_x, back_y = swap_dp(to_x, 2, owners), swap_dp(to_y, 4, owners)
        grads = bwd_attn(attn_perm, dres_low, *back_args, *fwd_kept, S0=half, N=half, carry=tuple(grads))
        from_y, from_x, *grads = together((from_y, from_x, *grads))
        to_x, to_y = side_sends(even_b, core_b2, from_y, from_x, 1)
        to_x, to_y, back_x, back_y = together((to_x, to_y, back_x, back_y))
        from_x, from_y = swap_dp(to_x, 2, owners), swap_dp(to_y, 4, owners)
        ring_1 = own_part(even_a, core_a, back_x, back_y, 1).astype(BF)
        ring_1, dres_turned = together((ring_1, dres_turned))
        ring_1 = to_ring_succ(ring_1, shards)
        out = grad_attn(attn_perm, slots, first_turned, dres_turned, xhat_low, attended, *grads, attn_pieces)
        from_x, from_y, ring_1, *out = lax.optimization_barrier((from_x, from_y, ring_1, *out))
        da_own, da_far, gain_one, attn_even, attn_odd = out
    else:
        queries, keys, values, attended, log_sums, resid, second_norm, stat_a = fwd_attn(*fwd_args, attn_pieces)
        output, dresid, dres_low, dres_turned, gain_two, stat_m, mlp_even, mlp_odd = mlp(
            mlp_perm, slots, second_norm, out_grad, resid, second_gain, keep_own,
            ([mlp_all], (None,), shards, mlp_all.shape[-1], hid_cols),
        )
        if joined > 1:
            merged = jnp.stack([mlp_even, mlp_odd], axis=1).reshape((owners // joined,) + mlp_even.shape[1:])
            merged = merged.reshape(merged.shape[:-1] + (joined, slab))
            merged = jnp.moveaxis(merged, -2, 1).reshape((owners,) + mlp_even.shape[1:-1] + (slab,))
            merged = jnp.take(merged, rel_owner, axis=0)
            mlp_even, mlp_odd = merged[0::2], merged[1::2]
        mlp_sum = reduce_pieces(mlp_even, mlp_odd, -(-hid_cols // 32) * 16, owners, shards)
        grads = bwd_attn(attn_perm, dres_low, *back_args, queries, keys, values, log_sums, attn_pieces)
        da_own, da_far, gain_one, attn_even, attn_odd = grad_attn(
            attn_perm, slots, first_turned, dres_turned, xhat_low, attended, *grads, attn_pieces
        )
    def send_back(da_far):
        got = []
        for d in range(1, span):
            pairs = [(g + w, g + (w + d) % span) for g in range(0, shards, span) for w in range(span)]
            got.append(lax.ppermute(da_far[(d - 1) * rows : d * rows], "tensor", pairs))
        return got

    def swap_line(value, bit):
        return lax.ppermute(value, "tensor", [(i, i ^ bit) for i in range(shards)])

    def finish_input(da_back):
        return input_back(hidden_in, da_own, dresid, first_gain, *da_back)

    step_count = step.astype(F32)
    step_size = (
        learn_rate
        * jnp.sqrt(1.0 - jnp.power(beta_second, step_count))
        / (1.0 - jnp.power(beta_first, step_count))
    )
    scalars = jnp.stack([step_size, beta_first, beta_second])

    def flip(value):
        return jnp.swapaxes(value, 1, 2)

    def soap_mlp(total, *part):
        return soap(scalars, total, flip(mlp_first), flip(mlp_second), mlp_left, mlp_right, True, *part)

    sums = jnp.concatenate([jnp.sum(stat_a, axis=1), jnp.sum(stat_m, axis=1), jnp.sum(keep_own)[None]])
    small = jnp.concatenate([gain_one, gain_two, jnp.pad(sums, (0, width - 5))[None]], axis=0)
    if fast:
        attn_core = swap_dp(attn_odd, 1, owners)
        ring_2 = (own_part(even_b, core_b2, from_x, from_y, 0) + ring_1.astype(F32)).astype(BF)
        ring_2 = to_ring_succ(ring_2, shards)
        small = small + swap_dp(small, 1, owners)
        small, attn_core = lax.optimization_barrier((small, attn_core))
        low, high = cross_sends(attn_even, attn_core, half)
        low, high, small = lax.optimization_barrier((low, high, small))
        cross_y, cross_x = swap_dp(low, 4, owners), swap_dp(high, 2, owners)
        small = small + swap_dp(small, 2, owners)
        ring_3 = (own_part(even_b, core_b2, from_x, from_y, 1) + ring_2.astype(F32)).astype(BF)
        ring_3 = to_ring_succ(ring_3, shards)
        small, cross_x, cross_y = lax.optimization_barrier((small, cross_x, cross_y))
        to_x, to_y = side_sends(attn_even, attn_core, cross_y, cross_x, half)
        to_x, to_y, small = lax.optimization_barrier((to_x, to_y, small))
        attn_x, attn_y = swap_dp(to_x, 2, owners), swap_dp(to_y, 4, owners)
        small = small + swap_dp(small, 4, owners)
        da_back = send_back(after(da_far, ring_3))
        mlp_sum = own_part(even_a, core_a, back_x, back_y, 0) + ring_3.astype(F32)
        mlp_new = soap_mlp(mlp_sum)
        attn_x, attn_y, mlp_sum, mlp_new = lax.optimization_barrier((attn_x, attn_y, mlp_sum, tuple(mlp_new)))
        moving = own_part(attn_even, attn_core, attn_x, attn_y, 1).astype(BF)
        for slot in range(1, shards):
            moving, small, da_back = lax.optimization_barrier((moving, small, da_back))
            moving = to_ring_succ(moving, shards)
            if slot < 3:
                small = small + swap_line(small, slot)
            if slot == 1:
                input_grad = finish_input(da_back)
                moving, input_grad = lax.optimization_barrier((moving, input_grad))
            moving, small = lax.optimization_barrier((moving, small))
            moving = moving.astype(F32) + own_part(attn_even, attn_core, attn_x, attn_y, (slot + 1) % shards)
            if slot + 1 < shards:
                moving = moving.astype(BF)
        attn_sum = moving
    else:
        attn_sum = reduce_pieces(attn_even, attn_odd, slab // 2, owners, shards)
        small = all_sum(small, owners, shards)
        mlp_new = soap_mlp(mlp_sum)
        input_grad = finish_input(send_back(da_far))
    gain_grad = small[:2]
    stat_sums = small[2]

    attn_grad = attn_sum
    attn_first_new, attn_second_new, attn_update, attn_scale = soap(
        scalars, attn_sum, attn_first, attn_second, attn_left, attn_right, False, 2
    )
    mlp_grad, mlp_first_new, mlp_second_new, mlp_update = (flip(v) for v in (mlp_sum, *mlp_new[:3]))
    mlp_scale = mlp_new[3]
    gain_first_new = beta_first * gain_first + (1.0 - beta_first) * gain_grad
    gain_second_new = beta_second * gain_second + (1.0 - beta_second) * gain_grad * gain_grad
    gain_update = -step_size * gain_first_new / (jnp.sqrt(gain_second_new) + ADAM_EPS)
    root_means = jnp.sqrt(stat_sums[:4] / (stat_sums[4] * width))
    norm_scale = jnp.concatenate([attn_scale[:, :1, :1], mlp_scale[:, :1, :1]], axis=0)
    return (
        output, input_grad, attn_grad, mlp_grad, gain_grad,
        attn_first_new, attn_second_new, mlp_first_new, mlp_second_new,
        gain_first_new, gain_second_new, attn_update, mlp_update, gain_update,
        norm_scale, root_means,
    )


def solution(mesh):
    rows = P(("dp", "tensor"), None)
    block = P(None, "dp", "tensor")
    return jax.shard_map(
        per_device,
        mesh=mesh,
        in_specs=(rows, rows, block, block, P()) + (block,) * 8 + (P(),) * 3 + (P("dp"),) * 3 + (P(),) * 4,
        out_specs=(rows, rows, block, block, P(), block, block, block, block, P(), P(), block, block, P(), block, P()),
        check_vma=False,
    )
```
